32 devices in a mesh: dp: 4 (over y, core), row: 2 (over x), col: 4 (over z).
Axes of the slice: x: 2, y: 2, z: 4, core: 2. Of those that a mesh axis runs over, the one named last changes fastest.
Arguments:
- inputs: bfloat16 [4096, 768], P(('dp', 'col'), 'row'), may hold values from -6 to 6
- cotangent: bfloat16 [4096, 768], P(('dp', 'col'), 'row'), may hold values from -6 to 6
- routes: int32 [4096, 2], P('dp'), may hold values from 0 to 15, all different within a row; in each aligned block of 1024 rows (0 to 1023, 1024 to 2047, ...) at most 192 rows name the same one
- cont_lengths: int32 [4, 8], P('dp'), may hold values from 1 to 128, 512 in all within a row
- first_gain: float32 [768], P('row'), may hold values from 0.5 to 1.5
- attend_in: bfloat16 [768, 2304], P('row', 'col'), may hold values from -0.21875 to 0.21875
- attend_out: bfloat16 [768, 768], P('col', 'row'), may hold values from -0.875 to 0.875
- second_gain: float32 [768], P('row'), may hold values from 0.5 to 1.5
- router_weight: float32 [768, 16], P('row'), may hold values from -0.15625 to 0.15625
- shared_gate: bfloat16 [768, 2048], P('row', 'col'), may hold values from -0.21875 to 0.21875
- shared_up: bfloat16 [768, 2048], P('row', 'col'), may hold values from -0.21875 to 0.21875
- shared_down: bfloat16 [2048, 768], P('col', 'row'), may hold values from -0.25 to 0.25
- expert_gate: bfloat16 [16, 768, 2048], P(None, 'row', 'col'), may hold values from -0.21875 to 0.21875
- expert_up: bfloat16 [16, 768, 2048], P(None, 'row', 'col'), may hold values from -0.21875 to 0.21875
- expert_down: bfloat16 [16, 2048, 768], P(None, 'col', 'row'), may hold values from -1 to 1
Outputs:
- layer_out: bfloat16 [4096, 768], P(('dp', 'col'), 'row')
- input_grad: bfloat16 [4096, 768], P(('dp', 'col'), 'row')
- first_gain_grad: float32 [768], P('row')
- attend_in_grad: float32 [768, 2304], P('row', 'col')
- attend_out_grad: float32 [768, 768], P('col', 'row')
- second_gain_grad: float32 [768], P('row')
- router_grad: float32 [768, 16], P('row')
- shared_gate_grad: float32 [768, 2048], P('row', 'col')
- shared_up_grad: float32 [768, 2048], P('row', 'col')
- shared_down_grad: float32 [2048, 768], P('col', 'row')
- expert_gate_grad: float32 [16, 768, 2048], P(None, 'row', 'col')
- expert_up_grad: float32 [16, 768, 2048], P(None, 'row', 'col')
- expert_down_grad: float32 [16, 2048, 768], P(None, 'col', 'row')
- balance_loss: float32 [], replicated
The draws below stay inside these ranges and needn't reach their ends.
Inputs may be any that keep to these rules, and one draw needn't show every extreme that they name: `routes`: in each aligned block of 1024 rows, the tokens of one index of dp, the two experts of a token differ and no expert is named by more than 192 entries; some expert is named by exactly 192. `cont_lengths`: each row sums to 512, and some entry equals 128.
All inputs are finite; a program needn't handle non-finite values.
Results may differ from the reference program's by a relative error of at most 0.023.
Values may be sent and summed in bfloat16 or wider, within the bound.
No kernel may reach another device: no remote copies, remote signals or barrier semaphores. Data moves between devices by JAX's collectives and lax.ppermute only.
A program may use at most 384 MiB of HBM per device.

```python
import math
import jax
import jax.numpy as jnp
import numpy as np
from jax import lax

D = 768
H = 12
HD = 64
E = 16
FE = 2048
FS = 2048
NCONT = 8
TOK_DP = 1024
TOKENS = 4096
GL = 1024
CONT = 64
GROUPS = 4
CAP = 192
N_DP = 4


def block_levels(key, dims, split, least, largest):
    def one(dim, parts):
        steps = jax.random.uniform(jax.random.fold_in(jax.random.fold_in(key, 6), dim), (parts,), jnp.float32, least / len(split), largest / len(split))
        return jnp.repeat(jnp.exp(steps), dims[dim] // parts).reshape((-1,) + (1,) * (len(dims) - dim - 1))

    gain = one(*split[0])
    for cut in split[1:]:
        gain = gain * one(*cut)
    return gain


def split_up(number_of, total, limit, slope):
    weights = [(1 << 20) // math.isqrt(rank ** slope) + 1 for rank in range(2, number_of + 1)]
    spare, given = total - limit - (number_of - 1), [1] * (number_of - 1)
    while spare > 0:
        candidates = [i for i in range(number_of - 1) if given[i] < limit]
        whole, budget = sum([weights[i] for i in candidates]), spare
        for i in candidates:
            extra = min(limit - given[i], max(1, budget * weights[i] // whole), spare)
            given[i] = given[i] + extra
            spare = spare - extra
    return np.array([limit] + given)


def uneven_parts(stream_key, number_of, total, most, skew):
    if number_of == 2:
        one = jax.random.randint(stream_key, (), max(1, total - most), min(most, total - 1) + 1)
        return jnp.stack([one, total - one])
    lengths = jnp.asarray(split_up(number_of, total, most, skew), jnp.int32)
    couples = (number_of - 1) // 2
    giver, sink = lengths[1:1 + 2 * couples:2], lengths[2:2 + 2 * couples:2]
    room = jnp.minimum(giver - 1, most - sink)
    passed = jax.random.randint(jax.random.fold_in(stream_key, 1), (couples,), 0, 1 << 20) % (room + 1)
    lengths = lengths.at[1:1 + 2 * couples:2].set(giver - passed).at[2:2 + 2 * couples:2].set(sink + passed)
    return lengths[jax.random.permutation(jax.random.fold_in(stream_key, 2), number_of)]


def deal_out(stream_key, own, number, rows, number_of, top, reach, skew):
    ranking = jax.random.permutation(stream_key, number_of)
    crowded, ordinary = load_shares(number_of, rows * top, reach, skew, True), load_shares(number_of, rows * top, reach, skew, False)
    places = jnp.arange(number_of)

    def named(tallies, turn):
        used = int((tallies > 0).sum())
        fixed = max(1, used // 4)
        moved = fixed + (places - fixed + turn * (used - fixed)) % max(1, number_of - fixed)
        return jnp.zeros((number_of,), jnp.int32).at[ranking[jnp.where(places < fixed, places, moved)]].set(jnp.asarray(tallies, jnp.int32))

    tallies = jnp.where(number % 4 == 0, named(crowded, number // 4), named(ordinary, number - number // 4 - 1))
    mixed = jax.random.permutation(jax.random.fold_in(own, 3), number_of)
    giver, sink = mixed[0:number_of // 2 * 2:2], mixed[1:number_of // 2 * 2:2]
    slack = jnp.minimum(tallies[giver] - 1, reach - tallies[sink]) // 2
    slack = jnp.where((giver == ranking[0]) | (sink == ranking[0]) | (tallies[sink] == 0), 0, jnp.maximum(slack, 0))
    moved = jax.random.randint(jax.random.fold_in(own, 4), (number_of // 2,), 0, 1 << 20) % (slack + 1)
    tallies = tallies.at[giver].add(-moved).at[sink].add(moved)
    labels = jnp.searchsorted(jnp.cumsum(tallies), jnp.arange(rows * top), side="right").astype(jnp.int32)
    listing = labels.reshape(top, rows).T
    listing = listing[jax.random.permutation(jax.random.fold_in(own, 1), rows)]
    turn = jax.random.randint(jax.random.fold_in(own, 2), (rows, 1), 0, top)
    return jnp.take_along_axis(listing, (jnp.arange(top)[None, :] + turn) % top, axis=1)


def load_shares(count, total, limit, lean, full):
    loads = [(1 << 20) // math.isqrt(grade ** lean) + 1 for grade in range(1, count + 1)]
    largest = limit if full else min(limit, max(-(-total // count), total * loads[0] // sum(loads)))
    least = 1 if total - largest >= count - 1 else 0
    given, surplus = [largest] + [least] * (count - 1), total - largest - least * (count - 1)
    while surplus > 0:
        candidates = [i for i in range(1, count) if given[i] < largest] or [i for i in range(1, count) if given[i] < limit]
        pool, budget = sum([loads[i] for i in candidates]), surplus
        for i in candidates:
            addition = min(limit - given[i], max(1, budget * loads[i] // pool), surplus)
            given[i] = given[i] + addition
            surplus = surplus - addition
    return np.array(given)


def gaussian(stream_key, shape, spread, most, split=(), held_as=jnp.bfloat16):
    entries = spread * jax.random.normal(stream_key, shape, jnp.float32)
    if split:
        entries = entries * block_levels(stream_key, shape, split, -0.22, 0.18)
    return jnp.clip(entries, -most, most).astype(held_as)


def setup_inputs(seed: int = 0) -> dict:
    streams_of = jax.random.split(jax.random.key(seed), 16)
    inputs = gaussian(streams_of[0], (TOKENS, D), 1.0, 6.0, ((0, 16), (1, 2)))
    cotangent = gaussian(streams_of[1], (TOKENS, D), 1.0, 6.0, ((0, 16), (1, 2)))
    routes_keys = jax.random.split(jax.random.fold_in(streams_of[2], 1), TOKENS // TOK_DP)
    routes_turns = jax.random.permutation(jax.random.fold_in(streams_of[2], 3), TOKENS // TOK_DP)
    routes = jax.vmap(lambda own, number: deal_out(jax.random.fold_in(streams_of[2], 2), own, number, TOK_DP, E, 2, CAP, 2))(routes_keys, routes_turns).reshape((TOKENS, 2))
    cont_lengths = jax.vmap(lambda own: uneven_parts(own, NCONT, NCONT * CONT, 2 * CONT, 2))(jax.random.split(streams_of[3], GROUPS)).reshape((GROUPS, NCONT)).astype(jnp.int32)
    first_gain = jnp.clip(1.0 + 0.1 * jax.random.normal(streams_of[4], (D,), jnp.float32), 0.5, 1.5)
    attend_in = gaussian(streams_of[5], (D, 3 * H * HD), D ** -0.5, 0.21875, ((0, 2), (1, 4)))
    attend_out = gaussian(streams_of[6], (H * HD, D), (H * HD // 16) ** -0.5, 0.875, ((0, 4), (1, 2)))
    second_gain = jnp.clip(1.0 + 0.1 * jax.random.normal(streams_of[7], (D,), jnp.float32), 0.5, 1.5)
    router_weight = gaussian(streams_of[8], (D, E), (2 * D) ** -0.5, 0.15625, ((0, 2),), jnp.float32)
    shared_gate = gaussian(streams_of[9], (D, FS), D ** -0.5, 0.21875, ((0, 2), (1, 4)))
    shared_up = gaussian(streams_of[10], (D, FS), D ** -0.5, 0.21875, ((0, 2), (1, 4)))
    shared_down = gaussian(streams_of[11], (FS, D), (FS // 4) ** -0.5, 0.25, ((0, 4), (1, 2)))
    expert_gate = gaussian(streams_of[12], (E, D, FE), D ** -0.5, 0.21875, ((1, 2), (2, 4)))
    expert_up = gaussian(streams_of[13], (E, D, FE), D ** -0.5, 0.21875, ((1, 2), (2, 4)))
    expert_down = gaussian(streams_of[14], (E, FE, D), (max(FE // 64, 1)) ** -0.5, 1.0, ((1, 4), (2, 2)))
    return dict(inputs=inputs, cotangent=cotangent, routes=routes, cont_lengths=cont_lengths, first_gain=first_gain, attend_in=attend_in, attend_out=attend_out, second_gain=second_gain, router_weight=router_weight, shared_gate=shared_gate, shared_up=shared_up, shared_down=shared_down, expert_gate=expert_gate, expert_up=expert_up, expert_down=expert_down)


EPSILON = 1e-05
HIGHEST = lax.Precision.HIGHEST

@jax.custom_vjp
def low(v):
    return lax.optimization_barrier(v.astype(jnp.bfloat16)).astype(jnp.float32)

@jax.custom_vjp
def low_back(v):
    return v

def low_keep(v):
    return (low(v), None)

def low_pass(kept, grad):
    return (grad,)

def back_keep(v):
    return (v, None)

def back_low(kept, grad):
    return (low(grad),)
low.defvjp(low_keep, low_pass)
low_back.defvjp(back_keep, back_low)

def product(left, right):
    return jnp.dot(left, right, precision=HIGHEST)

def angle_table(position):
    half_dim = HD // 2
    frequency = 10000.0 ** (-jnp.arange(half_dim, dtype=jnp.float32) * 2.0 / HD)
    return position.astype(jnp.float32)[:, None] * frequency[None, :]

def rotate(values, angles):
    half_dim = values.shape[-1] // 2
    cosine = jnp.cos(angles)[:, None, :]
    sine_part = jnp.sin(angles)[:, None, :]
    first_half = values[..., :half_dim]
    second_half = values[..., half_dim:]
    return jnp.concatenate([first_half * cosine - second_half * sine_part, first_half * sine_part + second_half * cosine], -1)

def token_layout(cont_lengths, offsets, group_len):
    prompt_len = group_len // 2
    group_ids = offsets // group_len
    inner_pos = offsets % group_len
    seg_ends = jnp.cumsum(cont_lengths, axis=1)
    seg_starts = seg_ends - cont_lengths
    group_pick = (group_ids[:, None] == jnp.arange(cont_lengths.shape[0], dtype=jnp.int32)[None, :]).astype(jnp.int32)
    ends_own = lax.optimization_barrier(jnp.sum(group_pick[:, :, None] * seg_ends[None, :, :], 1))
    starts_own = lax.optimization_barrier(jnp.sum(group_pick[:, :, None] * seg_starts[None, :, :], 1))
    after_prompt = inner_pos - prompt_len
    segment = 1 + lax.optimization_barrier(jnp.sum((after_prompt[:, None] >= ends_own).astype(jnp.int32), 1))
    segment = jnp.where(after_prompt < 0, 0, segment)
    slot_pick = segment[:, None] - 1 == jnp.arange(cont_lengths.shape[1], dtype=jnp.int32)[None, :]
    seg_begin = lax.optimization_barrier(jnp.sum(jnp.where(slot_pick, starts_own, 0), 1))
    position = jnp.where(segment == 0, inner_pos, prompt_len + after_prompt - seg_begin)
    return (group_ids, segment, position)

def slot_table(block_routes):
    flat_routes = block_routes.reshape(-1)
    flat_hot = (flat_routes[:, None] == jnp.arange(E, dtype=jnp.int32)[None, :]).astype(jnp.int32)
    earlier = jnp.cumsum(flat_hot, 0) - flat_hot
    slot_of = flat_routes * CAP + lax.optimization_barrier(jnp.sum(earlier * flat_hot, 1))
    entry_ids = jnp.arange(flat_routes.shape[0], dtype=jnp.int32)
    source = jnp.full((E * CAP,), flat_routes.shape[0], jnp.int32).at[slot_of].set(entry_ids)
    return (slot_of, source)

def attend_group(pieces):
    queries, key_rows, value_rows, segment, position = pieces
    scores = jnp.einsum('qhd,khd->hqk', queries, key_rows, precision=HIGHEST) * HD ** (-0.5)
    visible = ((segment[None, :] == 0) | (segment[None, :] == segment[:, None])) & (position[None, :] <= position[:, None])
    scores = jnp.where(visible[None], scores, -1e+30)
    weights = jax.nn.softmax(scores, -1)
    return jnp.einsum('hqk,khd->qhd', weights, value_rows, precision=HIGHEST)

def run_experts(normed, source, gate_w, up_w, down_w):
    padded = jnp.concatenate([normed, jnp.zeros((1, normed.shape[1]), normed.dtype)], 0)
    slot_rows = padded[source // 2].reshape(E, CAP, normed.shape[1])
    pre_gate = low_back(jnp.einsum('ecd,edf->ecf', slot_rows, gate_w, precision=HIGHEST))
    pre_up = low_back(jnp.einsum('ecd,edf->ecf', slot_rows, up_w, precision=HIGHEST))
    hidden = low(jax.nn.silu(pre_gate) * pre_up)
    return low_back(jnp.einsum('ecf,efd->ecd', hidden, down_w, precision=HIGHEST)).reshape(E * CAP, normed.shape[1])

def pick_rows(table_rows, row_ids):
    return table_rows[row_ids]

def reference(inputs, cotangent, routes, cont_lengths, first_gain, attend_in, attend_out, second_gain, router_weight, shared_gate, shared_up, shared_down, expert_gate, expert_up, expert_down):
    total = inputs.shape[0]
    offsets = jnp.arange(total, dtype=jnp.int32)
    group_ids, segment, position = token_layout(cont_lengths, offsets, GL)
    angles = angle_table(position)
    slot_pairs, sources = jax.vmap(slot_table)(routes.reshape(N_DP, TOK_DP, 2))
    route_hot = routes[:, :, None] == jnp.arange(E, dtype=jnp.int32)[None, None, :]
    counts = lax.optimization_barrier(jnp.sum(route_hot.astype(jnp.float32), (0, 1)))

    def forward(inputs_f, first_gain, attend_in, attend_out, second_gain, router_weight, shared_gate, shared_up, shared_down, expert_gate, expert_up, expert_down):
        scale_one = lax.rsqrt(lax.optimization_barrier(jnp.mean(inputs_f * inputs_f, -1, keepdims=True)) + EPSILON)
        normed_one = low(inputs_f * scale_one * first_gain)
        qkv_raw = low_back(product(normed_one, attend_in)).reshape(total, H, 3, HD)
        queries = low(rotate(qkv_raw[:, :, 0], angles))
        key_rows = low(rotate(qkv_raw[:, :, 1], angles))
        value_rows = low(qkv_raw[:, :, 2])
        shaped = (queries.reshape(GROUPS, GL, H, HD), key_rows.reshape(GROUPS, GL, H, HD), value_rows.reshape(GROUPS, GL, H, HD), segment.reshape(GROUPS, GL), position.reshape(GROUPS, GL))
        attended = lax.map(jax.checkpoint(attend_group), shaped).reshape(total, H * HD)
        attn_low = low(low_back(attended))
        mixed_one = inputs_f + low_back(product(attn_low, attend_out))
        scale_two = lax.rsqrt(lax.optimization_barrier(jnp.mean(mixed_one * mixed_one, -1, keepdims=True)) + EPSILON)
        unit_two = mixed_one * scale_two * second_gain
        router_probs = jax.nn.softmax(product(unit_two, router_weight), -1)
        gate_vals = lax.optimization_barrier(jnp.sum(jnp.where(route_hot, router_probs[:, None, :], 0.0), -1))
        balance = E * jnp.sum(counts / (2.0 * total) * lax.optimization_barrier(jnp.mean(router_probs, 0)))
        normed_two = low(unit_two)
        shared_g = low_back(product(normed_two, shared_gate))
        shared_u = low_back(product(normed_two, shared_up))
        shared_hidden = low(jax.nn.silu(shared_g) * shared_u)
        shared_result = low_back(product(shared_hidden, shared_down))

        def expert_block(pieces):
            return run_experts(pieces[0], pieces[1], expert_gate, expert_up, expert_down)
        expert_out = lax.map(jax.checkpoint(expert_block), (normed_two.reshape(N_DP, TOK_DP, D), sources))
        picked = jax.vmap(pick_rows)(expert_out, slot_pairs).reshape(total, 2, D)
        expert_result = lax.optimization_barrier(jnp.sum(gate_vals[:, :, None] * picked, 1))
        return (mixed_one + shared_result + expert_result, balance)
    primals = (inputs.astype(jnp.float32), first_gain, attend_in.astype(jnp.float32), attend_out.astype(jnp.float32), second_gain, router_weight, shared_gate.astype(jnp.float32), shared_up.astype(jnp.float32), shared_down.astype(jnp.float32), expert_gate.astype(jnp.float32), expert_up.astype(jnp.float32), expert_down.astype(jnp.float32))
    (layer_sum, balance), pullback = jax.vjp(forward, *primals)
    all_grads = pullback((cotangent.astype(jnp.float32), jnp.ones((), jnp.float32)))
    return (layer_sum.astype(jnp.bfloat16), all_grads[0].astype(jnp.bfloat16), all_grads[1], all_grads[2], all_grads[3], all_grads[4], all_grads[5], all_grads[6], all_grads[7], all_grads[8], all_grads[9], all_grads[10], all_grads[11], balance)
```

```python
import functools

import jax
import jax.numpy as jnp
from jax import lax
from jax.experimental import pallas as pl
from jax.experimental.pallas import tpu as pltpu
from jax.sharding import PartitionSpec as P

HD = 64


EPSILON = 1e-05
HIGHEST = lax.Precision.HIGHEST


def for_sending(value):
    return jax.tree.map(lambda a: a.astype(jnp.bfloat16) if a.dtype == jnp.float32 else a, value)


def feature_sums(values):
    return lax.psum(values, "row")


def token_gather(values):
    return lax.all_gather(values, "col", axis=0, tiled=True)


def slot_gather(values):
    return jax.tree.map(
        lambda part, own: part.astype(own.dtype),
        lax.all_gather(for_sending(values), "row", axis=0, tiled=True),
        values,
    )


def row_partials(term_fn, row_count):
    return lax.psum_scatter(
        term_fn(jnp.int32(0), lax.axis_size("row") * row_count),
        "row",
        scatter_dimension=0,
        tiled=True,
    )


def col_partials(term_fn, row_count):
    return lax.psum_scatter(
        term_fn(jnp.int32(0), lax.axis_size("col") * row_count).astype(jnp.bfloat16),
        "col",
        scatter_dimension=0,
        tiled=True,
    ).astype(jnp.float32)


def token_stats(values):
    return lax.psum(values, ("dp", "col"))


def rows_of(source, row_start, row_count):
    return lax.dynamic_slice_in_dim(source, row_start, row_count, 0)


def angle_table(position):
    half_dim = HD // 2
    frequency = 10000.0 ** (-jnp.arange(half_dim, dtype=jnp.float32) * 2.0 / HD)
    return position.astype(jnp.float32)[:, None] * frequency[None, :]


def rotate(values, angles):
    half_dim = values.shape[-1] // 2
    cosine = jnp.cos(angles)[:, None, :]
    sine_part = jnp.sin(angles)[:, None, :]
    first_half = values[..., :half_dim]
    second_half = values[..., half_dim:]
    return jnp.concatenate(
        [
            first_half * cosine - second_half * sine_part,
            first_half * sine_part + second_half * cosine,
        ],
        -1,
    )


def token_layout(cont_lengths, offsets, group_len):
    prompt_len = group_len // 2
    group_ids = offsets // group_len
    inner_pos = offsets % group_len
    seg_ends = jnp.cumsum(cont_lengths, axis=1)
    seg_starts = seg_ends - cont_lengths
    group_pick = (
        group_ids[:, None] == jnp.arange(cont_lengths.shape[0], dtype=jnp.int32)[None, :]
    ).astype(jnp.int32)
    ends_own = jnp.sum(group_pick[:, :, None] * seg_ends[None, :, :], 1)
    starts_own = jnp.sum(group_pick[:, :, None] * seg_starts[None, :, :], 1)
    after_prompt = inner_pos - prompt_len
    segment = 1 + jnp.sum((after_prompt[:, None] >= ends_own).astype(jnp.int32), 1)
    segment = jnp.where(after_prompt < 0, 0, segment)
    slot_pick = segment[:, None] - 1 == jnp.arange(cont_lengths.shape[1], dtype=jnp.int32)[None, :]
    seg_begin = jnp.sum(jnp.where(slot_pick, starts_own, 0), 1)
    position = jnp.where(segment == 0, inner_pos, prompt_len + after_prompt - seg_begin)
    return (group_ids, segment, position)


def gate_up_grad(pre_gate, pre_up, hidden_grad):
    gate_sig = jax.nn.sigmoid(pre_gate)
    grad_gate = hidden_grad * pre_up * gate_sig * (1.0 + pre_gate * (1.0 - gate_sig))
    grad_up = hidden_grad * pre_gate * gate_sig
    return jnp.concatenate([grad_gate, grad_up], 1).astype(jnp.bfloat16)


def body(
    inputs,
    cotangent,
    routes,
    cont_lengths,
    first_gain,
    attend_in,
    attend_out,
    second_gain,
    router_weight,
    shared_gate,
    shared_up,
    shared_down,
    expert_gate,
    expert_up,
    expert_down,
):
    row_size = lax.axis_size("row")
    col_size = lax.axis_size("col")
    data_size = lax.axis_size("dp")
    row_index = lax.axis_index("row")
    col_index = lax.axis_index("col")
    tok_rest, feat_dev = inputs.shape
    feat_full = feat_dev * row_size
    tok_block = tok_rest * col_size
    tok_query = tok_block // row_size
    experts = expert_gate.shape[0]
    hidden_dev = expert_gate.shape[2]
    shared_dev = shared_gate.shape[1]
    head_cols = attend_in.shape[1]
    heads_dev = head_cols // (3 * HD)
    capacity = tok_block * 3 // experts
    slots_dev = experts * capacity // row_size
    group_len = tok_block // cont_lengths.shape[0]
    key_block = min(1024, tok_query)
    block_count = group_len // key_block
    score_scale = HD ** (-0.5)
    tokens_all = float(data_size * tok_block)
    group_base = row_index * tok_query // group_len * group_len
    inputs_f = inputs.astype(jnp.float32)
    squares_one = feature_sums(jnp.sum(inputs_f * inputs_f, 1))
    scale_one = lax.rsqrt(squares_one / feat_full + EPSILON)[:, None]
    normed_one = (inputs_f * scale_one * first_gain).astype(jnp.bfloat16)
    normed_all = token_gather(normed_one)

    def qkv_term(row_start, row_count):
        return jnp.dot(
            rows_of(normed_all, row_start, row_count), attend_in, preferred_element_type=jnp.float32
        )

    qkv_raw = row_partials(qkv_term, tok_query).reshape(tok_query, heads_dev, 3, HD)
    query_offsets = row_index * tok_query + jnp.arange(tok_query, dtype=jnp.int32)
    query_group, query_segment, query_position = token_layout(
        cont_lengths, query_offsets, group_len
    )
    key_group, key_segment, key_position = token_layout(
        cont_lengths, jnp.arange(tok_block, dtype=jnp.int32), group_len
    )
    query_angles = angle_table(query_position)
    queries = rotate(qkv_raw[:, :, 0], query_angles).astype(jnp.bfloat16)
    keys_own = rotate(qkv_raw[:, :, 1], query_angles).astype(jnp.bfloat16)
    values_own = qkv_raw[:, :, 2].astype(jnp.bfloat16)
    keys_all, values_all = slot_gather(
        (keys_own.reshape(tok_query, heads_dev * HD), values_own.reshape(tok_query, heads_dev * HD))
    )

    def block_scores(block_start):
        key_rows = rows_of(keys_all, block_start, key_block).reshape(key_block, heads_dev, HD)
        block_group = rows_of(key_group, block_start, key_block)
        block_segment = rows_of(key_segment, block_start, key_block)
        block_position = rows_of(key_position, block_start, key_block)
        visible = (
            (query_group[:, None] == block_group[None, :])
            & ((block_segment[None, :] == 0) | (block_segment[None, :] == query_segment[:, None]))
            & (block_position[None, :] <= query_position[:, None])
        )
        scores = (
            jnp.einsum("qhd,khd->hqk", queries, key_rows, preferred_element_type=jnp.float32)
            * score_scale
        )
        return (scores, visible[None], key_rows)

    def forward_step(carry, block_index):
        run_max, run_total, run_accum = carry
        block_start = group_base + block_index * key_block
        scores, mask_now, key_rows = block_scores(block_start)
        value_rows = (
            rows_of(values_all, block_start, key_block)
            .reshape(key_block, heads_dev, HD)
            .astype(jnp.float32)
        )
        new_max = jnp.maximum(run_max, jnp.max(jnp.where(mask_now, scores, -1e30), -1))
        weights = jnp.where(mask_now, jnp.exp(scores - new_max[..., None]), 0.0)
        run_decay = jnp.exp(run_max - new_max)
        run_total = run_total * run_decay + jnp.sum(weights, -1)
        run_accum = run_accum * run_decay[..., None] + jnp.einsum(
            "hqk,khd->hqd", weights, value_rows, precision=HIGHEST
        )
        return ((new_max, run_total, run_accum), None)

    start_carry = (
        jnp.full((heads_dev, tok_query), -1e30, jnp.float32),
        jnp.zeros((heads_dev, tok_query), jnp.float32),
        jnp.zeros((heads_dev, tok_query, HD), jnp.float32),
    )
    (run_max, run_total, run_accum), unused_out = lax.scan(
        forward_step, start_carry, jnp.arange(block_count, dtype=jnp.int32)
    )
    log_total = run_max + jnp.log(run_total)
    attended = run_accum / run_total[..., None]
    attn_rows = attended.transpose(1, 0, 2).reshape(tok_query, heads_dev * HD).astype(jnp.bfloat16)
    outputs_all = slot_gather(attn_rows)

    def attention_term(row_start, row_count):
        return jnp.dot(
            rows_of(outputs_all, row_start, row_count),
            attend_out,
            preferred_element_type=jnp.float32,
        )

    mixed_one = inputs_f + col_partials(attention_term, tok_rest)
    gained = mixed_one * second_gain
    squares_two, logit_part = feature_sums(
        (jnp.sum(mixed_one * mixed_one, 1), jnp.dot(gained, router_weight, precision=HIGHEST))
    )
    scale_two = lax.rsqrt(squares_two / feat_full + EPSILON)[:, None]
    router_probs = jax.nn.softmax(logit_part * scale_two, -1)
    routes_rest = lax.dynamic_slice_in_dim(routes, col_index * tok_rest, tok_rest, 0)
    route_hot = routes_rest[:, :, None] == jnp.arange(experts, dtype=jnp.int32)[None, None, :]
    gate_vals = jnp.sum(jnp.where(route_hot, router_probs[:, None, :], 0.0), -1)
    count_total, prob_total = token_stats(
        (jnp.sum(route_hot.astype(jnp.float32), (0, 1)), jnp.sum(router_probs, 0))
    )
    balance_loss = experts * jnp.sum(count_total / (2.0 * tokens_all) * prob_total / tokens_all)
    unit_two = mixed_one * scale_two
    normed_two = (unit_two * second_gain).astype(jnp.bfloat16)
    normed_two_all = token_gather(normed_two)
    flat_routes = routes.reshape(-1)
    flat_hot = (flat_routes[:, None] == jnp.arange(experts, dtype=jnp.int32)[None, :]).astype(
        jnp.int32
    )
    earlier = jnp.cumsum(flat_hot, 0) - flat_hot
    slot_of = flat_routes * capacity + jnp.sum(earlier * flat_hot, 1)
    slot_pairs = slot_of.reshape(tok_block, 2)
    slot_source = (
        jnp.full((experts * capacity,), 2 * tok_block, jnp.int32)
        .at[slot_of]
        .set(jnp.arange(2 * tok_block, dtype=jnp.int32))
    )
    padded_two = jnp.concatenate([normed_two_all, jnp.zeros((1, feat_dev), jnp.bfloat16)], 0)
    expert_rows = padded_two[slot_source // 2]
    shared_both = jnp.concatenate([shared_gate, shared_up], 1)

    def shared_term(row_start, row_count):
        return jnp.dot(
            rows_of(normed_two_all, row_start, row_count),
            shared_both,
            preferred_element_type=jnp.float32,
        )

    shared_pre = row_partials(shared_term, tok_query)
    shared_g = shared_pre[:, :shared_dev]
    shared_u = shared_pre[:, shared_dev:]
    shared_hidden = (jax.nn.silu(shared_g) * shared_u).astype(jnp.bfloat16)
    expert_both = jnp.concatenate([expert_gate, expert_up], 2)

    def expert_term(row_start, row_count):
        group_count = row_count // capacity
        picked = rows_of(expert_rows, row_start, row_count).reshape(group_count, capacity, feat_dev)
        return jnp.einsum(
            "ecd,edf->ecf", picked, expert_both, preferred_element_type=jnp.float32
        ).reshape(row_count, 2 * hidden_dev)

    expert_pre = row_partials(expert_term, slots_dev)
    expert_g = expert_pre[:, :hidden_dev]
    expert_u = expert_pre[:, hidden_dev:]
    expert_hidden = (jax.nn.silu(expert_g) * expert_u).astype(jnp.bfloat16)
    shared_all, expert_all = slot_gather((shared_hidden, expert_hidden))
    expert_out = jnp.einsum(
        "ecf,efd->ecd",
        expert_all.reshape(experts, capacity, hidden_dev),
        expert_down,
        preferred_element_type=jnp.float32,
    ).reshape(experts * capacity, feat_dev)

    def output_term(row_start, row_count):
        shared_part = jnp.dot(
            rows_of(shared_all, row_start, row_count),
            shared_down,
            preferred_element_type=jnp.float32,
        )
        pair_slots = rows_of(slot_pairs, row_start, row_count)
        return jnp.concatenate(
            [shared_part, expert_out[pair_slots[:, 0]], expert_out[pair_slots[:, 1]]], 1
        )

    branch_sums = col_partials(output_term, tok_rest)
    shared_result = branch_sums[:, :feat_dev]
    expert_pick = branch_sums[:, feat_dev:].reshape(tok_rest, 2, feat_dev)
    expert_result = jnp.sum(gate_vals[:, :, None] * expert_pick, 1)
    layer_out = (mixed_one + shared_result + expert_result).astype(jnp.bfloat16)
    cot_f = cotangent.astype(jnp.float32)
    gate_grad = feature_sums(jnp.sum(expert_pick * cot_f[:, None, :], -1))
    expert_cot = (
        (gate_vals[:, :, None] * cot_f[:, None, :])
        .astype(jnp.bfloat16)
        .reshape(tok_rest, 2 * feat_dev)
    )
    cot_all = token_gather(jnp.concatenate([cotangent, expert_cot], 1))
    shared_cot = cot_all[:, :feat_dev]
    pair_cot = jnp.concatenate(
        [
            cot_all[:, feat_dev:].reshape(2 * tok_block, feat_dev),
            jnp.zeros((1, feat_dev), jnp.bfloat16),
        ],
        0,
    )
    slot_cot = pair_cot[slot_source]
    shared_down_grad = jnp.einsum(
        "tf,td->fd", shared_all, shared_cot, preferred_element_type=jnp.float32
    )

    def shared_back(row_start, row_count):
        return jnp.einsum(
            "td,fd->tf",
            rows_of(shared_cot, row_start, row_count),
            shared_down,
            preferred_element_type=jnp.float32,
        )

    shared_pgrad = gate_up_grad(shared_g, shared_u, row_partials(shared_back, tok_query))
    expert_down_grad = jnp.einsum(
        "ecf,ecd->efd",
        expert_all.reshape(experts, capacity, hidden_dev),
        slot_cot.reshape(experts, capacity, feat_dev),
        preferred_element_type=jnp.float32,
    )

    def expert_back(row_start, row_count):
        group_count = row_count // capacity
        picked = rows_of(slot_cot, row_start, row_count).reshape(group_count, capacity, feat_dev)
        return jnp.einsum(
            "ecd,efd->ecf", picked, expert_down, preferred_element_type=jnp.float32
        ).reshape(row_count, hidden_dev)

    expert_pgrad = gate_up_grad(expert_g, expert_u, row_partials(expert_back, slots_dev))
    shared_pall, expert_pall = slot_gather((shared_pgrad, expert_pgrad))
    expert_pall_view = expert_pall.reshape(experts, capacity, 2 * hidden_dev)
    expert_both_grad = jnp.einsum(
        "ecd,ecf->edf",
        expert_rows.reshape(experts, capacity, feat_dev),
        expert_pall_view,
        preferred_element_type=jnp.float32,
    )
    expert_input_grad = jnp.einsum(
        "ecf,edf->ecd", expert_pall_view, expert_both, preferred_element_type=jnp.float32
    ).reshape(experts * capacity, feat_dev)
    shared_both_grad = jnp.einsum(
        "td,tf->df", normed_two_all, shared_pall, preferred_element_type=jnp.float32
    )

    def normed_back(row_start, row_count):
        pair_slots = rows_of(slot_pairs, row_start, row_count)
        shared_part = jnp.einsum(
            "tf,df->td",
            rows_of(shared_pall, row_start, row_count),
            shared_both,
            preferred_element_type=jnp.float32,
        )
        return (
            shared_part + expert_input_grad[pair_slots[:, 0]] + expert_input_grad[pair_slots[:, 1]]
        )

    normed_grad = col_partials(normed_back, tok_rest)
    prob_grad = jnp.sum(
        jnp.where(route_hot, gate_grad[:, :, None], 0.0), 1
    ) + experts * count_total / (2.0 * tokens_all * tokens_all)
    logit_grad = router_probs * (prob_grad - jnp.sum(router_probs * prob_grad, -1, keepdims=True))
    router_grad = jnp.einsum("td,te->de", unit_two * second_gain, logit_grad, precision=HIGHEST)
    two_grad = normed_grad + jnp.einsum("te,de->td", logit_grad, router_weight, precision=HIGHEST)
    gained_two = two_grad * second_gain
    second_gain_grad = jnp.sum(two_grad * unit_two, 0)
    inner_two = feature_sums(jnp.sum(gained_two * unit_two, 1))[:, None] / feat_full
    mixed_grad = cot_f + scale_two * (gained_two - unit_two * inner_two)
    mix_all = token_gather(mixed_grad.astype(jnp.bfloat16))
    attend_out_grad = jnp.einsum(
        "tc,td->cd", outputs_all, mix_all, preferred_element_type=jnp.float32
    )

    def output_back(row_start, row_count):
        return jnp.einsum(
            "td,cd->tc",
            rows_of(mix_all, row_start, row_count),
            attend_out,
            preferred_element_type=jnp.float32,
        )

    attn_grad = (
        row_partials(output_back, tok_query).astype(jnp.bfloat16).reshape(tok_query, heads_dev, HD)
    )
    attn_grad_f = attn_grad.astype(jnp.float32)
    row_delta = jnp.sum(attn_grad_f.transpose(1, 0, 2) * attended, -1)
    queries_f = queries.astype(jnp.float32)

    def backward_step(query_grad, block_index):
        block_start = group_base + block_index * key_block
        scores, mask_now, key_rows = block_scores(block_start)
        value_rows = rows_of(values_all, block_start, key_block).reshape(key_block, heads_dev, HD)
        weights = jnp.where(mask_now, jnp.exp(scores - log_total[..., None]), 0.0)
        prob_dot = jnp.einsum(
            "qhd,khd->hqk", attn_grad, value_rows, preferred_element_type=jnp.float32
        )
        score_grad = weights * (prob_dot - row_delta[..., None])
        query_grad = (
            query_grad
            + jnp.einsum(
                "hqk,khd->qhd", score_grad, key_rows.astype(jnp.float32), precision=HIGHEST
            )
            * score_scale
        )
        key_grad = (
            jnp.einsum("hqk,qhd->khd", score_grad, queries_f, precision=HIGHEST) * score_scale
        )
        value_grad = jnp.einsum("hqk,qhd->khd", weights, attn_grad_f, precision=HIGHEST)
        return (
            query_grad,
            jnp.concatenate(
                [
                    key_grad.reshape(key_block, heads_dev * HD),
                    value_grad.reshape(key_block, heads_dev * HD),
                ],
                1,
            ),
        )

    query_grad, kv_terms = lax.scan(
        backward_step,
        jnp.zeros((tok_query, heads_dev, HD), jnp.float32),
        jnp.arange(block_count, dtype=jnp.int32),
    )
    kv_group = kv_terms.reshape(group_len, 2 * heads_dev * HD)
    kv_full = lax.dynamic_update_slice_in_dim(
        jnp.zeros((tok_block, 2 * heads_dev * HD), jnp.float32), kv_group, group_base, 0
    )

    def kv_term(row_start, row_count):
        return rows_of(kv_full, row_start, row_count)

    kv_grad = row_partials(kv_term, tok_query)
    key_grad_raw = rotate(
        kv_grad[:, : heads_dev * HD].reshape(tok_query, heads_dev, HD), -query_angles
    )
    value_grad_raw = kv_grad[:, heads_dev * HD :].reshape(tok_query, heads_dev, HD)
    query_grad_raw = rotate(query_grad, -query_angles)
    qkv_grad = (
        jnp.stack([query_grad_raw, key_grad_raw, value_grad_raw], 2)
        .reshape(tok_query, head_cols)
        .astype(jnp.bfloat16)
    )
    qkv_all = slot_gather(qkv_grad)
    attend_in_grad = jnp.einsum(
        "td,tc->dc", normed_all, qkv_all, preferred_element_type=jnp.float32
    )

    def input_back(row_start, row_count):
        return jnp.einsum(
            "tc,dc->td",
            rows_of(qkv_all, row_start, row_count),
            attend_in,
            preferred_element_type=jnp.float32,
        )

    one_grad = col_partials(input_back, tok_rest)
    unit_one = inputs_f * scale_one
    gained_one = one_grad * first_gain
    first_gain_grad = jnp.sum(one_grad * unit_one, 0)
    inner_one = feature_sums(jnp.sum(gained_one * unit_one, 1))[:, None] / feat_full
    input_grad = (mixed_grad + scale_one * (gained_one - unit_one * inner_one)).astype(jnp.bfloat16)
    first_gain_grad, second_gain_grad, router_grad = token_stats(
        (first_gain_grad, second_gain_grad, router_grad)
    )
    summed = (
        lax.psum(attend_in_grad.astype(jnp.bfloat16), "dp").astype(jnp.float32),
        lax.psum(attend_out_grad.astype(jnp.bfloat16), "dp").astype(jnp.float32),
        lax.psum(shared_both_grad.astype(jnp.bfloat16), "dp").astype(jnp.float32),
        lax.psum(shared_down_grad.astype(jnp.bfloat16), "dp").astype(jnp.float32),
        lax.psum(expert_both_grad.astype(jnp.bfloat16), "dp").astype(jnp.float32),
        lax.psum(expert_down_grad.astype(jnp.bfloat16), "dp").astype(jnp.float32),
    )
    shared_both_sum = summed[2]
    expert_both_sum = summed[4]
    return (
        layer_out,
        input_grad,
        first_gain_grad,
        summed[0],
        summed[1],
        second_gain_grad,
        router_grad,
        shared_both_sum[:, :shared_dev],
        shared_both_sum[:, shared_dev:],
        summed[3],
        expert_both_sum[:, :, :hidden_dev],
        expert_both_sum[:, :, hidden_dev:],
        summed[5],
        balance_loss,
    )


F32 = jnp.float32
BF16 = jnp.bfloat16
MASKED = -1e30


def swap(value, axis, step=1):
    size = lax.axis_size(axis)
    return lax.ppermute(value, axis, [(i, i ^ step) for i in range(size)])


def shifted(value, axis, step):
    size = lax.axis_size(axis)
    return lax.ppermute(value, axis, [(i, (i + step) % size) for i in range(size)])


def in_order(parts, axis):
    size, me = len(parts), lax.axis_index(axis)
    whole = jnp.zeros((size,) + parts[0].shape, parts[0].dtype)
    for step, part in enumerate(parts):
        whole = lax.dynamic_update_index_in_dim(whole, part, (me - step) % size, 0)
    return whole


def col_parts(value):
    return [value] + [shifted(value, "col", s) for s in range(1, lax.axis_size("col"))]


def col_rows(value):
    whole = in_order(col_parts(value), "col")
    return whole.reshape((-1,) + value.shape[1:])


def col_sum_rows(whole):
    size, me = lax.axis_size("col"), lax.axis_index("col")
    blocks = whole.reshape((size, whole.shape[0] // size) + whole.shape[1:])
    total = lax.dynamic_index_in_dim(blocks, me, 0, False).astype(F32)
    for step in range(1, size):
        block = lax.dynamic_index_in_dim(blocks, (me + step) % size, 0, False)
        total = total + shifted(block, "col", step).astype(F32)
    return total


def sum_by_swaps(value, axes):
    for axis in axes:
        step = 1
        while step < lax.axis_size(axis):
            value = value + swap(value, axis, step)
            step *= 2
    return value


def pair_halves(whole):
    core = lax.axis_index("dp") % 2
    halves = whole.reshape((2, whole.shape[0] // 2) + whole.shape[1:])
    mine = lax.dynamic_index_in_dim(halves, core, 0, False)
    other = lax.dynamic_index_in_dim(halves, 1 - core, 0, False)
    half = (mine.astype(F32) + swap(other, "dp", 1).astype(F32)).astype(BF16)
    step = 2
    while step < lax.axis_size("dp"):
        half = (half.astype(F32) + swap(half, "dp", step).astype(F32)).astype(BF16)
        step *= 2
    return half, swap(half, "dp", 1)


def dp_total(whole):
    core = lax.axis_index("dp") % 2
    half, rest = pair_halves(whole)
    first = jnp.where(core == 0, half, rest)
    second = jnp.where(core == 0, rest, half)
    return jnp.concatenate([first, second], 0).astype(F32)


def matmul(left, right, left_dim, right_dim):
    return lax.dot_general(
        left, right, (((left_dim,), (right_dim,)), ((), ())), preferred_element_type=F32
    )


def whole_block(shape):
    return pl.BlockSpec(shape, lambda *unused: (0,) * len(shape))


def visible_to(start_rows, row_base, row_count, key_count, prompt_len):
    row_ids = row_base + lax.broadcasted_iota(jnp.int32, (row_count, key_count), 0)
    key_ids = lax.broadcasted_iota(jnp.int32, (row_count, key_count), 1)
    own_segment = (key_ids < prompt_len) | (key_ids >= start_rows)
    return (key_ids <= row_ids) & own_segment


def attend_kernel(
    heads, block, prompt_len, scale,
    left_ref, right_ref, weight_left_ref, weight_right_ref, out_weight_ref, cos_ref, sin_ref, start_ref,
    qkv_ref, attended_ref, log_ref, partial_ref,
):
    raw = jnp.dot(left_ref[...], weight_left_ref[...], preferred_element_type=F32)
    raw = raw + jnp.dot(right_ref[...], weight_right_ref[...], preferred_element_type=F32)
    cosine, sine = cos_ref[...], sin_ref[...]
    half = HD // 2
    tokens = raw.shape[0]
    partial = jnp.zeros(partial_ref.shape, F32)
    for head in range(heads):
        base = head * 3 * HD
        for kind in range(3):
            piece = raw[:, base + kind * HD : base + (kind + 1) * HD]
            if kind < 2:
                one, two = piece[:, :half], piece[:, half:]
                piece = jnp.concatenate(
                    [one * cosine - two * sine, one * sine + two * cosine], 1
                )
            qkv_ref[3 * head + kind] = piece.astype(BF16)
        for low in range(0, tokens, block):
            rows = pl.ds(low, block)
            keys = low + block
            scores = matmul(qkv_ref[3 * head, rows], qkv_ref[3 * head + 1, :keys], 1, 1) * scale
            seen = visible_to(start_ref[rows], low, block, keys, prompt_len)
            scores = jnp.where(seen, scores, MASKED)
            top = jnp.max(scores, 1, keepdims=True)
            weights = jnp.exp(scores - top)
            total = jnp.sum(weights, 1, keepdims=True)
            result = matmul(weights.astype(BF16), qkv_ref[3 * head + 2, :keys], 1, 0) / total
            attended_ref[head, rows] = result
            log_ref[head, rows] = top + jnp.log(total)
        partial = partial + jnp.dot(
            attended_ref[head].astype(BF16),
            out_weight_ref[head * HD : (head + 1) * HD],
            preferred_element_type=F32,
        )
    partial_ref[...] = partial.astype(BF16)


def attend(left, right, weight_left, weight_right, out_weight, cosine, sine, start, block):
    tokens, features = left.shape
    heads = weight_left.shape[1] // (3 * HD)
    pairs = sum(block * (low + block) for low in range(0, tokens, block)) * heads
    return pl.pallas_call(
        functools.partial(attend_kernel, heads, block, tokens // 2, HD ** (-0.5)),
        out_shape=(
            jax.ShapeDtypeStruct((3 * heads, tokens, HD), BF16),
            jax.ShapeDtypeStruct((heads, tokens, HD), F32),
            jax.ShapeDtypeStruct((heads, tokens, 1), F32),
            jax.ShapeDtypeStruct((tokens, features), BF16),
        ),
        cost_estimate=pl.CostEstimate(
            flops=4 * pairs * HD + 4 * tokens * features * 3 * HD * heads,
            transcendentals=pairs,
            bytes_accessed=8 * tokens * features,
        ),
        name="attend",
    )(left, right, weight_left, weight_right, out_weight, cosine, sine, start)


def attend_back_kernel(
    heads, block, prompt_len, scale,
    own_ref, peer_ref, qkv_ref, attended_ref, log_ref, cos_ref, sin_ref, start_ref, normed_ref, weight_ref,
    one_ref, grad_ref, key_acc, value_acc, query_acc,
):
    cosine, sine = cos_ref[...], sin_ref[...]
    half = HD // 2
    tokens = own_ref.shape[0]
    upper = (own_ref[...].astype(F32) + peer_ref[...].astype(F32)).astype(BF16)
    pieces = []
    for head in range(heads):
        head_grad = upper[:, head * HD : (head + 1) * HD]
        delta = jnp.sum(head_grad.astype(F32) * attended_ref[head], 1, keepdims=True)
        key_acc[...] = jnp.zeros_like(key_acc)
        value_acc[...] = jnp.zeros_like(value_acc)
        for low in range(0, tokens, block):
            rows = pl.ds(low, block)
            keys = low + block
            query = qkv_ref[3 * head, rows]
            key = qkv_ref[3 * head + 1, :keys]
            scores = matmul(query, key, 1, 1) * scale
            seen = visible_to(start_ref[rows], low, block, keys, prompt_len)
            weights = jnp.where(seen, jnp.exp(scores - log_ref[head, rows]), 0.0)
            grad_rows = head_grad[low : low + block]
            prob_dot = matmul(grad_rows, qkv_ref[3 * head + 2, :keys], 1, 1)
            score_grad = (weights * (prob_dot - delta[low : low + block]) * scale).astype(BF16)
            query_acc[rows] = matmul(score_grad, key, 1, 0)
            key_acc[:keys] += matmul(score_grad, query, 0, 0)
            value_acc[:keys] += matmul(weights.astype(BF16), grad_rows, 0, 0)
        for piece in (query_acc[...], key_acc[...]):
            one, two = piece[:, :half], piece[:, half:]
            pieces += [one * cosine + two * sine, two * cosine - one * sine]
        pieces.append(value_acc[...])
    qkv_grad = jnp.concatenate(pieces, 1).astype(BF16)
    one_ref[...] = matmul(qkv_grad, weight_ref[...], 1, 1)
    grad_ref[...] = matmul(normed_ref[...], qkv_grad, 0, 0).astype(BF16)


def attend_back(own, peer, qkv, attended, log_total, cosine, sine, start, normed, weight, block):
    heads, tokens, unused = attended.shape
    pairs = sum(block * (low + block) for low in range(0, tokens, block)) * heads
    return pl.pallas_call(
        functools.partial(attend_back_kernel, heads, block, tokens // 2, HD ** (-0.5)),
        out_shape=(
            jax.ShapeDtypeStruct(normed.shape, F32),
            jax.ShapeDtypeStruct(weight.shape, BF16),
        ),
        scratch_shapes=[pltpu.VMEM((tokens, HD), F32)] * 3,
        cost_estimate=pl.CostEstimate(
            flops=10 * pairs * HD, transcendentals=pairs, bytes_accessed=16 * tokens * 3 * heads * HD
        ),
        name="attend_back",
    )(own, peer, qkv, attended, log_total, cosine, sine, start, normed, weight)


def picks(rank_ref, capacity):
    rank = rank_ref[0]
    return lax.broadcasted_iota(jnp.int32, (capacity, rank.shape[1]), 0) == rank


def ones_where(mask):
    return jnp.where(mask, 1.0, 0.0).astype(BF16)


def back_hidden_kernel(rank_ref, cot_ref, down_ref, grad_ref, rows_ref):
    chosen = ones_where(picks(rank_ref, rows_ref.shape[1]))
    rows = jnp.dot(chosen, cot_ref[...], preferred_element_type=F32).astype(BF16)
    rows_ref[0] = rows
    grad_ref[0] = matmul(rows, down_ref[0], 1, 1).astype(BF16)


def back_hidden(rank, cot_rows, down, first, count, capacity):
    tokens, features = cot_rows.shape
    hidden = down.shape[1]
    return pl.pallas_call(
        back_hidden_kernel,
        grid=(count,),
        in_specs=[
            pl.BlockSpec((1, 1, tokens), lambda i: (first + i, 0, 0)),
            whole_block((tokens, features)),
            pl.BlockSpec((1, hidden, features), lambda i: (first + i, 0, 0)),
        ],
        out_specs=(
            pl.BlockSpec((1, capacity, hidden), lambda i: (i, 0, 0)),
            pl.BlockSpec((1, capacity, features), lambda i: (i, 0, 0)),
        ),
        out_shape=(
            jax.ShapeDtypeStruct((count, capacity, hidden), BF16),
            jax.ShapeDtypeStruct((count, capacity, features), BF16),
        ),
        cost_estimate=pl.CostEstimate(
            flops=2 * count * capacity * features * (tokens + hidden),
            transcendentals=0,
            bytes_accessed=2 * count * (hidden * features + capacity * (hidden + features)),
        ),
        name="back_hidden",
    )(rank, cot_rows, down)


def open_experts_kernel(rank_ref, token_ref, gate_ref, up_ref, pre_ref, rows_ref):
    hidden = gate_ref.shape[2]
    chosen = ones_where(picks(rank_ref, rows_ref.shape[1]))
    rows = jnp.dot(chosen, token_ref[...], preferred_element_type=F32).astype(BF16)
    rows_ref[0] = rows
    pre_ref[0, :, :hidden] = jnp.dot(rows, gate_ref[0], preferred_element_type=F32).astype(BF16)
    pre_ref[0, :, hidden:] = jnp.dot(rows, up_ref[0], preferred_element_type=F32).astype(BF16)


def open_experts(rank, token_rows, gate, up, first, count, capacity):
    tokens, features = token_rows.shape
    hidden = gate.shape[2]
    return pl.pallas_call(
        open_experts_kernel,
        grid=(count,),
        in_specs=[
            pl.BlockSpec((1, 1, tokens), lambda i: (first + i, 0, 0)),
            whole_block((tokens, features)),
            pl.BlockSpec((1, features, hidden), lambda i: (first + i, 0, 0)),
            pl.BlockSpec((1, features, hidden), lambda i: (first + i, 0, 0)),
        ],
        out_specs=(
            pl.BlockSpec((1, capacity, 2 * hidden), lambda i: (i, 0, 0)),
            pl.BlockSpec((1, capacity, features), lambda i: (i, 0, 0)),
        ),
        out_shape=(
            jax.ShapeDtypeStruct((count, capacity, 2 * hidden), BF16),
            jax.ShapeDtypeStruct((count, capacity, features), BF16),
        ),
        cost_estimate=pl.CostEstimate(
            flops=2 * count * capacity * features * (tokens + 2 * hidden),
            transcendentals=0,
            bytes_accessed=2 * count * (2 * hidden * features + capacity * (2 * hidden + features)),
        ),
        name="open_experts",
    )(rank, token_rows, gate, up)


def gated(pre_gate, pre_up, hidden_grad):
    sigma = 1.0 / (1.0 + jnp.exp(-pre_gate))
    silu = pre_gate * sigma
    grad_gate = hidden_grad * pre_up * sigma * (1.0 + pre_gate * (1.0 - sigma))
    return silu * pre_up, grad_gate, hidden_grad * silu


def experts_kernel(
    rank_ref, prob_ref, pre_own_ref, pre_peer_ref, back_own_ref, back_peer_ref, rows_ref, cot_ref,
    gate_ref, up_ref, down_ref, out_in_ref, dx_in_ref,
    both_grad_ref, down_grad_ref, share_ref, out_ref, dx_ref,
):
    capacity, hidden = back_own_ref.shape[1:]

    @pl.when(pl.program_id(0) == 0)
    def start():
        out_ref[...] = out_in_ref[...]
        dx_ref[...] = dx_in_ref[...]

    mask = picks(rank_ref, capacity)
    chosen = ones_where(mask)
    gate_val = jnp.sum(jnp.where(mask, prob_ref[0], 0.0), 1, keepdims=True)
    pre = pre_own_ref[0].astype(F32) + pre_peer_ref[0].astype(F32)
    raw_back = back_own_ref[0].astype(F32) + back_peer_ref[0].astype(F32)
    result, grad_gate, grad_up = gated(pre[:, :hidden], pre[:, hidden:], gate_val * raw_back)
    result = result.astype(BF16).astype(F32)
    share = jnp.sum(result * raw_back, 1, keepdims=True)
    share_ref[0] = jnp.sum(jnp.where(mask, share, 0.0), 0, keepdims=True)
    scaled = (gate_val * result).astype(BF16)
    grad_gate = grad_gate.astype(BF16)
    grad_up = grad_up.astype(BF16)
    rows = rows_ref[0]
    out_rows = jnp.dot(scaled, down_ref[0], preferred_element_type=F32).astype(BF16)
    out_ref[...] += matmul(chosen, out_rows, 0, 0)
    dx_rows = (matmul(grad_gate, gate_ref[0], 1, 1) + matmul(grad_up, up_ref[0], 1, 1)).astype(BF16)
    dx_ref[...] += matmul(chosen, dx_rows, 0, 0)
    both_grad_ref[0, :, :hidden] = matmul(rows, grad_gate, 0, 0).astype(BF16)
    both_grad_ref[0, :, hidden:] = matmul(rows, grad_up, 0, 0).astype(BF16)
    down_grad_ref[0] = matmul(scaled, cot_ref[0], 0, 0).astype(BF16)


def run_experts(
    rank, probs, pre_own, pre_peer, back_own, back_peer, rows, cot_rows, gate, up, down, out_sum, dx_sum, first
):
    count, capacity, hidden = back_own.shape
    tokens, features = out_sum.shape

    def at(shape, base):
        return pl.BlockSpec((1,) + shape, lambda i: (base + i, 0, 0))

    return pl.pallas_call(
        experts_kernel,
        grid=(count,),
        in_specs=[
            at((1, tokens), first),
            at((1, tokens), first),
            at((capacity, 2 * hidden), 0),
            at((capacity, 2 * hidden), 0),
            at((capacity, hidden), 0),
            at((capacity, hidden), 0),
            at((capacity, features), 0),
            at((capacity, features), 0),
            at((features, hidden), first),
            at((features, hidden), first),
            at((hidden, features), first),
            whole_block((tokens, features)),
            whole_block((tokens, features)),
        ],
        out_specs=(
            at((features, 2 * hidden), 0),
            at((hidden, features), 0),
            at((1, tokens), 0),
            whole_block((tokens, features)),
            whole_block((tokens, features)),
        ),
        out_shape=(
            jax.ShapeDtypeStruct((count, features, 2 * hidden), BF16),
            jax.ShapeDtypeStruct((count, hidden, features), BF16),
            jax.ShapeDtypeStruct((count, 1, tokens), F32),
            jax.ShapeDtypeStruct((tokens, features), F32),
            jax.ShapeDtypeStruct((tokens, features), F32),
        ),
        cost_estimate=pl.CostEstimate(
            flops=2 * count * capacity * features * (2 * tokens + 6 * hidden),
            transcendentals=count * capacity * hidden,
            bytes_accessed=2 * count * (6 * hidden * features + 6 * capacity * hidden),
        ),
        name="run_experts",
    )(
        rank, probs, pre_own, pre_peer, back_own, back_peer, rows, cot_rows, gate, up, down, out_sum, dx_sum
    )


def spread_kernel(core_ref, both_half_ref, both_rest_ref, down_half_ref, down_rest_ref, *refs):
    gate_ref, up_ref, down_ref = refs[-3:]
    hidden = gate_ref.shape[2]
    own = pl.program_id(0) < pl.num_programs(0) // 2

    @pl.when(own)
    def first():
        both = both_half_ref[0].astype(F32)
        gate_ref[0] = both[:, :hidden]
        up_ref[0] = both[:, hidden:]
        down_ref[0] = down_half_ref[0].astype(F32)

    @pl.when(jnp.logical_not(own))
    def second():
        both = both_rest_ref[0].astype(F32)
        gate_ref[0] = both[:, :hidden]
        up_ref[0] = both[:, hidden:]
        down_ref[0] = down_rest_ref[0].astype(F32)


def spread(core, both_half, both_rest, down_half, down_rest, earlier, first, experts):
    half = both_half.shape[0]
    features, hidden = both_half.shape[1], both_half.shape[2] // 2

    def own_index(i, core):
        return (jnp.minimum(i, half - 1), 0, 0)

    def rest_index(i, core):
        return (jnp.maximum(i - half, 0), 0, 0)

    def out_index(i, core):
        place = jnp.where(i < half, core[0] * half + i, (1 - core[0]) * half + i - half)
        return (first + place, 0, 0)

    shapes = ((features, hidden), (features, hidden), (hidden, features))
    return pl.pallas_call(
        spread_kernel,
        grid_spec=pltpu.PrefetchScalarGridSpec(
            num_scalar_prefetch=1,
            grid=(2 * half,),
            in_specs=[
                pl.BlockSpec((1, features, 2 * hidden), own_index),
                pl.BlockSpec((1, features, 2 * hidden), rest_index),
                pl.BlockSpec((1, hidden, features), own_index),
                pl.BlockSpec((1, hidden, features), rest_index),
            ]
            + [pl.BlockSpec(memory_space=pl.ANY)] * len(earlier),
            out_specs=tuple(pl.BlockSpec((1,) + shape, out_index) for shape in shapes),
        ),
        out_shape=tuple(jax.ShapeDtypeStruct((experts,) + shape, F32) for shape in shapes),
        input_output_aliases={5 + i: i for i in range(len(earlier))},
        cost_estimate=pl.CostEstimate(
            flops=0, transcendentals=0, bytes_accessed=36 * half * features * hidden
        ),
        name="spread",
    )(core, both_half, both_rest, down_half, down_rest, *earlier)


def paired_body(
    inputs,
    cotangent,
    routes,
    cont_lengths,
    first_gain,
    attend_in,
    attend_out,
    second_gain,
    router_weight,
    shared_gate,
    shared_up,
    shared_down,
    expert_gate,
    expert_up,
    expert_down,
):
    col_size = lax.axis_size("col")
    data_size = lax.axis_size("dp")
    col_index = lax.axis_index("col")
    tok_rest, feat_dev = inputs.shape
    feat_full = feat_dev * 2
    tok_block = tok_rest * col_size
    experts = expert_gate.shape[0]
    shared_dev = shared_gate.shape[1]
    capacity = tok_block * 3 // experts
    tokens_all = float(data_size * tok_block)
    prompt_len = tok_block // 2
    block = 256
    chunk = 4
    core = (lax.axis_index("dp") % 2).reshape(1)

    own_parts = col_parts(inputs)
    peer_parts = [swap(part, "row") for part in own_parts]
    own_all = in_order(own_parts, "col").reshape(tok_block, feat_dev).astype(F32)
    peer_all = in_order(peer_parts, "col").reshape(tok_block, feat_dev).astype(F32)
    peer_weight = swap(attend_in, "row")
    peer_gain = swap(first_gain, "row")
    cot_all = col_rows(cotangent)

    squares_one = jnp.sum(own_all * own_all, 1) + jnp.sum(peer_all * peer_all, 1)
    scale_all = lax.rsqrt(squares_one / feat_full + EPSILON)[:, None]
    unit_all = own_all * scale_all
    normed_own = (unit_all * first_gain).astype(BF16)
    normed_peer = (peer_all * scale_all * peer_gain).astype(BF16)

    offsets = jnp.arange(tok_block, dtype=jnp.int32)
    after = offsets - prompt_len
    ends = jnp.cumsum(cont_lengths[0])
    begin = jnp.max(jnp.where(ends[None, :] <= after[:, None], ends[None, :], 0), 1)
    start = jnp.where(after < 0, 0, prompt_len + begin)
    position = jnp.where(after < 0, offsets, prompt_len + after - begin)
    angles = angle_table(position)
    cosine, sine = jnp.cos(angles), jnp.sin(angles)
    start = start[:, None]

    expert_ids = jnp.arange(experts, dtype=jnp.int32)
    named = (routes[:, 0][None, :] == expert_ids[:, None]) | (
        routes[:, 1][None, :] == expert_ids[:, None]
    )
    before = (offsets[:, None] < offsets[None, :]).astype(BF16)
    rank = jnp.dot(named.astype(BF16), before, preferred_element_type=F32).astype(jnp.int32)
    rank = jnp.where(named, rank, -1)[:, None, :]
    count_own = jnp.sum(named.astype(F32), 1)

    back_own, cot_rows, back_peer = [], [], []
    for first in range(0, experts, chunk):
        back, rows = back_hidden(rank, cot_all, expert_down, first, chunk, capacity)
        back_own.append(back)
        cot_rows.append(rows)
        back_peer.append(swap(back, "row"))
    shared_back_own = matmul(cot_all, shared_down, 1, 1).astype(BF16)
    shared_back_peer = swap(shared_back_own, "row")

    qkv, attended, log_total, out_partial = attend(
        normed_own, normed_peer, attend_in, peer_weight, attend_out, cosine, sine, start, block
    )
    inputs_f = inputs.astype(F32)
    mixed_one = inputs_f + col_sum_rows(out_partial)
    gained = mixed_one * second_gain
    partial_stats = jnp.concatenate(
        [
            jnp.sum(mixed_one * mixed_one, 1, keepdims=True),
            jnp.dot(gained, router_weight, precision=HIGHEST),
        ],
        1,
    )
    stats = partial_stats + swap(partial_stats, "row")
    scale_two = lax.rsqrt(stats[:, :1] / feat_full + EPSILON)
    router_probs = jax.nn.softmax(stats[:, 1:] * scale_two, -1)
    unit_two = mixed_one * scale_two
    normed_two = (unit_two * second_gain).astype(BF16)
    normed_all = col_rows(normed_two)
    probs_all = col_rows(router_probs)
    probs_rows = probs_all.T[:, None, :]
    count_total, prob_total = sum_by_swaps(jnp.stack([count_own, jnp.sum(probs_all, 0)]), ("dp",))
    balance_loss = experts * jnp.sum(count_total / (2.0 * tokens_all) * prob_total / tokens_all)

    shared_pre_own = jnp.concatenate(
        [matmul(normed_all, shared_gate, 1, 0), matmul(normed_all, shared_up, 1, 0)], 1
    ).astype(BF16)
    shared_pre_peer = swap(shared_pre_own, "row")
    pre_own, token_rows, pre_peer = [], [], []
    for first in range(0, experts, chunk):
        pre, rows = open_experts(rank, normed_all, expert_gate, expert_up, first, chunk, capacity)
        pre_own.append(pre)
        token_rows.append(rows)
        pre_peer.append(swap(pre, "row"))

    shared_pre = shared_pre_own.astype(F32) + shared_pre_peer.astype(F32)
    shared_back = shared_back_own.astype(F32) + shared_back_peer.astype(F32)
    shared_hidden, shared_gate_pgrad, shared_up_pgrad = (
        value.astype(BF16)
        for value in gated(shared_pre[:, :shared_dev], shared_pre[:, shared_dev:], shared_back)
    )
    out_sum = matmul(shared_hidden, shared_down, 1, 0)
    dx_sum = matmul(shared_gate_pgrad, shared_gate, 1, 1) + matmul(shared_up_pgrad, shared_up, 1, 1)
    shared_gate_grad = dp_total(matmul(normed_all, shared_gate_pgrad, 0, 0).astype(BF16))
    shared_up_grad = dp_total(matmul(normed_all, shared_up_pgrad, 0, 0).astype(BF16))
    shared_down_grad = dp_total(matmul(shared_hidden, cot_all, 0, 0).astype(BF16))

    shares, expert_grads = [], ()
    for index, first in enumerate(range(0, experts, chunk)):
        both_grad, down_grad, share, out_sum, dx_sum = run_experts(
            rank, probs_rows, pre_own[index], pre_peer[index], back_own[index], back_peer[index],
            token_rows[index], cot_rows[index], expert_gate, expert_up, expert_down, out_sum, dx_sum, first,
        )
        shares.append(share[:, 0])
        both_half, both_rest = pair_halves(both_grad)
        down_half, down_rest = pair_halves(down_grad)
        expert_grads = spread(
            core, both_half, both_rest, down_half, down_rest, expert_grads, first, experts
        )

    layer_out = (mixed_one + col_sum_rows(out_sum.astype(BF16))).astype(BF16)
    cot_f = cotangent.astype(F32)
    gate_grad = col_sum_rows(jnp.concatenate(shares, 0).T)
    prob_grad = gate_grad + experts * count_total / (2.0 * tokens_all * tokens_all)
    logit_grad = router_probs * (prob_grad - jnp.sum(router_probs * prob_grad, -1, keepdims=True))
    router_grad = jnp.einsum("td,te->ed", unit_two * second_gain, logit_grad, precision=HIGHEST)

    normed_grad = col_sum_rows(dx_sum.astype(BF16))
    two_grad = normed_grad + jnp.einsum("te,de->td", logit_grad, router_weight, precision=HIGHEST)
    gained_two = two_grad * second_gain
    second_gain_grad = jnp.sum(two_grad * unit_two, 0)
    inner_two = jnp.sum(gained_two * unit_two, 1, keepdims=True)
    inner_two = (inner_two + swap(inner_two, "row")) / feat_full
    mixed_grad = cot_f + scale_two * (gained_two - unit_two * inner_two)
    mix_all = col_rows(mixed_grad.astype(BF16))
    attn_own = matmul(mix_all, attend_out, 1, 1).astype(BF16)
    attn_peer = swap(attn_own, "row")
    heads = attended.shape[0]
    attn_rows = attended.astype(BF16)
    attend_out_grad = jnp.concatenate(
        [matmul(attn_rows[head], mix_all, 0, 0) for head in range(heads)], 0
    ).astype(BF16)
    attend_out_grad = dp_total(attend_out_grad)
    one_partial, attend_in_grad = attend_back(
        attn_own, attn_peer, qkv, attended, log_total, cosine, sine, start, normed_own, attend_in, block
    )
    attend_in_grad = dp_total(attend_in_grad)
    first_gain_grad = jnp.sum(one_partial * unit_all, 0)
    one_grad = col_sum_rows(one_partial.astype(BF16))
    own_rows = col_index * tok_rest
    unit_one = rows_of(unit_all, own_rows, tok_rest)
    scale_one = rows_of(scale_all, own_rows, tok_rest)
    gained_one = one_grad * first_gain
    inner_one = jnp.sum(gained_one * unit_one, 1, keepdims=True)
    inner_one = (inner_one + swap(inner_one, "row")) / feat_full
    input_grad = (mixed_grad + scale_one * (gained_one - unit_one * inner_one)).astype(BF16)
    early = sum_by_swaps(jnp.concatenate([second_gain_grad[None], router_grad], 0), ("dp", "col"))
    first_gain_grad = sum_by_swaps(first_gain_grad, ("dp", "col"))
    return (
        layer_out,
        input_grad,
        first_gain_grad,
        attend_in_grad,
        attend_out_grad,
        early[0],
        early[1:].T,
        shared_gate_grad,
        shared_up_grad,
        shared_down_grad,
        expert_grads[0],
        expert_grads[1],
        expert_grads[2],
        balance_loss,
    )


def power_of_two(number):
    return number & (number - 1) == 0


def chosen_body(*shards):
    inputs, cont_lengths = shards[0], shards[3]
    tok_block = inputs.shape[0] * lax.axis_size("col")
    paired = (
        lax.axis_size("row") == 2
        and lax.axis_size("dp") >= 2
        and power_of_two(lax.axis_size("dp"))
        and power_of_two(lax.axis_size("col"))
        and cont_lengths.shape[0] == 1
        and tok_block % 512 == 0
        and tok_block <= 2048
    )
    return (paired_body if paired else body)(*shards)


def solution(mesh):
    in_specs = (
        P(("dp", "col"), "row"),
        P(("dp", "col"), "row"),
        P("dp", None),
        P("dp", None),
        P("row"),
        P("row", "col"),
        P("col", "row"),
        P("row"),
        P("row", None),
        P("row", "col"),
        P("row", "col"),
        P("col", "row"),
        P(None, "row", "col"),
        P(None, "row", "col"),
        P(None, "col", "row"),
    )
    out_specs = (
        P(("dp", "col"), "row"),
        P(("dp", "col"), "row"),
        P("row"),
        P("row", "col"),
        P("col", "row"),
        P("row"),
        P("row", None),
        P("row", "col"),
        P("row", "col"),
        P("col", "row"),
        P(None, "row", "col"),
        P(None, "row", "col"),
        P(None, "col", "row"),
        P(),
    )
    return jax.shard_map(chosen_body, mesh=mesh, in_specs=in_specs, out_specs=out_specs, check_vma=False)
```

```python
import functools

import jax
import jax.numpy as jnp
from jax import lax
from jax.experimental import pallas as pl
from jax.experimental.pallas import tpu as pltpu
from jax.sharding import PartitionSpec as P

HD = 64


EPSILON = 1e-05
HIGHEST = lax.Precision.HIGHEST


def for_sending(value):
    return jax.tree.map(lambda a: a.astype(jnp.bfloat16) if a.dtype == jnp.float32 else a, value)


def feature_sums(values):
    return lax.psum(values, "row")


def token_gather(values):
    return lax.all_gather(values, "col", axis=0, tiled=True)


def slot_gather(values):
    return jax.tree.map(
        lambda part, own: part.astype(own.dtype),
        lax.all_gather(for_sending(values), "row", axis=0, tiled=True),
        values,
    )


def row_partials(term_fn, row_count):
    return lax.psum_scatter(
        term_fn(jnp.int32(0), lax.axis_size("row") * row_count),
        "row",
        scatter_dimension=0,
        tiled=True,
    )


def col_partials(term_fn, row_count):
    return lax.psum_scatter(
        term_fn(jnp.int32(0), lax.axis_size("col") * row_count).astype(jnp.bfloat16),
        "col",
        scatter_dimension=0,
        tiled=True,
    ).astype(jnp.float32)


def token_stats(values):
    return lax.psum(values, ("dp", "col"))


def rows_of(source, row_start, row_count):
    return lax.dynamic_slice_in_dim(source, row_start, row_count, 0)


def angle_table(position):
    half_dim = HD // 2
    frequency = 10000.0 ** (-jnp.arange(half_dim, dtype=jnp.float32) * 2.0 / HD)
    return position.astype(jnp.float32)[:, None] * frequency[None, :]


def rotate(values, angles):
    half_dim = values.shape[-1] // 2
    cosine = jnp.cos(angles)[:, None, :]
    sine_part = jnp.sin(angles)[:, None, :]
    first_half = values[..., :half_dim]
    second_half = values[..., half_dim:]
    return jnp.concatenate(
        [
            first_half * cosine - second_half * sine_part,
            first_half * sine_part + second_half * cosine,
        ],
        -1,
    )


def token_layout(cont_lengths, offsets, group_len):
    prompt_len = group_len // 2
    group_ids = offsets // group_len
    inner_pos = offsets % group_len
    seg_ends = jnp.cumsum(cont_lengths, axis=1)
    seg_starts = seg_ends - cont_lengths
    group_pick = (
        group_ids[:, None] == jnp.arange(cont_lengths.shape[0], dtype=jnp.int32)[None, :]
    ).astype(jnp.int32)
    ends_own = jnp.sum(group_pick[:, :, None] * seg_ends[None, :, :], 1)
    starts_own = jnp.sum(group_pick[:, :, None] * seg_starts[None, :, :], 1)
    after_prompt = inner_pos - prompt_len
    segment = 1 + jnp.sum((after_prompt[:, None] >= ends_own).astype(jnp.int32), 1)
    segment = jnp.where(after_prompt < 0, 0, segment)
    slot_pick = segment[:, None] - 1 == jnp.arange(cont_lengths.shape[1], dtype=jnp.int32)[None, :]
    seg_begin = jnp.sum(jnp.where(slot_pick, starts_own, 0), 1)
    position = jnp.where(segment == 0, inner_pos, prompt_len + after_prompt - seg_begin)
    return (group_ids, segment, position)


def gate_up_grad(pre_gate, pre_up, hidden_grad):
    gate_sig = jax.nn.sigmoid(pre_gate)
    grad_gate = hidden_grad * pre_up * gate_sig * (1.0 + pre_gate * (1.0 - gate_sig))
    grad_up = hidden_grad * pre_gate * gate_sig
    return jnp.concatenate([grad_gate, grad_up], 1).astype(jnp.bfloat16)


def body(
    inputs,
    cotangent,
    routes,
    cont_lengths,
    first_gain,
    attend_in,
    attend_out,
    second_gain,
    router_weight,
    shared_gate,
    shared_up,
    shared_down,
    expert_gate,
    expert_up,
    expert_down,
):
    row_size = lax.axis_size("row")
    col_size = lax.axis_size("col")
    data_size = lax.axis_size("dp")
    row_index = lax.axis_index("row")
    col_index = lax.axis_index("col")
    tok_rest, feat_dev = inputs.shape
    feat_full = feat_dev * row_size
    tok_block = tok_rest * col_size
    tok_query = tok_block // row_size
    experts = expert_gate.shape[0]
    hidden_dev = expert_gate.shape[2]
    shared_dev = shared_gate.shape[1]
    head_cols = attend_in.shape[1]
    heads_dev = head_cols // (3 * HD)
    capacity = tok_block * 3 // experts
    slots_dev = experts * capacity // row_size
    group_len = tok_block // cont_lengths.shape[0]
    key_block = min(1024, tok_query)
    block_count = group_len // key_block
    score_scale = HD ** (-0.5)
    tokens_all = float(data_size * tok_block)
    group_base = row_index * tok_query // group_len * group_len
    inputs_f = inputs.astype(jnp.float32)
    squares_one = feature_sums(jnp.sum(inputs_f * inputs_f, 1))
    scale_one = lax.rsqrt(squares_one / feat_full + EPSILON)[:, None]
    normed_one = (inputs_f * scale_one * first_gain).astype(jnp.bfloat16)
    normed_all = token_gather(normed_one)

    def qkv_term(row_start, row_count):
        return jnp.dot(
            rows_of(normed_all, row_start, row_count), attend_in, preferred_element_type=jnp.float32
        )

    qkv_raw = row_partials(qkv_term, tok_query).reshape(tok_query, heads_dev, 3, HD)
    query_offsets = row_index * tok_query + jnp.arange(tok_query, dtype=jnp.int32)
    query_group, query_segment, query_position = token_layout(
        cont_lengths, query_offsets, group_len
    )
    key_group, key_segment, key_position = token_layout(
        cont_lengths, jnp.arange(tok_block, dtype=jnp.int32), group_len
    )
    query_angles = angle_table(query_position)
    queries = rotate(qkv_raw[:, :, 0], query_angles).astype(jnp.bfloat16)
    keys_own = rotate(qkv_raw[:, :, 1], query_angles).astype(jnp.bfloat16)
    values_own = qkv_raw[:, :, 2].astype(jnp.bfloat16)
    keys_all, values_all = slot_gather(
        (keys_own.reshape(tok_query, heads_dev * HD), values_own.reshape(tok_query, heads_dev * HD))
    )

    def block_scores(block_start):
        key_rows = rows_of(keys_all, block_start, key_block).reshape(key_block, heads_dev, HD)
        block_group = rows_of(key_group, block_start, key_block)
        block_segment = rows_of(key_segment, block_start, key_block)
        block_position = rows_of(key_position, block_start, key_block)
        visible = (
            (query_group[:, None] == block_group[None, :])
            & ((block_segment[None, :] == 0) | (block_segment[None, :] == query_segment[:, None]))
            & (block_position[None, :] <= query_position[:, None])
        )
        scores = (
            jnp.einsum("qhd,khd->hqk", queries, key_rows, preferred_element_type=jnp.float32)
            * score_scale
        )
        return (scores, visible[None], key_rows)

    def forward_step(carry, block_index):
        run_max, run_total, run_accum = carry
        block_start = group_base + block_index * key_block
        scores, mask_now, key_rows = block_scores(block_start)
        value_rows = (
            rows_of(values_all, block_start, key_block)
            .reshape(key_block, heads_dev, HD)
            .astype(jnp.float32)
        )
        new_max = jnp.maximum(run_max, jnp.max(jnp.where(mask_now, scores, -1e30), -1))
        weights = jnp.where(mask_now, jnp.exp(scores - new_max[..., None]), 0.0)
        run_decay = jnp.exp(run_max - new_max)
        run_total = run_total * run_decay + jnp.sum(weights, -1)
        run_accum = run_accum * run_decay[..., None] + jnp.einsum(
            "hqk,khd->hqd", weights, value_rows, precision=HIGHEST
        )
        return ((new_max, run_total, run_accum), None)

    start_carry = (
        jnp.full((heads_dev, tok_query), -1e30, jnp.float32),
        jnp.zeros((heads_dev, tok_query), jnp.float32),
        jnp.zeros((heads_dev, tok_query, HD), jnp.float32),
    )
    (run_max, run_total, run_accum), unused_out = lax.scan(
        forward_step, start_carry, jnp.arange(block_count, dtype=jnp.int32)
    )
    log_total = run_max + jnp.log(run_total)
    attended = run_accum / run_total[..., None]
    attn_rows = attended.transpose(1, 0, 2).reshape(tok_query, heads_dev * HD).astype(jnp.bfloat16)
    outputs_all = slot_gather(attn_rows)

    def attention_term(row_start, row_count):
        return jnp.dot(
            rows_of(outputs_all, row_start, row_count),
            attend_out,
            preferred_element_type=jnp.float32,
        )

    mixed_one = inputs_f + col_partials(attention_term, tok_rest)
    gained = mixed_one * second_gain
    squares_two, logit_part = feature_sums(
        (jnp.sum(mixed_one * mixed_one, 1), jnp.dot(gained, router_weight, precision=HIGHEST))
    )
    scale_two = lax.rsqrt(squares_two / feat_full + EPSILON)[:, None]
    router_probs = jax.nn.softmax(logit_part * scale_two, -1)
    routes_rest = lax.dynamic_slice_in_dim(routes, col_index * tok_rest, tok_rest, 0)
    route_hot = routes_rest[:, :, None] == jnp.arange(experts, dtype=jnp.int32)[None, None, :]
    gate_vals = jnp.sum(jnp.where(route_hot, router_probs[:, None, :], 0.0), -1)
    count_total, prob_total = token_stats(
        (jnp.sum(route_hot.astype(jnp.float32), (0, 1)), jnp.sum(router_probs, 0))
    )
    balance_loss = experts * jnp.sum(count_total / (2.0 * tokens_all) * prob_total / tokens_all)
    unit_two = mixed_one * scale_two
    normed_two = (unit_two * second_gain).astype(jnp.bfloat16)
    normed_two_all = token_gather(normed_two)
    flat_routes = routes.reshape(-1)
    flat_hot = (flat_routes[:, None] == jnp.arange(experts, dtype=jnp.int32)[None, :]).astype(
        jnp.int32
    )
    earlier = jnp.cumsum(flat_hot, 0) - flat_hot
    slot_of = flat_routes * capacity + jnp.sum(earlier * flat_hot, 1)
    slot_pairs = slot_of.reshape(tok_block, 2)
    slot_source = (
        jnp.full((experts * capacity,), 2 * tok_block, jnp.int32)
        .at[slot_of]
        .set(jnp.arange(2 * tok_block, dtype=jnp.int32))
    )
    padded_two = jnp.concatenate([normed_two_all, jnp.zeros((1, feat_dev), jnp.bfloat16)], 0)
    expert_rows = padded_two[slot_source // 2]
    shared_both = jnp.concatenate([shared_gate, shared_up], 1)

    def shared_term(row_start, row_count):
        return jnp.dot(
            rows_of(normed_two_all, row_start, row_count),
            shared_both,
            preferred_element_type=jnp.float32,
        )

    shared_pre = row_partials(shared_term, tok_query)
    shared_g = shared_pre[:, :shared_dev]
    shared_u = shared_pre[:, shared_dev:]
    shared_hidden = (jax.nn.silu(shared_g) * shared_u).astype(jnp.bfloat16)
    expert_both = jnp.concatenate([expert_gate, expert_up], 2)

    def expert_term(row_start, row_count):
        group_count = row_count // capacity
        picked = rows_of(expert_rows, row_start, row_count).reshape(group_count, capacity, feat_dev)
        return jnp.einsum(
            "ecd,edf->ecf", picked, expert_both, preferred_element_type=jnp.float32
        ).reshape(row_count, 2 * hidden_dev)

    expert_pre = row_partials(expert_term, slots_dev)
    expert_g = expert_pre[:, :hidden_dev]
    expert_u = expert_pre[:, hidden_dev:]
    expert_hidden = (jax.nn.silu(expert_g) * expert_u).astype(jnp.bfloat16)
    shared_all, expert_all = slot_gather((shared_hidden, expert_hidden))
    expert_out = jnp.einsum(
        "ecf,efd->ecd",
        expert_all.reshape(experts, capacity, hidden_dev),
        expert_down,
        preferred_element_type=jnp.float32,
    ).reshape(experts * capacity, feat_dev)

    def output_term(row_start, row_count):
        shared_part = jnp.dot(
            rows_of(shared_all, row_start, row_count),
            shared_down,
            preferred_element_type=jnp.float32,
        )
        pair_slots = rows_of(slot_pairs, row_start, row_count)
        return jnp.concatenate(
            [shared_part, expert_out[pair_slots[:, 0]], expert_out[pair_slots[:, 1]]], 1
        )

    branch_sums = col_partials(output_term, tok_rest)
    shared_result = branch_sums[:, :feat_dev]
    expert_pick = branch_sums[:, feat_dev:].reshape(tok_rest, 2, feat_dev)
    expert_result = jnp.sum(gate_vals[:, :, None] * expert_pick, 1)
    layer_out = (mixed_one + shared_result + expert_result).astype(jnp.bfloat16)
    cot_f = cotangent.astype(jnp.float32)
    gate_grad = feature_sums(jnp.sum(expert_pick * cot_f[:, None, :], -1))
    expert_cot = (
        (gate_vals[:, :, None] * cot_f[:, None, :])
        .astype(jnp.bfloat16)
        .reshape(tok_rest, 2 * feat_dev)
    )
    cot_all = token_gather(jnp.concatenate([cotangent, expert_cot], 1))
    shared_cot = cot_all[:, :feat_dev]
    pair_cot = jnp.concatenate(
        [
            cot_all[:, feat_dev:].reshape(2 * tok_block, feat_dev),
            jnp.zeros((1, feat_dev), jnp.bfloat16),
        ],
        0,
    )
    slot_cot = pair_cot[slot_source]
    shared_down_grad = jnp.einsum(
        "tf,td->fd", shared_all, shared_cot, preferred_element_type=jnp.float32
    )

    def shared_back(row_start, row_count):
        return jnp.einsum(
            "td,fd->tf",
            rows_of(shared_cot, row_start, row_count),
            shared_down,
            preferred_element_type=jnp.float32,
        )

    shared_pgrad = gate_up_grad(shared_g, shared_u, row_partials(shared_back, tok_query))
    expert_down_grad = jnp.einsum(
        "ecf,ecd->efd",
        expert_all.reshape(experts, capacity, hidden_dev),
        slot_cot.reshape(experts, capacity, feat_dev),
        preferred_element_type=jnp.float32,
    )

    def expert_back(row_start, row_count):
        group_count = row_count // capacity
        picked = rows_of(slot_cot, row_start, row_count).reshape(group_count, capacity, feat_dev)
        return jnp.einsum(
            "ecd,efd->ecf", picked, expert_down, preferred_element_type=jnp.float32
        ).reshape(row_count, hidden_dev)

    expert_pgrad = gate_up_grad(expert_g, expert_u, row_partials(expert_back, slots_dev))
    shared_pall, expert_pall = slot_gather((shared_pgrad, expert_pgrad))
    expert_pall_view = expert_pall.reshape(experts, capacity, 2 * hidden_dev)
    expert_both_grad = jnp.einsum(
        "ecd,ecf->edf",
        expert_rows.reshape(experts, capacity, feat_dev),
        expert_pall_view,
        preferred_element_type=jnp.float32,
    )
    expert_input_grad = jnp.einsum(
        "ecf,edf->ecd", expert_pall_view, expert_both, preferred_element_type=jnp.float32
    ).reshape(experts * capacity, feat_dev)
    shared_both_grad = jnp.einsum(
        "td,tf->df", normed_two_all, shared_pall, preferred_element_type=jnp.float32
    )

    def normed_back(row_start, row_count):
        pair_slots = rows_of(slot_pairs, row_start, row_count)
        shared_part = jnp.einsum(
            "tf,df->td",
            rows_of(shared_pall, row_start, row_count),
            shared_both,
            preferred_element_type=jnp.float32,
        )
        return (
            shared_part + expert_input_grad[pair_slots[:, 0]] + expert_input_grad[pair_slots[:, 1]]
        )

    normed_grad = col_partials(normed_back, tok_rest)
    prob_grad = jnp.sum(
        jnp.where(route_hot, gate_grad[:, :, None], 0.0), 1
    ) + experts * count_total / (2.0 * tokens_all * tokens_all)
    logit_grad = router_probs * (prob_grad - jnp.sum(router_probs * prob_grad, -1, keepdims=True))
    router_grad = jnp.einsum("td,te->de", unit_two * second_gain, logit_grad, precision=HIGHEST)
    two_grad = normed_grad + jnp.einsum("te,de->td", logit_grad, router_weight, precision=HIGHEST)
    gained_two = two_grad * second_gain
    second_gain_grad = jnp.sum(two_grad * unit_two, 0)
    inner_two = feature_sums(jnp.sum(gained_two * unit_two, 1))[:, None] / feat_full
    mixed_grad = cot_f + scale_two * (gained_two - unit_two * inner_two)
    mix_all = token_gather(mixed_grad.astype(jnp.bfloat16))
    attend_out_grad = jnp.einsum(
        "tc,td->cd", outputs_all, mix_all, preferred_element_type=jnp.float32
    )

    def output_back(row_start, row_count):
        return jnp.einsum(
            "td,cd->tc",
            rows_of(mix_all, row_start, row_count),
            attend_out,
            preferred_element_type=jnp.float32,
        )

    attn_grad = (
        row_partials(output_back, tok_query).astype(jnp.bfloat16).reshape(tok_query, heads_dev, HD)
    )
    attn_grad_f = attn_grad.astype(jnp.float32)
    row_delta = jnp.sum(attn_grad_f.transpose(1, 0, 2) * attended, -1)
    queries_f = queries.astype(jnp.float32)

    def backward_step(query_grad, block_index):
        block_start = group_base + block_index * key_block
        scores, mask_now, key_rows = block_scores(block_start)
        value_rows = rows_of(values_all, block_start, key_block).reshape(key_block, heads_dev, HD)
        weights = jnp.where(mask_now, jnp.exp(scores - log_total[..., None]), 0.0)
        prob_dot = jnp.einsum(
            "qhd,khd->hqk", attn_grad, value_rows, preferred_element_type=jnp.float32
        )
        score_grad = weights * (prob_dot - row_delta[..., None])
        query_grad = (
            query_grad
            + jnp.einsum(
                "hqk,khd->qhd", score_grad, key_rows.astype(jnp.float32), precision=HIGHEST
            )
            * score_scale
        )
        key_grad = (
            jnp.einsum("hqk,qhd->khd", score_grad, queries_f, precision=HIGHEST) * score_scale
        )
        value_grad = jnp.einsum("hqk,qhd->khd", weights, attn_grad_f, precision=HIGHEST)
        return (
            query_grad,
            jnp.concatenate(
                [
                    key_grad.reshape(key_block, heads_dev * HD),
                    value_grad.reshape(key_block, heads_dev * HD),
                ],
                1,
            ),
        )

    query_grad, kv_terms = lax.scan(
        backward_step,
        jnp.zeros((tok_query, heads_dev, HD), jnp.float32),
        jnp.arange(block_count, dtype=jnp.int32),
    )
    kv_group = kv_terms.reshape(group_len, 2 * heads_dev * HD)
    kv_full = lax.dynamic_update_slice_in_dim(
        jnp.zeros((tok_block, 2 * heads_dev * HD), jnp.float32), kv_group, group_base, 0
    )

    def kv_term(row_start, row_count):
        return rows_of(kv_full, row_start, row_count)

    kv_grad = row_partials(kv_term, tok_query)
    key_grad_raw = rotate(
        kv_grad[:, : heads_dev * HD].reshape(tok_query, heads_dev, HD), -query_angles
    )
    value_grad_raw = kv_grad[:, heads_dev * HD :].reshape(tok_query, heads_dev, HD)
    query_grad_raw = rotate(query_grad, -query_angles)
    qkv_grad = (
        jnp.stack([query_grad_raw, key_grad_raw, value_grad_raw], 2)
        .reshape(tok_query, head_cols)
        .astype(jnp.bfloat16)
    )
    qkv_all = slot_gather(qkv_grad)
    attend_in_grad = jnp.einsum(
        "td,tc->dc", normed_all, qkv_all, preferred_element_type=jnp.float32
    )

    def input_back(row_start, row_count):
        return jnp.einsum(
            "tc,dc->td",
            rows_of(qkv_all, row_start, row_count),
            attend_in,
            preferred_element_type=jnp.float32,
        )

    one_grad = col_partials(input_back, tok_rest)
    unit_one = inputs_f * scale_one
    gained_one = one_grad * first_gain
    first_gain_grad = jnp.sum(one_grad * unit_one, 0)
    inner_one = feature_sums(jnp.sum(gained_one * unit_one, 1))[:, None] / feat_full
    input_grad = (mixed_grad + scale_one * (gained_one - unit_one * inner_one)).astype(jnp.bfloat16)
    first_gain_grad, second_gain_grad, router_grad = token_stats(
        (first_gain_grad, second_gain_grad, router_grad)
    )
    summed = (
        lax.psum(attend_in_grad.astype(jnp.bfloat16), "dp").astype(jnp.float32),
        lax.psum(attend_out_grad.astype(jnp.bfloat16), "dp").astype(jnp.float32),
        lax.psum(shared_both_grad.astype(jnp.bfloat16), "dp").astype(jnp.float32),
        lax.psum(shared_down_grad.astype(jnp.bfloat16), "dp").astype(jnp.float32),
        lax.psum(expert_both_grad.astype(jnp.bfloat16), "dp").astype(jnp.float32),
        lax.psum(expert_down_grad.astype(jnp.bfloat16), "dp").astype(jnp.float32),
    )
    shared_both_sum = summed[2]
    expert_both_sum = summed[4]
    return (
        layer_out,
        input_grad,
        first_gain_grad,
        summed[0],
        summed[1],
        second_gain_grad,
        router_grad,
        shared_both_sum[:, :shared_dev],
        shared_both_sum[:, shared_dev:],
        summed[3],
        expert_both_sum[:, :, :hidden_dev],
        expert_both_sum[:, :, hidden_dev:],
        summed[5],
        balance_loss,
    )


F32 = jnp.float32
BF16 = jnp.bfloat16
MASKED = -1e30
LIGHT = pl.CostEstimate(flops=1, transcendentals=0, bytes_accessed=1)


def swap(value, axis, step=1):
    size = lax.axis_size(axis)
    return lax.ppermute(value, axis, [(i, i ^ step) for i in range(size)])


def shifted(value, axis, step):
    size = lax.axis_size(axis)
    return lax.ppermute(value, axis, [(i, (i + step) % size) for i in range(size)])


def in_order(parts, axis):
    size, me = len(parts), lax.axis_index(axis)
    whole = jnp.zeros((size,) + parts[0].shape, parts[0].dtype)
    for step, part in enumerate(parts):
        whole = lax.dynamic_update_index_in_dim(whole, part, (me - step) % size, 0)
    return whole


def col_parts(value):
    return [value] + [shifted(value, "col", s) for s in range(1, lax.axis_size("col"))]


def col_rows(value):
    whole = in_order(col_parts(value), "col")
    return whole.reshape((-1,) + value.shape[1:])


def col_sum_rows(whole):
    size, me = lax.axis_size("col"), lax.axis_index("col")
    blocks = whole.reshape((size, whole.shape[0] // size) + whole.shape[1:])
    total = lax.dynamic_index_in_dim(blocks, me, 0, False).astype(F32)
    for step in range(1, size):
        block = lax.dynamic_index_in_dim(blocks, (me + step) % size, 0, False)
        total = total + shifted(block, "col", step).astype(F32)
    return total


def sum_by_swaps(value, axes):
    for axis in axes:
        step = 1
        while step < lax.axis_size(axis):
            value = value + swap(value, axis, step)
            step *= 2
    return value


def held(value, *others):
    return lax.optimization_barrier((value,) + others)[0]


def high_low(value):
    high = value.astype(BF16)
    return high, (value - high.astype(F32)).astype(BF16)


def with_rows(value, extra):
    high, low = high_low(extra)
    rows = jnp.concatenate([high, low], -2)
    room = [(0, 0)] * (rows.ndim - 1) + [(0, value.shape[-1] - rows.shape[-1])]
    return jnp.concatenate([value, jnp.pad(rows, room)], -2)


def split_rows(value, count, extra, width):
    tail = value[..., count:, :width].astype(F32)
    return value[..., :count, :], tail[..., :extra, :] + tail[..., extra:, :]


def pair_half(whole):
    core = lax.axis_index("dp") % 2
    halves = whole.reshape((2, whole.shape[0] // 2) + whole.shape[1:])
    mine = lax.dynamic_index_in_dim(halves, core, 0, False)
    other = lax.dynamic_index_in_dim(halves, 1 - core, 0, False)
    return (mine.astype(F32) + swap(other, "dp", 1).astype(F32)).astype(BF16)


def cross_sum(half):
    step = 2
    while step < lax.axis_size("dp"):
        half = (half.astype(F32) + swap(half, "dp", step).astype(F32)).astype(BF16)
        step *= 2
    return half


def both_halves(half):
    core = lax.axis_index("dp") % 2
    rest = swap(half, "dp", 1)
    first = jnp.where(core == 0, half, rest)
    second = jnp.where(core == 0, rest, half)
    return jnp.concatenate([first, second], 0).astype(F32)


def matmul(left, right, left_dim, right_dim):
    return lax.dot_general(
        left, right, (((left_dim,), (right_dim,)), ((), ())), preferred_element_type=F32
    )


def whole_block(shape):
    return pl.BlockSpec(shape, lambda *unused: (0,) * len(shape))


def visible_to(start_rows, row_base, row_count, key_count, prompt_len):
    row_ids = row_base + lax.broadcasted_iota(jnp.int32, (row_count, key_count), 0)
    key_ids = lax.broadcasted_iota(jnp.int32, (row_count, key_count), 1)
    own_segment = (key_ids < prompt_len) | (key_ids >= start_rows)
    return (key_ids <= row_ids) & own_segment


def attend_kernel(
    heads, block, prompt_len, scale,
    left_ref, right_ref, weight_left_ref, weight_right_ref, out_weight_ref, cos_ref, sin_ref, start_ref,
    qkv_ref, attended_ref, log_ref, partial_ref,
):
    raw = jnp.dot(left_ref[...], weight_left_ref[...], preferred_element_type=F32)
    raw = raw + jnp.dot(right_ref[...], weight_right_ref[...], preferred_element_type=F32)
    cosine, sine = cos_ref[...], sin_ref[...]
    half = HD // 2
    tokens = raw.shape[0]
    partial = jnp.zeros(partial_ref.shape, F32)
    for head in range(heads):
        base = head * 3 * HD
        for kind in range(3):
            piece = raw[:, base + kind * HD : base + (kind + 1) * HD]
            if kind < 2:
                one, two = piece[:, :half], piece[:, half:]
                piece = jnp.concatenate(
                    [one * cosine - two * sine, one * sine + two * cosine], 1
                )
            qkv_ref[3 * head + kind] = piece.astype(BF16)
        for low in range(0, tokens, block):
            rows = pl.ds(low, block)
            keys = low + block
            scores = matmul(qkv_ref[3 * head, rows], qkv_ref[3 * head + 1, :keys], 1, 1) * scale
            seen = visible_to(start_ref[rows], low, block, keys, prompt_len)
            scores = jnp.where(seen, scores, MASKED)
            top = jnp.max(scores, 1, keepdims=True)
            weights = jnp.exp(scores - top)
            total = jnp.sum(weights, 1, keepdims=True)
            result = matmul(weights.astype(BF16), qkv_ref[3 * head + 2, :keys], 1, 0) / total
            attended_ref[head, rows] = result
            log_ref[head, rows] = top + jnp.log(total)
        partial = partial + jnp.dot(
            attended_ref[head].astype(BF16),
            out_weight_ref[head * HD : (head + 1) * HD],
            preferred_element_type=F32,
        )
    partial_ref[...] = partial.astype(BF16)


def attend(left, right, weight_left, weight_right, out_weight, cosine, sine, start, block):
    tokens, features = left.shape
    heads = weight_left.shape[1] // (3 * HD)
    return pl.pallas_call(
        functools.partial(attend_kernel, heads, block, tokens // 2, HD ** (-0.5)),
        out_shape=(
            jax.ShapeDtypeStruct((3 * heads, tokens, HD), BF16),
            jax.ShapeDtypeStruct((heads, tokens, HD), F32),
            jax.ShapeDtypeStruct((heads, tokens, 1), F32),
            jax.ShapeDtypeStruct((tokens, features), BF16),
        ),
        cost_estimate=LIGHT,
        name="attend",
    )(left, right, weight_left, weight_right, out_weight, cosine, sine, start)


def attend_back_kernel(
    heads, block, prompt_len, scale,
    own_ref, peer_ref, qkv_ref, attended_ref, log_ref, cos_ref, sin_ref, start_ref, normed_ref, weight_ref,
    one_ref, grad_ref, key_acc, value_acc, query_acc,
):
    cosine, sine = cos_ref[...], sin_ref[...]
    half = HD // 2
    tokens = own_ref.shape[0]
    upper = (own_ref[...].astype(F32) + peer_ref[...].astype(F32)).astype(BF16)
    pieces = []
    for head in range(heads):
        head_grad = upper[:, head * HD : (head + 1) * HD]
        delta = jnp.sum(head_grad.astype(F32) * attended_ref[head], 1, keepdims=True)
        key_acc[...] = jnp.zeros_like(key_acc)
        value_acc[...] = jnp.zeros_like(value_acc)
        for low in range(0, tokens, block):
            rows = pl.ds(low, block)
            keys = low + block
            query = qkv_ref[3 * head, rows]
            key = qkv_ref[3 * head + 1, :keys]
            scores = matmul(query, key, 1, 1) * scale
            seen = visible_to(start_ref[rows], low, block, keys, prompt_len)
            weights = jnp.where(seen, jnp.exp(scores - log_ref[head, rows]), 0.0)
            grad_rows = head_grad[low : low + block]
            prob_dot = matmul(grad_rows, qkv_ref[3 * head + 2, :keys], 1, 1)
            score_grad = (weights * (prob_dot - delta[low : low + block]) * scale).astype(BF16)
            query_acc[rows] = matmul(score_grad, key, 1, 0)
            key_acc[:keys] += matmul(score_grad, query, 0, 0)
            value_acc[:keys] += matmul(weights.astype(BF16), grad_rows, 0, 0)
        for piece in (query_acc[...], key_acc[...]):
            one, two = piece[:, :half], piece[:, half:]
            pieces += [one * cosine + two * sine, two * cosine - one * sine]
        pieces.append(value_acc[...])
    qkv_grad = jnp.concatenate(pieces, 1).astype(BF16)
    one_ref[...] = matmul(qkv_grad, weight_ref[...], 1, 1)
    grad_ref[...] = matmul(normed_ref[...], qkv_grad, 0, 0).astype(BF16)


def attend_back(own, peer, qkv, attended, log_total, cosine, sine, start, normed, weight, block):
    heads, tokens, unused = attended.shape
    return pl.pallas_call(
        functools.partial(attend_back_kernel, heads, block, tokens // 2, HD ** (-0.5)),
        out_shape=(
            jax.ShapeDtypeStruct(normed.shape, F32),
            jax.ShapeDtypeStruct(weight.shape, BF16),
        ),
        scratch_shapes=[pltpu.VMEM((tokens, HD), F32)] * 3,
        cost_estimate=LIGHT,
        name="attend_back",
    )(own, peer, qkv, attended, log_total, cosine, sine, start, normed, weight)


def picks(rank_ref, capacity):
    rank = rank_ref[0]
    return lax.broadcasted_iota(jnp.int32, (capacity, rank.shape[1]), 0) == rank


def ones_where(mask):
    return jnp.where(mask, 1.0, 0.0).astype(BF16)


def back_hidden_kernel(rank_ref, cot_ref, down_ref, grad_ref, rows_ref):
    chosen = ones_where(picks(rank_ref, rows_ref.shape[1]))
    rows = jnp.dot(chosen, cot_ref[...], preferred_element_type=F32).astype(BF16)
    rows_ref[0] = rows
    grad_ref[0] = matmul(rows, down_ref[0], 1, 1).astype(BF16)


def back_hidden(rank, cot_rows, down, first, count, capacity):
    tokens, features = cot_rows.shape
    hidden = down.shape[1]
    return pl.pallas_call(
        back_hidden_kernel,
        grid=(count,),
        in_specs=[
            pl.BlockSpec((1, 1, tokens), lambda i: (first + i, 0, 0)),
            whole_block((tokens, features)),
            pl.BlockSpec((1, hidden, features), lambda i: (first + i, 0, 0)),
        ],
        out_specs=(
            pl.BlockSpec((1, capacity, hidden), lambda i: (i, 0, 0)),
            pl.BlockSpec((1, capacity, features), lambda i: (i, 0, 0)),
        ),
        out_shape=(
            jax.ShapeDtypeStruct((count, capacity, hidden), BF16),
            jax.ShapeDtypeStruct((count, capacity, features), BF16),
        ),
        cost_estimate=LIGHT,
        name="back_hidden",
    )(rank, cot_rows, down)


def open_experts_kernel(rank_ref, token_ref, gate_ref, up_ref, pre_ref, rows_ref):
    hidden = gate_ref.shape[2]
    chosen = ones_where(picks(rank_ref, rows_ref.shape[1]))
    rows = jnp.dot(chosen, token_ref[...], preferred_element_type=F32).astype(BF16)
    rows_ref[0] = rows
    pre_ref[0, :, :hidden] = jnp.dot(rows, gate_ref[0], preferred_element_type=F32).astype(BF16)
    pre_ref[0, :, hidden:] = jnp.dot(rows, up_ref[0], preferred_element_type=F32).astype(BF16)


def open_experts(rank, token_rows, gate, up, first, count, capacity):
    tokens, features = token_rows.shape
    hidden = gate.shape[2]
    return pl.pallas_call(
        open_experts_kernel,
        grid=(count,),
        in_specs=[
            pl.BlockSpec((1, 1, tokens), lambda i: (first + i, 0, 0)),
            whole_block((tokens, features)),
            pl.BlockSpec((1, features, hidden), lambda i: (first + i, 0, 0)),
            pl.BlockSpec((1, features, hidden), lambda i: (first + i, 0, 0)),
        ],
        out_specs=(
            pl.BlockSpec((1, capacity, 2 * hidden), lambda i: (i, 0, 0)),
            pl.BlockSpec((1, capacity, features), lambda i: (i, 0, 0)),
        ),
        out_shape=(
            jax.ShapeDtypeStruct((count, capacity, 2 * hidden), BF16),
            jax.ShapeDtypeStruct((count, capacity, features), BF16),
        ),
        cost_estimate=LIGHT,
        name="open_experts",
    )(rank, token_rows, gate, up)


def gated(pre_gate, pre_up, hidden_grad):
    sigma = 1.0 / (1.0 + jnp.exp(-pre_gate))
    silu = pre_gate * sigma
    grad_gate = hidden_grad * pre_up * sigma * (1.0 + pre_gate * (1.0 - sigma))
    return silu * pre_up, grad_gate, hidden_grad * silu


def experts_kernel(
    rank_ref, prob_ref, pre_own_ref, pre_peer_ref, back_own_ref, back_peer_ref, rows_ref, cot_ref,
    gate_ref, up_ref, down_ref, out_in_ref, dx_in_ref,
    grad_ref, share_ref, out_ref, dx_ref,
):
    capacity, hidden = back_own_ref.shape[1:]

    @pl.when(pl.program_id(0) == 0)
    def start():
        out_ref[...] = out_in_ref[...]
        dx_ref[...] = dx_in_ref[...]

    mask = picks(rank_ref, capacity)
    chosen = ones_where(mask)
    gate_val = jnp.sum(jnp.where(mask, prob_ref[0], 0.0), 1, keepdims=True)
    pre = pre_own_ref[0].astype(F32) + pre_peer_ref[0].astype(F32)
    raw_back = back_own_ref[0].astype(F32) + back_peer_ref[0].astype(F32)
    result, grad_gate, grad_up = gated(pre[:, :hidden], pre[:, hidden:], gate_val * raw_back)
    result = result.astype(BF16).astype(F32)
    share = jnp.sum(result * raw_back, 1, keepdims=True)
    share_ref[0] = jnp.sum(jnp.where(mask, share, 0.0), 0, keepdims=True)
    scaled = (gate_val * result).astype(BF16)
    grad_gate = grad_gate.astype(BF16)
    grad_up = grad_up.astype(BF16)
    rows = rows_ref[0]
    out_rows = jnp.dot(scaled, down_ref[0], preferred_element_type=F32).astype(BF16)
    out_ref[...] += matmul(chosen, out_rows, 0, 0)
    dx_rows = (matmul(grad_gate, gate_ref[0], 1, 1) + matmul(grad_up, up_ref[0], 1, 1)).astype(BF16)
    dx_ref[...] += matmul(chosen, dx_rows, 0, 0)
    grad_ref[0, 0] = matmul(rows, grad_gate, 0, 0).astype(BF16)
    grad_ref[0, 1] = matmul(rows, grad_up, 0, 0).astype(BF16)
    grad_ref[0, 2] = matmul(cot_ref[0], scaled, 0, 0).astype(BF16)


def run_experts(
    rank, probs, pre_own, pre_peer, back_own, back_peer, rows, cot_rows, gate, up, down, out_sum, dx_sum, first
):
    count, capacity, features = rows.shape
    hidden = gate.shape[2]
    tokens = out_sum.shape[0]

    def at(shape, base):
        return pl.BlockSpec((1,) + shape, lambda i: (base + i, 0, 0))

    return pl.pallas_call(
        experts_kernel,
        grid=(count,),
        in_specs=[
            at((1, tokens), first),
            at((1, tokens), first),
            at((capacity, 2 * hidden), 0),
            at((capacity, 2 * hidden), 0),
            at((capacity, hidden), first),
            at((capacity, hidden), first),
            at((capacity, features), 0),
            at((capacity, features), first),
            at((features, hidden), first),
            at((features, hidden), first),
            at((hidden, features), first),
            whole_block((tokens, features)),
            whole_block((tokens, features)),
        ],
        out_specs=(
            pl.BlockSpec((1, 3, features, hidden), lambda i: (i, 0, 0, 0)),
            at((1, tokens), 0),
            whole_block((tokens, features)),
            whole_block((tokens, features)),
        ),
        out_shape=(
            jax.ShapeDtypeStruct((count, 3, features, hidden), BF16),
            jax.ShapeDtypeStruct((count, 1, tokens), F32),
            jax.ShapeDtypeStruct((tokens, features), F32),
            jax.ShapeDtypeStruct((tokens, features), F32),
        ),
        cost_estimate=LIGHT,
        name="run_experts",
    )(
        rank, probs, pre_own, pre_peer, back_own, back_peer, rows, cot_rows, gate, up, down, out_sum, dx_sum
    )


def spread_kernel(core_ref, half_ref, rest_ref, *refs):
    gate_ref, up_ref, down_ref, flag_ref = refs[-4:]
    flag_ref[...] = jnp.zeros_like(flag_ref)

    def write(source_ref):
        gate_ref[0] = source_ref[0, 0].astype(F32)
        up_ref[0] = source_ref[0, 1].astype(F32)
        down_ref[0] = source_ref[0, 2].astype(F32).T

    own = pl.program_id(0) < pl.num_programs(0) // 2
    pl.when(own)(lambda: write(half_ref))
    pl.when(jnp.logical_not(own))(lambda: write(rest_ref))


def spread(core, half_grads, rest_grads, earlier, first, experts):
    half, unused, features, hidden = half_grads.shape

    def own_index(i, core):
        return (jnp.minimum(i, half - 1), 0, 0, 0)

    def rest_index(i, core):
        return (jnp.maximum(i - half, 0), 0, 0, 0)

    def out_index(i, core):
        place = jnp.where(i < half, core[0] * half + i, (1 - core[0]) * half + i - half)
        return (first + place, 0, 0)

    shapes = ((features, hidden), (features, hidden), (hidden, features))
    return pl.pallas_call(
        spread_kernel,
        grid_spec=pltpu.PrefetchScalarGridSpec(
            num_scalar_prefetch=1,
            grid=(2 * half,),
            in_specs=[
                pl.BlockSpec((1, 3, features, hidden), own_index),
                pl.BlockSpec((1, 3, features, hidden), rest_index),
            ]
            + [pl.BlockSpec(memory_space=pl.ANY)] * len(earlier),
            out_specs=tuple(pl.BlockSpec((1,) + shape, out_index) for shape in shapes)
            + (whole_block((8, 128)),),
        ),
        out_shape=tuple(jax.ShapeDtypeStruct((experts,) + shape, F32) for shape in shapes)
        + (jax.ShapeDtypeStruct((8, 128), F32),),
        input_output_aliases={3 + i: i for i in range(len(earlier))},
        cost_estimate=LIGHT,
        name="spread",
    )(core, half_grads, rest_grads, *earlier)


def paired_body(
    inputs,
    cotangent,
    routes,
    cont_lengths,
    first_gain,
    attend_in,
    attend_out,
    second_gain,
    router_weight,
    shared_gate,
    shared_up,
    shared_down,
    expert_gate,
    expert_up,
    expert_down,
):
    col_size = lax.axis_size("col")
    data_size = lax.axis_size("dp")
    col_index = lax.axis_index("col")
    tok_rest, feat_dev = inputs.shape
    feat_full = feat_dev * 2
    tok_block = tok_rest * col_size
    experts = expert_gate.shape[0]
    shared_dev = shared_gate.shape[1]
    capacity = tok_block * 3 // experts
    tokens_all = float(data_size * tok_block)
    prompt_len = tok_block // 2
    block = 256
    chunk = 4
    core = (lax.axis_index("dp") % 2).reshape(1)

    gain_high, gain_low = high_low(first_gain)
    gain_last = (first_gain - gain_high.astype(F32) - gain_low.astype(F32)).astype(BF16)
    gain_rows = jnp.pad(jnp.stack([gain_high, gain_low, gain_last]), ((0, 5), (0, 0)))
    peer_first = swap(jnp.concatenate([inputs, gain_rows], 0), "row")
    peer_gain = jnp.sum(peer_first[tok_rest : tok_rest + 3].astype(F32)[::-1], 0)
    peer_weight = swap(attend_in, "row")
    own_parts = col_parts(inputs)
    peer_parts = [peer_first[:tok_rest]] + [swap(part, "row") for part in own_parts[1:]]
    own_all = in_order(own_parts, "col").reshape(tok_block, feat_dev).astype(F32)
    peer_all = in_order(peer_parts, "col").reshape(tok_block, feat_dev).astype(F32)
    cot_all = col_rows(held(cotangent, *own_parts))

    squares_one = jnp.sum(own_all * own_all, 1) + jnp.sum(peer_all * peer_all, 1)
    scale_all = lax.rsqrt(squares_one / feat_full + EPSILON)[:, None]
    unit_all = own_all * scale_all
    normed_own = (unit_all * first_gain).astype(BF16)
    normed_peer = (peer_all * scale_all * peer_gain).astype(BF16)

    offsets = jnp.arange(tok_block, dtype=jnp.int32)
    after = offsets - prompt_len
    ends = jnp.cumsum(cont_lengths[0])
    begin = jnp.max(jnp.where(ends[None, :] <= after[:, None], ends[None, :], 0), 1)
    start = jnp.where(after < 0, 0, prompt_len + begin)
    position = jnp.where(after < 0, offsets, prompt_len + after - begin)
    angles = angle_table(position)
    cosine, sine = jnp.cos(angles), jnp.sin(angles)
    start = start[:, None]

    expert_ids = jnp.arange(experts, dtype=jnp.int32)
    named = (routes[:, 0][None, :] == expert_ids[:, None]) | (
        routes[:, 1][None, :] == expert_ids[:, None]
    )
    before = (offsets[:, None] < offsets[None, :]).astype(BF16)
    rank = jnp.dot(named.astype(BF16), before, preferred_element_type=F32).astype(jnp.int32)
    rank = jnp.where(named, rank, -1)[:, None, :]
    count_total = sum_by_swaps(jnp.sum(named.astype(F32), 1), ("dp",))

    qkv, attended, log_total, out_partial = attend(
        normed_own, normed_peer, attend_in, peer_weight, attend_out, cosine, sine, start, block
    )
    cot_all = held(cot_all, out_partial)
    back_own, cot_rows = back_hidden(rank, cot_all, expert_down, 0, experts, capacity)
    back_peer = swap(back_own, "row")
    shared_back_own = matmul(cot_all, shared_down, 1, 1).astype(BF16)
    shared_back_peer = swap(shared_back_own, "row")

    inputs_f = inputs.astype(F32)
    mixed_one = inputs_f + held(col_sum_rows(out_partial), back_own, shared_back_own)
    gained = mixed_one * second_gain
    partial_stats = jnp.concatenate(
        [
            jnp.sum(mixed_one * mixed_one, 1, keepdims=True),
            jnp.dot(gained, router_weight, precision=HIGHEST),
        ],
        1,
    )
    stats = partial_stats + swap(partial_stats, "row")
    scale_two = lax.rsqrt(stats[:, :1] / feat_full + EPSILON)
    router_probs = jax.nn.softmax(stats[:, 1:] * scale_two, -1)
    unit_two = mixed_one * scale_two
    normed_two = (unit_two * second_gain).astype(BF16)
    sent = in_order(col_parts(with_rows(normed_two, router_probs.T)), "col")
    normed_all, probs_all = split_rows(sent, tok_rest, experts, tok_rest)
    normed_all = normed_all.reshape(tok_block, feat_dev)
    probs_rows = probs_all.transpose(1, 0, 2).reshape(experts, 1, tok_block)

    pre_own, token_rows, pre_peer = [], [], []
    firsts = list(range(0, experts, chunk))
    for first in firsts:
        pre, rows = open_experts(rank, normed_all, expert_gate, expert_up, first, chunk, capacity)
        pre_own.append(pre)
        token_rows.append(rows)
    shared_pre_own = jnp.concatenate(
        [matmul(normed_all, shared_gate, 1, 0), matmul(normed_all, shared_up, 1, 0)], 1
    ).astype(BF16)
    order = pre_own[:-1] + [shared_pre_own] + pre_own[-1:]
    arrived = []
    for index, value in enumerate(order):
        arrived.append(swap(held(value, *arrived[index - 2 : index - 1]) if index > 1 else value, "row"))
    pre_peer = arrived[:-2] + arrived[-1:]
    shared_pre_peer = arrived[-2]

    out_sum = jnp.zeros((tok_block, feat_dev), F32)
    dx_sum = jnp.zeros((tok_block, feat_dev), F32)
    shares, halves, crossed = [], [], []
    for index, first in enumerate(firsts):
        pre = pre_peer[index]
        if index:
            pre = held(pre, halves[-1])
        if index > 2:
            pre = held(pre, crossed[index - 3])
        grads, share, out_sum, dx_sum = run_experts(
            rank, probs_rows, pre_own[index], pre, back_own, back_peer,
            token_rows[index], cot_rows, expert_gate, expert_up, expert_down, out_sum, dx_sum, first,
        )
        shares.append(share[:, 0])
        halves.append(pair_half(grads))
        crossed.append(cross_sum(held(halves[-1], crossed[-1]) if index else halves[-1]))

    shared_pre = shared_pre_own.astype(F32) + shared_pre_peer.astype(F32)
    shared_back = shared_back_own.astype(F32) + shared_back_peer.astype(F32)
    shared_hidden, shared_gate_pgrad, shared_up_pgrad = (
        value.astype(BF16)
        for value in gated(shared_pre[:, :shared_dev], shared_pre[:, shared_dev:], shared_back)
    )
    out_sum = out_sum + matmul(shared_hidden, shared_down, 1, 0)
    dx_sum = (
        dx_sum + matmul(shared_gate_pgrad, shared_gate, 1, 1) + matmul(shared_up_pgrad, shared_up, 1, 1)
    )
    shared_half = pair_half(
        jnp.stack(
            [
                matmul(normed_all, shared_gate_pgrad, 0, 0).astype(BF16),
                matmul(normed_all, shared_up_pgrad, 0, 0).astype(BF16),
                matmul(cot_all, shared_hidden, 0, 0).astype(BF16),
            ],
            1,
        )
    )

    share_rows = jnp.concatenate(shares, 0).reshape(experts, col_size, tok_rest).transpose(1, 0, 2)
    dx_blocks = with_rows(dx_sum.astype(BF16).reshape(col_size, tok_rest, feat_dev), share_rows)
    dx_blocks = col_sum_rows(dx_blocks.reshape(-1, feat_dev))
    normed_grad, gate_grad = split_rows(dx_blocks, tok_rest, experts, tok_rest)
    normed_grad = held(normed_grad, crossed[1], shared_half)
    prob_grad = gate_grad.T + experts * count_total / (2.0 * tokens_all * tokens_all)
    logit_grad = router_probs * (prob_grad - jnp.sum(router_probs * prob_grad, -1, keepdims=True))
    router_grad = jnp.einsum("td,te->ed", unit_two * second_gain, logit_grad, precision=HIGHEST)
    two_grad = normed_grad + jnp.einsum("te,de->td", logit_grad, router_weight, precision=HIGHEST)
    gained_two = two_grad * second_gain
    second_gain_grad = jnp.sum(two_grad * unit_two, 0)
    inner_two = jnp.sum(gained_two * unit_two, 1, keepdims=True)
    inner_two = (inner_two + swap(inner_two, "row")) / feat_full
    cot_f = cotangent.astype(F32)
    mixed_grad = cot_f + scale_two * (gained_two - unit_two * inner_two)
    mix_all = col_rows(mixed_grad.astype(BF16))
    attn_own = matmul(mix_all, attend_out, 1, 1).astype(BF16)
    attn_peer = swap(attn_own, "row")

    expert_grads = ()
    flags = []
    for index, first in enumerate(firsts):
        rest = swap(crossed[index], "dp", 1)
        *expert_grads, flag = spread(core, crossed[index], rest, expert_grads, first, experts)
        flags.append(flag)

    layer_out = (
        mixed_one + col_sum_rows(held(out_sum.astype(BF16), mix_all))
    ).astype(BF16)
    attn_peer = held(attn_peer, crossed[2], flags[0])
    one_partial, attend_in_grad = attend_back(
        attn_own, attn_peer, qkv, attended, log_total, cosine, sine, start, normed_own, attend_in, block
    )
    one_partial = held(one_partial, layer_out)
    heads = attended.shape[0]
    attn_rows = attended.astype(BF16)
    attend_out_grad = jnp.concatenate(
        [matmul(attn_rows[head], mix_all, 0, 0) for head in range(heads)], 0
    ).astype(BF16)
    width = attend_in_grad.shape[1]
    attend_half = pair_half(
        jnp.concatenate([attend_in_grad, attend_out_grad.reshape(-1, width)], 0)
    )
    first_gain_grad = jnp.sum(one_partial * unit_all, 0)
    one_grad = col_sum_rows(one_partial.astype(BF16))
    own_rows = col_index * tok_rest
    unit_one = rows_of(unit_all, own_rows, tok_rest)
    scale_one = rows_of(scale_all, own_rows, tok_rest)
    gained_one = one_grad * first_gain
    inner_one = jnp.sum(gained_one * unit_one, 1, keepdims=True)
    inner_one = (inner_one + swap(inner_one, "row")) / feat_full
    input_grad = (mixed_grad + scale_one * (gained_one - unit_one * inner_one)).astype(BF16)

    prob_sums = jnp.pad(jnp.sum(router_probs, 0), (0, feat_dev - experts))
    totals = sum_by_swaps(
        jnp.concatenate(
            [first_gain_grad[None], second_gain_grad[None], prob_sums[None], router_grad], 0
        ),
        ("dp", "col"),
    )
    prob_total = totals[2, :experts]
    balance_loss = experts * jnp.sum(count_total / (2.0 * tokens_all) * prob_total / tokens_all)
    shared_grads = both_halves(cross_sum(shared_half))
    attend_grads = both_halves(cross_sum(held(attend_half, crossed[3])))
    return (
        layer_out,
        input_grad,
        totals[0],
        attend_grads[:feat_dev],
        attend_grads[feat_dev:].reshape(attend_out_grad.shape),
        totals[1],
        totals[3:].T,
        shared_grads[:, 0],
        shared_grads[:, 1],
        shared_grads[:, 2].T,
        expert_grads[0],
        expert_grads[1],
        expert_grads[2],
        balance_loss,
    )


def power_of_two(number):
    return number & (number - 1) == 0


def chosen_body(*shards):
    inputs, cont_lengths = shards[0], shards[3]
    tok_block = inputs.shape[0] * lax.axis_size("col")
    paired = (
        lax.axis_size("row") == 2
        and lax.axis_size("dp") >= 2
        and power_of_two(lax.axis_size("dp"))
        and power_of_two(lax.axis_size("col"))
        and cont_lengths.shape[0] == 1
        and tok_block % 512 == 0
        and tok_block <= 2048
    )
    return (paired_body if paired else body)(*shards)


def solution(mesh):
    in_specs = (
        P(("dp", "col"), "row"),
        P(("dp", "col"), "row"),
        P("dp", None),
        P("dp", None),
        P("row"),
        P("row", "col"),
        P("col", "row"),
        P("row"),
        P("row", None),
        P("row", "col"),
        P("row", "col"),
        P("col", "row"),
        P(None, "row", "col"),
        P(None, "row", "col"),
        P(None, "col", "row"),
    )
    out_specs = (
        P(("dp", "col"), "row"),
        P(("dp", "col"), "row"),
        P("row"),
        P("row", "col"),
        P("col", "row"),
        P("row"),
        P("row", None),
        P("row", "col"),
        P("row", "col"),
        P("col", "row"),
        P(None, "row", "col"),
        P(None, "row", "col"),
        P(None, "col", "row"),
        P(),
    )
    return jax.shard_map(chosen_body, mesh=mesh, in_specs=in_specs, out_specs=out_specs, check_vma=False)
```

```python
import functools

import jax
import jax.numpy as jnp
from jax import lax
from jax.experimental import pallas as pl
from jax.experimental.pallas import tpu as pltpu
from jax.sharding import PartitionSpec as P

HD = 64


EPSILON = 1e-05
HIGHEST = lax.Precision.HIGHEST


def for_sending(value):
    return jax.tree.map(lambda a: a.astype(jnp.bfloat16) if a.dtype == jnp.float32 else a, value)


def feature_sums(values):
    return lax.psum(values, "row")


def token_gather(values):
    return lax.all_gather(values, "col", axis=0, tiled=True)


def slot_gather(values):
    return jax.tree.map(
        lambda part, own: part.astype(own.dtype),
        lax.all_gather(for_sending(values), "row", axis=0, tiled=True),
        values,
    )


def row_partials(term_fn, row_count):
    return lax.psum_scatter(
        term_fn(jnp.int32(0), lax.axis_size("row") * row_count),
        "row",
        scatter_dimension=0,
        tiled=True,
    )


def col_partials(term_fn, row_count):
    return lax.psum_scatter(
        term_fn(jnp.int32(0), lax.axis_size("col") * row_count).astype(jnp.bfloat16),
        "col",
        scatter_dimension=0,
        tiled=True,
    ).astype(jnp.float32)


def token_stats(values):
    return lax.psum(values, ("dp", "col"))


def rows_of(source, row_start, row_count):
    return lax.dynamic_slice_in_dim(source, row_start, row_count, 0)


def angle_table(position):
    half_dim = HD // 2
    frequency = 10000.0 ** (-jnp.arange(half_dim, dtype=jnp.float32) * 2.0 / HD)
    return position.astype(jnp.float32)[:, None] * frequency[None, :]


def rotate(values, angles):
    half_dim = values.shape[-1] // 2
    cosine = jnp.cos(angles)[:, None, :]
    sine_part = jnp.sin(angles)[:, None, :]
    first_half = values[..., :half_dim]
    second_half = values[..., half_dim:]
    return jnp.concatenate(
        [
            first_half * cosine - second_half * sine_part,
            first_half * sine_part + second_half * cosine,
        ],
        -1,
    )


def token_layout(cont_lengths, offsets, group_len):
    prompt_len = group_len // 2
    group_ids = offsets // group_len
    inner_pos = offsets % group_len
    seg_ends = jnp.cumsum(cont_lengths, axis=1)
    seg_starts = seg_ends - cont_lengths
    group_pick = (
        group_ids[:, None] == jnp.arange(cont_lengths.shape[0], dtype=jnp.int32)[None, :]
    ).astype(jnp.int32)
    ends_own = jnp.sum(group_pick[:, :, None] * seg_ends[None, :, :], 1)
    starts_own = jnp.sum(group_pick[:, :, None] * seg_starts[None, :, :], 1)
    after_prompt = inner_pos - prompt_len
    segment = 1 + jnp.sum((after_prompt[:, None] >= ends_own).astype(jnp.int32), 1)
    segment = jnp.where(after_prompt < 0, 0, segment)
    slot_pick = segment[:, None] - 1 == jnp.arange(cont_lengths.shape[1], dtype=jnp.int32)[None, :]
    seg_begin = jnp.sum(jnp.where(slot_pick, starts_own, 0), 1)
    position = jnp.where(segment == 0, inner_pos, prompt_len + after_prompt - seg_begin)
    return (group_ids, segment, position)


def gate_up_grad(pre_gate, pre_up, hidden_grad):
    gate_sig = jax.nn.sigmoid(pre_gate)
    grad_gate = hidden_grad * pre_up * gate_sig * (1.0 + pre_gate * (1.0 - gate_sig))
    grad_up = hidden_grad * pre_gate * gate_sig
    return jnp.concatenate([grad_gate, grad_up], 1).astype(jnp.bfloat16)


def body(
    inputs,
    cotangent,
    routes,
    cont_lengths,
    first_gain,
    attend_in,
    attend_out,
    second_gain,
    router_weight,
    shared_gate,
    shared_up,
    shared_down,
    expert_gate,
    expert_up,
    expert_down,
):
    row_size = lax.axis_size("row")
    col_size = lax.axis_size("col")
    data_size = lax.axis_size("dp")
    row_index = lax.axis_index("row")
    col_index = lax.axis_index("col")
    tok_rest, feat_dev = inputs.shape
    feat_full = feat_dev * row_size
    tok_block = tok_rest * col_size
    tok_query = tok_block // row_size
    experts = expert_gate.shape[0]
    hidden_dev = expert_gate.shape[2]
    shared_dev = shared_gate.shape[1]
    head_cols = attend_in.shape[1]
    heads_dev = head_cols // (3 * HD)
    capacity = tok_block * 3 // experts
    slots_dev = experts * capacity // row_size
    group_len = tok_block // cont_lengths.shape[0]
    key_block = min(1024, tok_query)
    block_count = group_len // key_block
    score_scale = HD ** (-0.5)
    tokens_all = float(data_size * tok_block)
    group_base = row_index * tok_query // group_len * group_len
    inputs_f = inputs.astype(jnp.float32)
    squares_one = feature_sums(jnp.sum(inputs_f * inputs_f, 1))
    scale_one = lax.rsqrt(squares_one / feat_full + EPSILON)[:, None]
    normed_one = (inputs_f * scale_one * first_gain).astype(jnp.bfloat16)
    normed_all = token_gather(normed_one)

    def qkv_term(row_start, row_count):
        return jnp.dot(
            rows_of(normed_all, row_start, row_count), attend_in, preferred_element_type=jnp.float32
        )

    qkv_raw = row_partials(qkv_term, tok_query).reshape(tok_query, heads_dev, 3, HD)
    query_offsets = row_index * tok_query + jnp.arange(tok_query, dtype=jnp.int32)
    query_group, query_segment, query_position = token_layout(
        cont_lengths, query_offsets, group_len
    )
    key_group, key_segment, key_position = token_layout(
        cont_lengths, jnp.arange(tok_block, dtype=jnp.int32), group_len
    )
    query_angles = angle_table(query_position)
    queries = rotate(qkv_raw[:, :, 0], query_angles).astype(jnp.bfloat16)
    keys_own = rotate(qkv_raw[:, :, 1], query_angles).astype(jnp.bfloat16)
    values_own = qkv_raw[:, :, 2].astype(jnp.bfloat16)
    keys_all, values_all = slot_gather(
        (keys_own.reshape(tok_query, heads_dev * HD), values_own.reshape(tok_query, heads_dev * HD))
    )

    def block_scores(block_start):
        key_rows = rows_of(keys_all, block_start, key_block).reshape(key_block, heads_dev, HD)
        block_group = rows_of(key_group, block_start, key_block)
        block_segment = rows_of(key_segment, block_start, key_block)
        block_position = rows_of(key_position, block_start, key_block)
        visible = (
            (query_group[:, None] == block_group[None, :])
            & ((block_segment[None, :] == 0) | (block_segment[None, :] == query_segment[:, None]))
            & (block_position[None, :] <= query_position[:, None])
        )
        scores = (
            jnp.einsum("qhd,khd->hqk", queries, key_rows, preferred_element_type=jnp.float32)
            * score_scale
        )
        return (scores, visible[None], key_rows)

    def forward_step(carry, block_index):
        run_max, run_total, run_accum = carry
        block_start = group_base + block_index * key_block
        scores, mask_now, key_rows = block_scores(block_start)
        value_rows = (
            rows_of(values_all, block_start, key_block)
            .reshape(key_block, heads_dev, HD)
            .astype(jnp.float32)
        )
        new_max = jnp.maximum(run_max, jnp.max(jnp.where(mask_now, scores, -1e30), -1))
        weights = jnp.where(mask_now, jnp.exp(scores - new_max[..., None]), 0.0)
        run_decay = jnp.exp(run_max - new_max)
        run_total = run_total * run_decay + jnp.sum(weights, -1)
        run_accum = run_accum * run_decay[..., None] + jnp.einsum(
            "hqk,khd->hqd", weights, value_rows, precision=HIGHEST
        )
        return ((new_max, run_total, run_accum), None)

    start_carry = (
        jnp.full((heads_dev, tok_query), -1e30, jnp.float32),
        jnp.zeros((heads_dev, tok_query), jnp.float32),
        jnp.zeros((heads_dev, tok_query, HD), jnp.float32),
    )
    (run_max, run_total, run_accum), unused_out = lax.scan(
        forward_step, start_carry, jnp.arange(block_count, dtype=jnp.int32)
    )
    log_total = run_max + jnp.log(run_total)
    attended = run_accum / run_total[..., None]
    attn_rows = attended.transpose(1, 0, 2).reshape(tok_query, heads_dev * HD).astype(jnp.bfloat16)
    outputs_all = slot_gather(attn_rows)

    def attention_term(row_start, row_count):
        return jnp.dot(
            rows_of(outputs_all, row_start, row_count),
            attend_out,
            preferred_element_type=jnp.float32,
        )

    mixed_one = inputs_f + col_partials(attention_term, tok_rest)
    gained = mixed_one * second_gain
    squares_two, logit_part = feature_sums(
        (jnp.sum(mixed_one * mixed_one, 1), jnp.dot(gained, router_weight, precision=HIGHEST))
    )
    scale_two = lax.rsqrt(squares_two / feat_full + EPSILON)[:, None]
    router_probs = jax.nn.softmax(logit_part * scale_two, -1)
    routes_rest = lax.dynamic_slice_in_dim(routes, col_index * tok_rest, tok_rest, 0)
    route_hot = routes_rest[:, :, None] == jnp.arange(experts, dtype=jnp.int32)[None, None, :]
    gate_vals = jnp.sum(jnp.where(route_hot, router_probs[:, None, :], 0.0), -1)
    count_total, prob_total = token_stats(
        (jnp.sum(route_hot.astype(jnp.float32), (0, 1)), jnp.sum(router_probs, 0))
    )
    balance_loss = experts * jnp.sum(count_total / (2.0 * tokens_all) * prob_total / tokens_all)
    unit_two = mixed_one * scale_two
    normed_two = (unit_two * second_gain).astype(jnp.bfloat16)
    normed_two_all = token_gather(normed_two)
    flat_routes = routes.reshape(-1)
    flat_hot = (flat_routes[:, None] == jnp.arange(experts, dtype=jnp.int32)[None, :]).astype(
        jnp.int32
    )
    earlier = jnp.cumsum(flat_hot, 0) - flat_hot
    slot_of = flat_routes * capacity + jnp.sum(earlier * flat_hot, 1)
    slot_pairs = slot_of.reshape(tok_block, 2)
    slot_source = (
        jnp.full((experts * capacity,), 2 * tok_block, jnp.int32)
        .at[slot_of]
        .set(jnp.arange(2 * tok_block, dtype=jnp.int32))
    )
    padded_two = jnp.concatenate([normed_two_all, jnp.zeros((1, feat_dev), jnp.bfloat16)], 0)
    expert_rows = padded_two[slot_source // 2]
    shared_both = jnp.concatenate([shared_gate, shared_up], 1)

    def shared_term(row_start, row_count):
        return jnp.dot(
            rows_of(normed_two_all, row_start, row_count),
            shared_both,
            preferred_element_type=jnp.float32,
        )

    shared_pre = row_partials(shared_term, tok_query)
    shared_g = shared_pre[:, :shared_dev]
    shared_u = shared_pre[:, shared_dev:]
    shared_hidden = (jax.nn.silu(shared_g) * shared_u).astype(jnp.bfloat16)
    expert_both = jnp.concatenate([expert_gate, expert_up], 2)

    def expert_term(row_start, row_count):
        group_count = row_count // capacity
        picked = rows_of(expert_rows, row_start, row_count).reshape(group_count, capacity, feat_dev)
        return jnp.einsum(
            "ecd,edf->ecf", picked, expert_both, preferred_element_type=jnp.float32
        ).reshape(row_count, 2 * hidden_dev)

    expert_pre = row_partials(expert_term, slots_dev)
    expert_g = expert_pre[:, :hidden_dev]
    expert_u = expert_pre[:, hidden_dev:]
    expert_hidden = (jax.nn.silu(expert_g) * expert_u).astype(jnp.bfloat16)
    shared_all, expert_all = slot_gather((shared_hidden, expert_hidden))
    expert_out = jnp.einsum(
        "ecf,efd->ecd",
        expert_all.reshape(experts, capacity, hidden_dev),
        expert_down,
        preferred_element_type=jnp.float32,
    ).reshape(experts * capacity, feat_dev)

    def output_term(row_start, row_count):
        shared_part = jnp.dot(
            rows_of(shared_all, row_start, row_count),
            shared_down,
            preferred_element_type=jnp.float32,
        )
        pair_slots = rows_of(slot_pairs, row_start, row_count)
        return jnp.concatenate(
            [shared_part, expert_out[pair_slots[:, 0]], expert_out[pair_slots[:, 1]]], 1
        )

    branch_sums = col_partials(output_term, tok_rest)
    shared_result = branch_sums[:, :feat_dev]
    expert_pick = branch_sums[:, feat_dev:].reshape(tok_rest, 2, feat_dev)
    expert_result = jnp.sum(gate_vals[:, :, None] * expert_pick, 1)
    layer_out = (mixed_one + shared_result + expert_result).astype(jnp.bfloat16)
    cot_f = cotangent.astype(jnp.float32)
    gate_grad = feature_sums(jnp.sum(expert_pick * cot_f[:, None, :], -1))
    expert_cot = (
        (gate_vals[:, :, None] * cot_f[:, None, :])
        .astype(jnp.bfloat16)
        .reshape(tok_rest, 2 * feat_dev)
    )
    cot_all = token_gather(jnp.concatenate([cotangent, expert_cot], 1))
    shared_cot = cot_all[:, :feat_dev]
    pair_cot = jnp.concatenate(
        [
            cot_all[:, feat_dev:].reshape(2 * tok_block, feat_dev),
            jnp.zeros((1, feat_dev), jnp.bfloat16),
        ],
        0,
    )
    slot_cot = pair_cot[slot_source]
    shared_down_grad = jnp.einsum(
        "tf,td->fd", shared_all, shared_cot, preferred_element_type=jnp.float32
    )

    def shared_back(row_start, row_count):
        return jnp.einsum(
            "td,fd->tf",
            rows_of(shared_cot, row_start, row_count),
            shared_down,
            preferred_element_type=jnp.float32,
        )

    shared_pgrad = gate_up_grad(shared_g, shared_u, row_partials(shared_back, tok_query))
    expert_down_grad = jnp.einsum(
        "ecf,ecd->efd",
        expert_all.reshape(experts, capacity, hidden_dev),
        slot_cot.reshape(experts, capacity, feat_dev),
        preferred_element_type=jnp.float32,
    )

    def expert_back(row_start, row_count):
        group_count = row_count // capacity
        picked = rows_of(slot_cot, row_start, row_count).reshape(group_count, capacity, feat_dev)
        return jnp.einsum(
            "ecd,efd->ecf", picked, expert_down, preferred_element_type=jnp.float32
        ).reshape(row_count, hidden_dev)

    expert_pgrad = gate_up_grad(expert_g, expert_u, row_partials(expert_back, slots_dev))
    shared_pall, expert_pall = slot_gather((shared_pgrad, expert_pgrad))
    expert_pall_view = expert_pall.reshape(experts, capacity, 2 * hidden_dev)
    expert_both_grad = jnp.einsum(
        "ecd,ecf->edf",
        expert_rows.reshape(experts, capacity, feat_dev),
        expert_pall_view,
        preferred_element_type=jnp.float32,
    )
    expert_input_grad = jnp.einsum(
        "ecf,edf->ecd", expert_pall_view, expert_both, preferred_element_type=jnp.float32
    ).reshape(experts * capacity, feat_dev)
    shared_both_grad = jnp.einsum(
        "td,tf->df", normed_two_all, shared_pall, preferred_element_type=jnp.float32
    )

    def normed_back(row_start, row_count):
        pair_slots = rows_of(slot_pairs, row_start, row_count)
        shared_part = jnp.einsum(
            "tf,df->td",
            rows_of(shared_pall, row_start, row_count),
            shared_both,
            preferred_element_type=jnp.float32,
        )
        return (
            shared_part + expert_input_grad[pair_slots[:, 0]] + expert_input_grad[pair_slots[:, 1]]
        )

    normed_grad = col_partials(normed_back, tok_rest)
    prob_grad = jnp.sum(
        jnp.where(route_hot, gate_grad[:, :, None], 0.0), 1
    ) + experts * count_total / (2.0 * tokens_all * tokens_all)
    logit_grad = router_probs * (prob_grad - jnp.sum(router_probs * prob_grad, -1, keepdims=True))
    router_grad = jnp.einsum("td,te->de", unit_two * second_gain, logit_grad, precision=HIGHEST)
    two_grad = normed_grad + jnp.einsum("te,de->td", logit_grad, router_weight, precision=HIGHEST)
    gained_two = two_grad * second_gain
    second_gain_grad = jnp.sum(two_grad * unit_two, 0)
    inner_two = feature_sums(jnp.sum(gained_two * unit_two, 1))[:, None] / feat_full
    mixed_grad = cot_f + scale_two * (gained_two - unit_two * inner_two)
    mix_all = token_gather(mixed_grad.astype(jnp.bfloat16))
    attend_out_grad = jnp.einsum(
        "tc,td->cd", outputs_all, mix_all, preferred_element_type=jnp.float32
    )

    def output_back(row_start, row_count):
        return jnp.einsum(
            "td,cd->tc",
            rows_of(mix_all, row_start, row_count),
            attend_out,
            preferred_element_type=jnp.float32,
        )

    attn_grad = (
        row_partials(output_back, tok_query).astype(jnp.bfloat16).reshape(tok_query, heads_dev, HD)
    )
    attn_grad_f = attn_grad.astype(jnp.float32)
    row_delta = jnp.sum(attn_grad_f.transpose(1, 0, 2) * attended, -1)
    queries_f = queries.astype(jnp.float32)

    def backward_step(query_grad, block_index):
        block_start = group_base + block_index * key_block
        scores, mask_now, key_rows = block_scores(block_start)
        value_rows = rows_of(values_all, block_start, key_block).reshape(key_block, heads_dev, HD)
        weights = jnp.where(mask_now, jnp.exp(scores - log_total[..., None]), 0.0)
        prob_dot = jnp.einsum(
            "qhd,khd->hqk", attn_grad, value_rows, preferred_element_type=jnp.float32
        )
        score_grad = weights * (prob_dot - row_delta[..., None])
        query_grad = (
            query_grad
            + jnp.einsum(
                "hqk,khd->qhd", score_grad, key_rows.astype(jnp.float32), precision=HIGHEST
            )
            * score_scale
        )
        key_grad = (
            jnp.einsum("hqk,qhd->khd", score_grad, queries_f, precision=HIGHEST) * score_scale
        )
        value_grad = jnp.einsum("hqk,qhd->khd", weights, attn_grad_f, precision=HIGHEST)
        return (
            query_grad,
            jnp.concatenate(
                [
                    key_grad.reshape(key_block, heads_dev * HD),
                    value_grad.reshape(key_block, heads_dev * HD),
                ],
                1,
            ),
        )

    query_grad, kv_terms = lax.scan(
        backward_step,
        jnp.zeros((tok_query, heads_dev, HD), jnp.float32),
        jnp.arange(block_count, dtype=jnp.int32),
    )
    kv_group = kv_terms.reshape(group_len, 2 * heads_dev * HD)
    kv_full = lax.dynamic_update_slice_in_dim(
        jnp.zeros((tok_block, 2 * heads_dev * HD), jnp.float32), kv_group, group_base, 0
    )

    def kv_term(row_start, row_count):
        return rows_of(kv_full, row_start, row_count)

    kv_grad = row_partials(kv_term, tok_query)
    key_grad_raw = rotate(
        kv_grad[:, : heads_dev * HD].reshape(tok_query, heads_dev, HD), -query_angles
    )
    value_grad_raw = kv_grad[:, heads_dev * HD :].reshape(tok_query, heads_dev, HD)
    query_grad_raw = rotate(query_grad, -query_angles)
    qkv_grad = (
        jnp.stack([query_grad_raw, key_grad_raw, value_grad_raw], 2)
        .reshape(tok_query, head_cols)
        .astype(jnp.bfloat16)
    )
    qkv_all = slot_gather(qkv_grad)
    attend_in_grad = jnp.einsum(
        "td,tc->dc", normed_all, qkv_all, preferred_element_type=jnp.float32
    )

    def input_back(row_start, row_count):
        return jnp.einsum(
            "tc,dc->td",
            rows_of(qkv_all, row_start, row_count),
            attend_in,
            preferred_element_type=jnp.float32,
        )

    one_grad = col_partials(input_back, tok_rest)
    unit_one = inputs_f * scale_one
    gained_one = one_grad * first_gain
    first_gain_grad = jnp.sum(one_grad * unit_one, 0)
    inner_one = feature_sums(jnp.sum(gained_one * unit_one, 1))[:, None] / feat_full
    input_grad = (mixed_grad + scale_one * (gained_one - unit_one * inner_one)).astype(jnp.bfloat16)
    first_gain_grad, second_gain_grad, router_grad = token_stats(
        (first_gain_grad, second_gain_grad, router_grad)
    )
    summed = (
        lax.psum(attend_in_grad.astype(jnp.bfloat16), "dp").astype(jnp.float32),
        lax.psum(attend_out_grad.astype(jnp.bfloat16), "dp").astype(jnp.float32),
        lax.psum(shared_both_grad.astype(jnp.bfloat16), "dp").astype(jnp.float32),
        lax.psum(shared_down_grad.astype(jnp.bfloat16), "dp").astype(jnp.float32),
        lax.psum(expert_both_grad.astype(jnp.bfloat16), "dp").astype(jnp.float32),
        lax.psum(expert_down_grad.astype(jnp.bfloat16), "dp").astype(jnp.float32),
    )
    shared_both_sum = summed[2]
    expert_both_sum = summed[4]
    return (
        layer_out,
        input_grad,
        first_gain_grad,
        summed[0],
        summed[1],
        second_gain_grad,
        router_grad,
        shared_both_sum[:, :shared_dev],
        shared_both_sum[:, shared_dev:],
        summed[3],
        expert_both_sum[:, :, :hidden_dev],
        expert_both_sum[:, :, hidden_dev:],
        summed[5],
        balance_loss,
    )


F32 = jnp.float32
BF16 = jnp.bfloat16
MASKED = -1e30
LIGHT = pl.CostEstimate(flops=1, transcendentals=0, bytes_accessed=1)


def swap(value, axis, step=1):
    size = lax.axis_size(axis)
    return lax.ppermute(value, axis, [(i, i ^ step) for i in range(size)])


def shifted(value, axis, step):
    size = lax.axis_size(axis)
    return lax.ppermute(value, axis, [(i, (i + step) % size) for i in range(size)])


def in_order(parts, axis):
    size, me = len(parts), lax.axis_index(axis)
    whole = jnp.zeros((size,) + parts[0].shape, parts[0].dtype)
    for step, part in enumerate(parts):
        whole = lax.dynamic_update_index_in_dim(whole, part, (me - step) % size, 0)
    return whole


def col_parts(value):
    return [value] + [shifted(value, "col", s) for s in range(1, lax.axis_size("col"))]


def col_rows(value):
    whole = in_order(col_parts(value), "col")
    return whole.reshape((-1,) + value.shape[1:])


def col_sum_rows(whole):
    size, me = lax.axis_size("col"), lax.axis_index("col")
    blocks = whole.reshape((size, whole.shape[0] // size) + whole.shape[1:])
    total = lax.dynamic_index_in_dim(blocks, me, 0, False).astype(F32)
    for step in range(1, size):
        block = lax.dynamic_index_in_dim(blocks, (me + step) % size, 0, False)
        total = total + shifted(block, "col", step).astype(F32)
    return total


def sum_by_swaps(value, axes):
    for axis in axes:
        step = 1
        while step < lax.axis_size(axis):
            value = value + swap(value, axis, step)
            step *= 2
    return value


def stage(*values):
    return lax.optimization_barrier(values)


def held(value, *others):
    return lax.optimization_barrier((value,) + others)[0]


def high_low(value):
    high = value.astype(BF16)
    return high, (value - high.astype(F32)).astype(BF16)


def with_rows(value, extra):
    high, low = high_low(extra)
    rows = jnp.concatenate([high, low], -2)
    room = [(0, 0)] * (rows.ndim - 1) + [(0, value.shape[-1] - rows.shape[-1])]
    return jnp.concatenate([value, jnp.pad(rows, room)], -2)


def split_rows(value, count, extra, width):
    tail = value[..., count:, :width].astype(F32)
    return value[..., :count, :], tail[..., :extra, :] + tail[..., extra:, :]


def add_kernel(one_ref, two_ref, *sum_refs):
    total = (one_ref[...].astype(F32) + two_ref[...].astype(F32)).astype(BF16)
    for index, sum_ref in enumerate(sum_refs):
        pl.when(pl.program_id(0) == index)(lambda sum_ref=sum_ref: sum_ref.__setitem__(Ellipsis, total))


def added(one, two):
    steps = one.shape[0]
    shape = (1,) + one.shape[1:]
    spec = pl.BlockSpec(shape, lambda i: (i,) + (0,) * (one.ndim - 1))
    return pl.pallas_call(
        add_kernel,
        grid=(steps,),
        in_specs=[spec, spec],
        out_specs=[whole_block(shape)] * steps,
        out_shape=[jax.ShapeDtypeStruct(shape, BF16)] * steps,
        cost_estimate=LIGHT,
        name="added",
    )(one, two)


def join_kernel(one_ref, two_ref, pair_ref):
    pl.when(pl.program_id(0) == 0)(lambda: pair_ref.__setitem__(Ellipsis, one_ref[...]))
    pl.when(pl.program_id(0) == 1)(lambda: pair_ref.__setitem__(Ellipsis, two_ref[...]))


def joined(one, two):
    return pl.pallas_call(
        join_kernel,
        grid=(2,),
        in_specs=[whole_block(one.shape)] * 2,
        out_specs=pl.BlockSpec(one.shape, lambda i: (i,) + (0,) * (one.ndim - 1)),
        out_shape=jax.ShapeDtypeStruct((2,) + one.shape[1:], BF16),
        cost_estimate=LIGHT,
        name="joined",
    )(one, two)


def pair_half(whole):
    core = lax.axis_index("dp") % 2
    halves = whole.reshape((2, whole.shape[0] // 2) + whole.shape[1:])
    mine = lax.dynamic_index_in_dim(halves, core, 0, False)
    other = lax.dynamic_index_in_dim(halves, 1 - core, 0, False)
    return (mine.astype(F32) + swap(other, "dp", 1).astype(F32)).astype(BF16)


def sent_back(blocks):
    return [blocks[0]] + [shifted(blocks[step], "col", -step) for step in range(1, len(blocks))]


def summed_up(blocks):
    total = blocks[0].astype(F32)
    for block in blocks[1:]:
        total = total + block.astype(F32)
    return total


def cross_sum(half):
    step = 2
    while step < lax.axis_size("dp"):
        half = (half.astype(F32) + swap(half, "dp", step).astype(F32)).astype(BF16)
        step *= 2
    return half


def both_halves(half):
    core = lax.axis_index("dp") % 2
    rest = swap(half, "dp", 1)
    first = jnp.where(core == 0, half, rest)
    second = jnp.where(core == 0, rest, half)
    return jnp.concatenate([first, second], 0).astype(F32)


def matmul(left, right, left_dim, right_dim):
    return lax.dot_general(
        left, right, (((left_dim,), (right_dim,)), ((), ())), preferred_element_type=F32
    )


def whole_block(shape):
    return pl.BlockSpec(shape, lambda *unused: (0,) * len(shape))


def visible_to(start_rows, row_base, row_count, key_count, prompt_len):
    row_ids = row_base + lax.broadcasted_iota(jnp.int32, (row_count, key_count), 0)
    key_ids = lax.broadcasted_iota(jnp.int32, (row_count, key_count), 1)
    own_segment = (key_ids < prompt_len) | (key_ids >= start_rows)
    return (key_ids <= row_ids) & own_segment


def attend_kernel(
    heads, block, prompt_len, scale,
    left_ref, right_ref, weight_left_ref, weight_right_ref, out_weight_ref, cos_ref, sin_ref, start_ref,
    qkv_ref, attended_ref, log_ref, partial_ref,
):
    raw = jnp.dot(left_ref[...], weight_left_ref[...], preferred_element_type=F32)
    raw = raw + jnp.dot(right_ref[...], weight_right_ref[...], preferred_element_type=F32)
    cosine, sine = cos_ref[...], sin_ref[...]
    half = HD // 2
    tokens = raw.shape[0]
    partial = jnp.zeros(partial_ref.shape, F32)
    for head in range(heads):
        base = head * 3 * HD
        for kind in range(3):
            piece = raw[:, base + kind * HD : base + (kind + 1) * HD]
            if kind < 2:
                one, two = piece[:, :half], piece[:, half:]
                piece = jnp.concatenate(
                    [one * cosine - two * sine, one * sine + two * cosine], 1
                )
            qkv_ref[3 * head + kind] = piece.astype(BF16)
        for low in range(0, tokens, block):
            rows = pl.ds(low, block)
            keys = low + block
            scores = matmul(qkv_ref[3 * head, rows], qkv_ref[3 * head + 1, :keys], 1, 1) * scale
            seen = visible_to(start_ref[rows], low, block, keys, prompt_len)
            scores = jnp.where(seen, scores, MASKED)
            top = jnp.max(scores, 1, keepdims=True)
            weights = jnp.exp(scores - top)
            total = jnp.sum(weights, 1, keepdims=True)
            result = matmul(weights.astype(BF16), qkv_ref[3 * head + 2, :keys], 1, 0) / total
            attended_ref[head, rows] = result
            log_ref[head, rows] = top + jnp.log(total)
        partial = partial + jnp.dot(
            attended_ref[head].astype(BF16),
            out_weight_ref[head * HD : (head + 1) * HD],
            preferred_element_type=F32,
        )
    partial_ref[...] = partial.astype(BF16)


def attend(left, right, weight_left, weight_right, out_weight, cosine, sine, start, block):
    tokens, features = left.shape
    heads = weight_left.shape[1] // (3 * HD)
    return pl.pallas_call(
        functools.partial(attend_kernel, heads, block, tokens // 2, HD ** (-0.5)),
        out_shape=(
            jax.ShapeDtypeStruct((3 * heads, tokens, HD), BF16),
            jax.ShapeDtypeStruct((heads, tokens, HD), F32),
            jax.ShapeDtypeStruct((heads, tokens, 1), F32),
            jax.ShapeDtypeStruct((tokens, features), BF16),
        ),
        cost_estimate=LIGHT,
        name="attend",
    )(left, right, weight_left, weight_right, out_weight, cosine, sine, start)


def attend_back_kernel(
    heads, block, prompt_len, scale,
    own_ref, peer_ref, qkv_ref, attended_ref, log_ref, cos_ref, sin_ref, start_ref, normed_ref, weight_ref,
    one_ref, grad_ref, key_acc, value_acc, query_acc,
):
    cosine, sine = cos_ref[...], sin_ref[...]
    half = HD // 2
    tokens = own_ref.shape[0]
    upper = (own_ref[...].astype(F32) + peer_ref[...].astype(F32)).astype(BF16)
    pieces = []
    for head in range(heads):
        head_grad = upper[:, head * HD : (head + 1) * HD]
        delta = jnp.sum(head_grad.astype(F32) * attended_ref[head], 1, keepdims=True)
        key_acc[...] = jnp.zeros_like(key_acc)
        value_acc[...] = jnp.zeros_like(value_acc)
        for low in range(0, tokens, block):
            rows = pl.ds(low, block)
            keys = low + block
            query = qkv_ref[3 * head, rows]
            key = qkv_ref[3 * head + 1, :keys]
            scores = matmul(query, key, 1, 1) * scale
            seen = visible_to(start_ref[rows], low, block, keys, prompt_len)
            weights = jnp.where(seen, jnp.exp(scores - log_ref[head, rows]), 0.0)
            grad_rows = head_grad[low : low + block]
            prob_dot = matmul(grad_rows, qkv_ref[3 * head + 2, :keys], 1, 1)
            score_grad = (weights * (prob_dot - delta[low : low + block]) * scale).astype(BF16)
            query_acc[rows] = matmul(score_grad, key, 1, 0)
            key_acc[:keys] += matmul(score_grad, query, 0, 0)
            value_acc[:keys] += matmul(weights.astype(BF16), grad_rows, 0, 0)
        for piece in (query_acc[...], key_acc[...]):
            one, two = piece[:, :half], piece[:, half:]
            pieces += [one * cosine + two * sine, two * cosine - one * sine]
        pieces.append(value_acc[...])
    qkv_grad = jnp.concatenate(pieces, 1).astype(BF16)
    one_ref[...] = matmul(qkv_grad, weight_ref[...], 1, 1)
    grad_ref[...] = matmul(normed_ref[...], qkv_grad, 0, 0).astype(BF16)


def attend_back(own, peer, qkv, attended, log_total, cosine, sine, start, normed, weight, block):
    heads, tokens, unused = attended.shape
    return pl.pallas_call(
        functools.partial(attend_back_kernel, heads, block, tokens // 2, HD ** (-0.5)),
        out_shape=(
            jax.ShapeDtypeStruct(normed.shape, F32),
            jax.ShapeDtypeStruct(weight.shape, BF16),
        ),
        scratch_shapes=[pltpu.VMEM((tokens, HD), F32)] * 3,
        cost_estimate=LIGHT,
        name="attend_back",
    )(own, peer, qkv, attended, log_total, cosine, sine, start, normed, weight)


def picks(rank_ref, capacity):
    rank = rank_ref[0]
    return lax.broadcasted_iota(jnp.int32, (capacity, rank.shape[1]), 0) == rank


def ones_where(mask):
    return jnp.where(mask, 1.0, 0.0).astype(BF16)


def pack_kernel(place_ref, gate_ref, up_ref, down_ref, out_ref):
    out_ref[0, 0] = gate_ref[0]
    out_ref[0, 1] = up_ref[0]
    out_ref[0, 2] = down_ref[0].astype(F32).T.astype(BF16)


def pack(place, gate, up, down, first, count, parts):
    features, hidden = gate.shape[1], gate.shape[2] // parts

    def row_place(i, place):
        return (0, place[i], 0) if parts > 1 else (first + place[i], 0, 0)

    def lane_place(i, place):
        return (0, 0, place[i]) if parts > 1 else (first + place[i], 0, 0)

    return pl.pallas_call(
        pack_kernel,
        grid_spec=pltpu.PrefetchScalarGridSpec(
            num_scalar_prefetch=1,
            grid=(count,),
            in_specs=[
                pl.BlockSpec((1, features, hidden), lane_place),
                pl.BlockSpec((1, features, hidden), lane_place),
                pl.BlockSpec((1, hidden, features), row_place),
            ],
            out_specs=pl.BlockSpec((1, 3, features, hidden), lambda i, place: (i, 0, 0, 0)),
        ),
        out_shape=jax.ShapeDtypeStruct((count, 3, features, hidden), BF16),
        cost_estimate=LIGHT,
        name="pack",
    )(place, gate, up, down)


def gated(pre_gate, pre_up, hidden_grad):
    sigma = 1.0 / (1.0 + jnp.exp(-pre_gate))
    silu = pre_gate * sigma
    grad_gate = hidden_grad * pre_up * sigma * (1.0 + pre_gate * (1.0 - sigma))
    return silu * pre_up, grad_gate, hidden_grad * silu


def shared_kernel(
    place_ref, token_ref, token_peer_ref, cot_ref, cot_peer_ref, gate_ref, up_ref, down_ref, near_ref, far_ref,
    own_grad_ref, other_grad_ref, out_ref, dx_ref, peer_ref,
):
    step = pl.program_id(0)

    @pl.when(step == 0)
    def start():
        peer_ref[...] = near_ref[0]
        out_ref[...] = jnp.zeros_like(out_ref)
        dx_ref[...] = jnp.zeros_like(dx_ref)

    @pl.when(step > 0)
    def turn():
        peer_ref[...] = far_ref[0]

    rows, rows_peer = token_ref[...], token_peer_ref[...]
    gate, up, down = gate_ref[0], up_ref[0], down_ref[0]
    pre_gate = matmul(rows, gate, 1, 0) + matmul(rows_peer, peer_ref[0], 1, 0)
    pre_up = matmul(rows, up, 1, 0) + matmul(rows_peer, peer_ref[1], 1, 0)
    back = matmul(cot_ref[...], down, 1, 1) + matmul(cot_peer_ref[...], peer_ref[2], 1, 0)
    result, grad_gate, grad_up = gated(pre_gate, pre_up, back)
    result, grad_gate, grad_up = result.astype(BF16), grad_gate.astype(BF16), grad_up.astype(BF16)
    out_ref[...] += matmul(result, down, 1, 0)
    dx_ref[...] += matmul(grad_gate, gate, 1, 1) + matmul(grad_up, up, 1, 1)
    grads = (
        matmul(rows, grad_gate, 0, 0).astype(BF16),
        matmul(rows, grad_up, 0, 0).astype(BF16),
        matmul(cot_ref[...], result, 0, 0).astype(BF16),
    )

    def write(target_ref):
        for kind in range(3):
            target_ref[0, kind] = grads[kind]

    pl.when(step == 0)(lambda: write(own_grad_ref))
    pl.when(step > 0)(lambda: write(other_grad_ref))


def run_shared(place, tokens_own, tokens_peer, cot_own, cot_peer, gate, up, down, near, far):
    tokens, features = tokens_own.shape
    hidden = gate.shape[2] // 2
    grads = jax.ShapeDtypeStruct((1, 3, features, hidden), BF16)
    sums = jax.ShapeDtypeStruct((tokens, features), F32)
    return pl.pallas_call(
        shared_kernel,
        grid_spec=pltpu.PrefetchScalarGridSpec(
            num_scalar_prefetch=1,
            grid=(2,),
            in_specs=[whole_block((tokens, features))] * 4
            + [
                pl.BlockSpec((1, features, hidden), lambda i, place: (0, 0, place[i])),
                pl.BlockSpec((1, features, hidden), lambda i, place: (0, 0, place[i])),
                pl.BlockSpec((1, hidden, features), lambda i, place: (0, place[i], 0)),
            ]
            + [whole_block((1, 3, features, hidden))] * 2,
            out_specs=(whole_block(grads.shape),) * 2 + (whole_block(sums.shape),) * 2,
            scratch_shapes=[pltpu.VMEM((3, features, hidden), BF16)],
        ),
        out_shape=(grads, grads, sums, sums),
        cost_estimate=LIGHT,
        name="run_shared",
    )(place, tokens_own, tokens_peer, cot_own, cot_peer, gate, up, down, near, far)


def experts_kernel(
    capacity,
    place_ref, rank_ref, prob_ref, token_ref, token_peer_ref, cot_ref, cot_peer_ref,
    gate_ref, up_ref, down_ref, near_ref, far_ref, out_in_ref, dx_in_ref,
    own_grad_ref, other_grad_ref, share_ref, out_ref, dx_ref, peer_ref,
):
    step = pl.program_id(0)

    @pl.when(step == 0)
    def start():
        out_ref[...] = out_in_ref[...]
        dx_ref[...] = dx_in_ref[...]

    @pl.when(step < 2)
    def first_pair():
        peer_ref[...] = near_ref[0]

    @pl.when(step >= 2)
    def second_pair():
        peer_ref[...] = far_ref[0]

    mask = picks(rank_ref, capacity)
    chosen = ones_where(mask)
    gate_val = jnp.sum(jnp.where(mask, prob_ref[0], 0.0), 1, keepdims=True)
    rows, rows_peer, cot_rows, cot_rows_peer = (
        jnp.dot(chosen, ref[...], preferred_element_type=F32).astype(BF16)
        for ref in (token_ref, token_peer_ref, cot_ref, cot_peer_ref)
    )
    gate, up, down = gate_ref[0], up_ref[0], down_ref[0]
    pre_gate = matmul(rows, gate, 1, 0) + matmul(rows_peer, peer_ref[0], 1, 0)
    pre_up = matmul(rows, up, 1, 0) + matmul(rows_peer, peer_ref[1], 1, 0)
    raw_back = matmul(cot_rows, down, 1, 1) + matmul(cot_rows_peer, peer_ref[2], 1, 0)
    result, grad_gate, grad_up = gated(pre_gate, pre_up, gate_val * raw_back)
    result = result.astype(BF16).astype(F32)
    share = jnp.sum(result * raw_back, 1, keepdims=True)
    share_ref[0] = jnp.sum(jnp.where(mask, share, 0.0), 0, keepdims=True)
    scaled = (gate_val * result).astype(BF16)
    grad_gate = grad_gate.astype(BF16)
    grad_up = grad_up.astype(BF16)
    out_rows = matmul(scaled, down, 1, 0).astype(BF16)
    out_ref[...] += matmul(chosen, out_rows, 0, 0)
    dx_rows = (matmul(grad_gate, gate, 1, 1) + matmul(grad_up, up, 1, 1)).astype(BF16)
    dx_ref[...] += matmul(chosen, dx_rows, 0, 0)
    grads = (
        matmul(rows, grad_gate, 0, 0).astype(BF16),
        matmul(rows, grad_up, 0, 0).astype(BF16),
        matmul(cot_rows, scaled, 0, 0).astype(BF16),
    )

    def write(target_ref):
        for kind in range(3):
            target_ref[0, kind] = grads[kind]

    pl.when(step < 2)(lambda: write(own_grad_ref))
    pl.when(step >= 2)(lambda: write(other_grad_ref))


def run_experts(
    place, rank, probs, tokens_own, tokens_peer, cot_own, cot_peer, gate, up, down, near, far,
    out_sum, dx_sum, first, capacity,
):
    tokens, features = out_sum.shape
    hidden = gate.shape[2]

    def at(shape, base):
        return pl.BlockSpec((1,) + shape, lambda i, place: (base + place[i], 0, 0))

    block = (1, 3, features, hidden)
    grads = jax.ShapeDtypeStruct((2, 3, features, hidden), BF16)
    sums = jax.ShapeDtypeStruct((tokens, features), F32)
    return pl.pallas_call(
        functools.partial(experts_kernel, capacity),
        grid_spec=pltpu.PrefetchScalarGridSpec(
            num_scalar_prefetch=1,
            grid=(4,),
            in_specs=[at((1, tokens), first)] * 2
            + [whole_block((tokens, features))] * 4
            + [
                at((features, hidden), first),
                at((features, hidden), first),
                at((hidden, features), first),
                pl.BlockSpec(block, lambda i, place: (jnp.minimum(i, 1), 0, 0, 0)),
                pl.BlockSpec(block, lambda i, place: (jnp.maximum(i, 2) - 2, 0, 0, 0)),
                whole_block((tokens, features)),
                whole_block((tokens, features)),
            ],
            out_specs=(
                pl.BlockSpec(block, lambda i, place: (place[jnp.minimum(i, 1)] // 2, 0, 0, 0)),
                pl.BlockSpec(block, lambda i, place: (place[jnp.maximum(i, 2)] // 2, 0, 0, 0)),
                at((1, tokens), 0),
                whole_block(sums.shape),
                whole_block(sums.shape),
            ),
            scratch_shapes=[pltpu.VMEM((3, features, hidden), BF16)],
        ),
        out_shape=(grads, grads, jax.ShapeDtypeStruct((4, 1, tokens), F32), sums, sums),
        cost_estimate=LIGHT,
        name="run_experts",
    )(
        place, rank, probs, tokens_own, tokens_peer, cot_own, cot_peer, gate, up, down, near, far,
        out_sum, dx_sum,
    )


def spread_kernel(core_ref, half_ref, rest_ref, *refs):
    gate_ref, up_ref, down_ref, flag_ref = refs[-4:]
    flag_ref[...] = jnp.zeros_like(flag_ref)

    def write(source_ref):
        gate_ref[0] = source_ref[0, 0].astype(F32)
        up_ref[0] = source_ref[0, 1].astype(F32)
        down_ref[0] = source_ref[0, 2].astype(F32).T

    own = pl.program_id(0) < pl.num_programs(0) // 2
    pl.when(own)(lambda: write(half_ref))
    pl.when(jnp.logical_not(own))(lambda: write(rest_ref))


def spread(core, half_grads, rest_grads, earlier, first, experts):
    aliased = min(len(earlier), 3)
    half, unused, features, hidden = half_grads.shape

    def own_index(i, core):
        return (jnp.minimum(i, half - 1), 0, 0, 0)

    def rest_index(i, core):
        return (jnp.maximum(i - half, 0), 0, 0, 0)

    def out_index(i, core):
        place = jnp.where(i < half, 2 * i + core[0], 2 * (i - half) + 1 - core[0])
        return (first + place, 0, 0)

    shapes = ((features, hidden), (features, hidden), (hidden, features))
    return pl.pallas_call(
        spread_kernel,
        grid_spec=pltpu.PrefetchScalarGridSpec(
            num_scalar_prefetch=1,
            grid=(2 * half,),
            in_specs=[
                pl.BlockSpec((1, 3, features, hidden), own_index),
                pl.BlockSpec((1, 3, features, hidden), rest_index),
            ]
            + [pl.BlockSpec(memory_space=pl.ANY)] * len(earlier),
            out_specs=tuple(pl.BlockSpec((1,) + shape, out_index) for shape in shapes)
            + (whole_block((8, 128)),),
        ),
        out_shape=tuple(jax.ShapeDtypeStruct((experts,) + shape, F32) for shape in shapes)
        + (jax.ShapeDtypeStruct((8, 128), F32),),
        input_output_aliases={3 + i: i for i in range(aliased)},
        cost_estimate=LIGHT,
        name="spread",
    )(core, half_grads, rest_grads, *earlier)


def paired_body(
    inputs,
    cotangent,
    routes,
    cont_lengths,
    first_gain,
    attend_in,
    attend_out,
    second_gain,
    router_weight,
    shared_gate,
    shared_up,
    shared_down,
    expert_gate,
    expert_up,
    expert_down,
):
    col_size = lax.axis_size("col")
    data_size = lax.axis_size("dp")
    col_index = lax.axis_index("col")
    tok_rest, feat_dev = inputs.shape
    feat_full = feat_dev * 2
    tok_block = tok_rest * col_size
    experts = expert_gate.shape[0]
    shared_dev = shared_gate.shape[1]
    capacity = tok_block * 3 // experts
    tokens_all = float(data_size * tok_block)
    prompt_len = tok_block // 2
    block = 256
    chunk = 4
    shards = lax.axis_index("dp")
    core = (shards % 2).reshape(1)
    place = jnp.stack([shards, shards ^ 2, shards ^ 1, shards ^ 3])
    sides = jnp.stack([shards % 2, 1 - shards % 2])
    firsts = list(range(0, experts, 4))
    by_quarters = 2

    own_parts = col_parts(inputs)
    gain_high, gain_low = high_low(first_gain)
    gain_last = (first_gain - gain_high.astype(F32) - gain_low.astype(F32)).astype(BF16)
    gain_rows = jnp.pad(jnp.stack([gain_high, gain_low, gain_last]), ((0, 5), (0, 0)))
    peer_first = swap(jnp.concatenate([inputs, gain_rows], 0), "row")
    peer_gain = jnp.sum(peer_first[tok_rest : tok_rest + 3].astype(F32)[::-1], 0)
    peer_weight = swap(attend_in, "row")
    peer_parts = [peer_first[:tok_rest]] + [swap(part, "row") for part in own_parts[1:]]
    own_all = in_order(own_parts, "col").reshape(tok_block, feat_dev).astype(F32)
    peer_all = in_order(peer_parts, "col").reshape(tok_block, feat_dev).astype(F32)

    shared_gate, shared_up, shared_down = shared_gate[None], shared_up[None], shared_down[None]

    def pack_experts(place, index):
        return pack(place, expert_gate, expert_up, expert_down, firsts[index], 1, 1)

    late_place = held(place, peer_parts[1])
    packed = [pack_experts(late_place, 0), pack_experts(late_place, 1)]

    squares_one = jnp.sum(own_all * own_all, 1) + jnp.sum(peer_all * peer_all, 1)
    scale_all = lax.rsqrt(squares_one / feat_full + EPSILON)[:, None]
    unit_all = own_all * scale_all
    normed_own = (unit_all * first_gain).astype(BF16)
    normed_peer = (peer_all * scale_all * peer_gain).astype(BF16)

    offsets = jnp.arange(tok_block, dtype=jnp.int32)
    after = offsets - prompt_len
    ends = jnp.cumsum(cont_lengths[0])
    begin = jnp.max(jnp.where(ends[None, :] <= after[:, None], ends[None, :], 0), 1)
    start = jnp.where(after < 0, 0, prompt_len + begin)
    position = jnp.where(after < 0, offsets, prompt_len + after - begin)
    angles = angle_table(position)
    cosine, sine = jnp.cos(angles), jnp.sin(angles)
    start = start[:, None]

    expert_ids = jnp.arange(experts, dtype=jnp.int32)
    named = (routes[:, 0][None, :] == expert_ids[:, None]) | (
        routes[:, 1][None, :] == expert_ids[:, None]
    )
    before = (offsets[:, None] < offsets[None, :]).astype(BF16)
    rank = jnp.dot(named.astype(BF16), before, preferred_element_type=F32).astype(jnp.int32)
    rank = jnp.where(named, rank, -1).reshape(experts, col_size, tok_rest)
    rank = jnp.concatenate(
        [
            lax.dynamic_index_in_dim(rank, (col_index - step) % col_size, 1, False)
            for step in range(col_size)
        ],
        1,
    )[:, None, :]
    count_total = sum_by_swaps(jnp.sum(named.astype(F32), 1), ("dp",))

    packed, place, sides, normed_own, normed_peer, peer_weight, cot_sent, count_total = stage(
        packed, place, sides, normed_own, normed_peer, peer_weight, cotangent, count_total
    )
    weights = [swap(packed[0], "row")]
    cot_parts = col_parts(cot_sent)
    qkv, attended, log_total, out_partial = attend(
        normed_own, normed_peer, attend_in, peer_weight, attend_out, cosine, sine, start, block
    )
    late_place = held(place, out_partial)
    packed += [pack_experts(late_place, 2), pack_experts(late_place, 3)]
    weights, cot_parts, out_partial, packed, place = stage(weights, cot_parts, out_partial, packed, place)

    weights.append(swap(packed[1], "row"))
    across = swap(weights[0], "dp", 2)
    cot_own = jnp.concatenate(cot_parts, 0)
    inputs_f = inputs.astype(F32)
    mixed_one = inputs_f + col_sum_rows(out_partial)
    late_place, late_sides = held((place[1:], sides), cot_own)
    packed.append(pack_experts(late_place, 3))
    shared_packed = pack(late_sides, shared_gate, shared_up, shared_down, 0, 1, 2)
    weights, across, cot_own, mixed_one, shared_packed, packed = stage(
        weights, across, cot_own, mixed_one, shared_packed, packed
    )

    gained = mixed_one * second_gain
    partial_stats = jnp.concatenate(
        [
            jnp.sum(mixed_one * mixed_one, 1, keepdims=True),
            jnp.dot(gained, router_weight, precision=HIGHEST),
        ],
        1,
    )
    stats = partial_stats + swap(partial_stats, "row")
    scale_two = lax.rsqrt(stats[:, :1] / feat_full + EPSILON)
    router_probs = jax.nn.softmax(stats[:, 1:] * scale_two, -1)
    unit_two = mixed_one * scale_two
    normed_two = (unit_two * second_gain).astype(BF16)
    normed_sent = with_rows(normed_two, router_probs.T)
    normed_sent, cot_own, shared_packed, weights, across = stage(
        normed_sent, cot_own, shared_packed, weights, across
    )

    sent_parts = col_parts(normed_sent)
    cot_peer = swap(cot_own, "row")
    shared_near = swap(shared_packed, "row")
    near = [joined(weights[0], across)]
    sent_parts, cot_peer, shared_near, near, weights, packed = stage(
        sent_parts, cot_peer, shared_near, near, weights, packed
    )

    opened = [split_rows(part, tok_rest, experts, tok_rest) for part in sent_parts]
    tokens_own = jnp.concatenate([part[0] for part in opened], 0)
    probs = jnp.concatenate([part[1] for part in opened], 1)[:, None, :]
    tokens_peer = swap(tokens_own, "row")
    shared_far = swap(shared_near, "dp", 1)
    far = [swap(near[0], "dp", 1)]
    across = swap(weights[1], "dp", 2)
    tokens_own, tokens_peer, probs, shared_far, far, packed, weights = stage(
        tokens_own, tokens_peer, probs, shared_far, far, packed, weights
    )

    ready, landed, totalled, arrived = [], [], [], []
    expert_grads, finished = [], {}

    def launch(count):
        flights = [(name, half, swap(half, "dp", 2)) for name, half in ready[:count]]
        returns = [(name, total, swap(total, "dp", 1)) for name, total in totalled]
        del ready[:count], totalled[:]
        return flights, returns

    def follow(*values):
        for name, mine, theirs in landed:
            totalled.append((name, added(held(mine, *values) if values else mine, theirs)[0]))
        for name, total, rest in arrived:
            if isinstance(name, int):
                turn = held(core, *values) if values else core
                expert_grads[:] = spread(turn, total, rest, tuple(expert_grads), name, experts)
            else:
                finished[name] = (total, rest)
        del landed[:], arrived[:]

    def land(launched, *values):
        flights, returns = launched
        got = stage(flights_of(flights), flights_of(returns), flights_of(ready), flights_of(totalled),
                    expert_grads[3:], values)
        landed[:] = [(old[0],) + new for old, new in zip(flights, got[0])]
        arrived[:] = [(old[0],) + new for old, new in zip(returns, got[1])]
        ready[:] = [(old[0],) + new for old, new in zip(ready, got[2])]
        totalled[:] = [(old[0],) + new for old, new in zip(totalled, got[3])]
        expert_grads[3:] = got[4]
        return got[5]

    def flights_of(items):
        return [item[1:] for item in items]

    def pair_up(name, mine, theirs, *values):
        for index, half in enumerate(added(held(mine, *values) if values else mine, theirs)):
            ready.append((name + 2 * index if isinstance(name, int) else name, half))

    weights.append(swap(packed[2], "row"))
    shared_mine, shared_other, out_sum, dx_sum = run_shared(
        sides, tokens_own, tokens_peer, cot_own, cot_peer,
        shared_gate, shared_up, shared_down, shared_near, shared_far,
    )
    weights, across, packed, out_sum, dx_sum, shared_mine, shared_other = stage(
        weights, across, packed, out_sum, dx_sum, shared_mine, shared_other
    )
    near.append(joined(weights[1], across))
    shares = []

    def run(index):
        mine, other, share, out_new, dx_new = run_experts(
            place, rank, probs, tokens_own, tokens_peer, cot_own, cot_peer,
            expert_gate, expert_up, expert_down, near[index], far[index], out_sum, dx_sum, firsts[index], capacity,
        )
        shares.append(share[:, 0])
        return mine, other, out_new, dx_new

    far.append(swap(near[1], "dp", 1))
    weights.append(swap(packed[3], "row"))
    across = swap(weights[2], "dp", 2)
    mine, other, out_sum, dx_sum = run(0)
    near.append(joined(held(weights[2], out_sum), across))
    far, weights, mine, other, out_sum, dx_sum, packed, near = stage(
        far, weights, mine, other, out_sum, dx_sum, packed, near
    )
    pair_up(firsts[0], mine, swap(other, "dp", 1))
    launched = launch(1)
    far.append(swap(near[2], "dp", 1))
    weights.append(swap(packed[4], "row"))
    mine, other, out_sum, dx_sum = run(1)
    near.append(joined(held(weights[3], out_sum), weights[4]))
    far, mine, other, out_sum, dx_sum, near = land(launched, far, mine, other, out_sum, dx_sum, near)
    launched = launch(1)
    far.append(swap(near[3], "dp", 1))
    theirs = swap(other, "dp", 1)
    earlier = mine
    mine, other, out_sum, dx_sum = run(2)
    pair_up(firsts[1], earlier, theirs, out_sum)
    follow(out_sum)
    far, mine, other, out_sum, dx_sum = land(launched, far, mine, other, out_sum, dx_sum)
    launched = launch(1)
    theirs = swap(other, "dp", 1)
    shared_theirs = swap(shared_other, "dp", 1)
    earlier = mine
    mine, other, out_sum, dx_sum = run(3)
    pair_up("shared", shared_mine, shared_theirs, out_sum)
    pair_up(firsts[2], earlier, theirs, out_sum)
    follow(out_sum)
    mine, other, out_sum, dx_sum, shares = land(launched, mine, other, out_sum, dx_sum, shares)

    launched = launch(2)
    shares = jnp.concatenate(shares, 0)
    dx_blocks = []
    for step in range(col_size):
        rows = slice(step * tok_rest, (step + 1) * tok_rest)
        dx_blocks.append(with_rows(dx_sum[rows].astype(BF16), shares[:, rows]))
    dx_blocks = sent_back(dx_blocks)
    theirs = swap(other, "dp", 1)
    pair_up(firsts[3], mine, theirs, dx_blocks[1])
    follow(dx_blocks[1])
    (dx_blocks,) = land(launched, dx_blocks)
    launched = launch(2)
    normed_grad, gate_grad = split_rows(summed_up(dx_blocks), tok_rest, experts, tok_rest)
    prob_grad = gate_grad.T + experts * count_total / (2.0 * tokens_all * tokens_all)
    logit_grad = router_probs * (prob_grad - jnp.sum(router_probs * prob_grad, -1, keepdims=True))
    two_grad = normed_grad + jnp.einsum("te,de->td", logit_grad, router_weight, precision=HIGHEST)
    gained_two = two_grad * second_gain
    inner_two = jnp.sum(gained_two * unit_two, 1, keepdims=True)
    inner_two = (inner_two + swap(inner_two, "row")) / feat_full
    cot_f = cotangent.astype(F32)
    mixed_grad = cot_f + scale_two * (gained_two - unit_two * inner_two)
    mix_parts = col_parts(mixed_grad.astype(BF16))
    follow(mix_parts[1])
    mix_parts, logit_grad, two_grad = land(launched, mix_parts, logit_grad, two_grad)

    launched = launch(1)
    mix_all = in_order(mix_parts, "col").reshape(tok_block, feat_dev)
    attn_own = matmul(mix_all, attend_out, 1, 1).astype(BF16)
    attn_peer = swap(attn_own, "row")
    out_low = held(out_sum.astype(BF16), mix_all)
    out_blocks = sent_back([out_low[step * tok_rest : (step + 1) * tok_rest] for step in range(col_size)])
    heads = attended.shape[0]
    attn_rows = attended.astype(BF16)
    attend_out_grad = jnp.concatenate(
        [matmul(attn_rows[head], mix_all, 0, 0) for head in range(heads)], 0
    ).astype(BF16)
    router_grad = jnp.einsum("td,te->ed", unit_two * second_gain, logit_grad, precision=HIGHEST)
    second_gain_grad = jnp.sum(two_grad * unit_two, 0)
    one_partial, attend_in_grad = attend_back(
        attn_own, attn_peer, qkv, attended, log_total, cosine, sine, start, normed_own, attend_in, block
    )
    follow(one_partial)
    one_partial, attend_in_grad, attend_out_grad, out_blocks, router_grad, second_gain_grad = land(
        launched, one_partial, attend_in_grad, attend_out_grad, out_blocks, router_grad, second_gain_grad
    )

    launched = launch(1)
    one_low = one_partial.astype(BF16)
    one_blocks = one_low.reshape(col_size, tok_rest, feat_dev)
    one_blocks = sent_back(
        [
            lax.dynamic_index_in_dim(one_blocks, (col_index - step) % col_size, 0, False)
            for step in range(col_size)
        ]
    )
    layer_out = (mixed_one + summed_up(out_blocks)).astype(BF16)
    width = attend_in_grad.shape[1]
    attend_half = pair_half(
        jnp.concatenate([attend_in_grad, attend_out_grad.reshape(-1, width)], 0)
    )
    first_gain_grad = jnp.sum(one_partial * unit_all, 0)
    prob_sums = jnp.pad(jnp.sum(router_probs, 0), (0, feat_dev - experts))
    totals = jnp.concatenate(
        [first_gain_grad[None], second_gain_grad[None], prob_sums[None], router_grad], 0
    )
    totals = totals + swap(totals, "dp", 1)
    follow(one_blocks[1])
    one_blocks, attend_half, totals = land(launched, one_blocks, attend_half, totals)

    totals = totals + swap(totals, "dp", 2)
    ready.insert(0, ("attend", attend_half[None]))
    launched = launch(2)
    one_grad = summed_up(one_blocks)
    own_rows = col_index * tok_rest
    unit_one = rows_of(unit_all, own_rows, tok_rest)
    scale_one = rows_of(scale_all, own_rows, tok_rest)
    gained_one = one_grad * first_gain
    inner_one = jnp.sum(gained_one * unit_one, 1, keepdims=True)
    inner_one = (inner_one + swap(inner_one, "row")) / feat_full
    input_grad = (mixed_grad + scale_one * (gained_one - unit_one * inner_one)).astype(BF16)
    follow()
    input_grad, totals = land(launched, input_grad, totals)
    totals = sum_by_swaps(totals, ("col",))
    while ready or landed or totalled or arrived:
        follow()
        (totals,) = land(launch(2), totals)

    prob_total = totals[2, :experts]
    balance_loss = experts * jnp.sum(count_total / (2.0 * tokens_all) * prob_total / tokens_all)
    shared_grads = [jnp.concatenate(pair, 3) for pair in (finished["shared"], finished["shared"][::-1])]
    shared_grads = jnp.where(core == 0, *shared_grads)[0].astype(F32)
    attend_grads = [jnp.concatenate(pair, 1) for pair in (finished["attend"], finished["attend"][::-1])]
    attend_grads = jnp.where(core == 0, *attend_grads)[0].astype(F32)
    return (
        layer_out,
        input_grad,
        totals[0],
        attend_grads[:feat_dev],
        attend_grads[feat_dev:].reshape(attend_out_grad.shape),
        totals[1],
        totals[3:].T,
        shared_grads[0],
        shared_grads[1],
        shared_grads[2].T,
        expert_grads[0],
        expert_grads[1],
        expert_grads[2],
        balance_loss,
    )


def power_of_two(number):
    return number & (number - 1) == 0


def chosen_body(*shards):
    inputs, cont_lengths, shared_gate = shards[0], shards[3], shards[9]
    experts, unused, hidden = shards[12].shape
    tok_block = inputs.shape[0] * lax.axis_size("col")
    paired = (
        lax.axis_size("row") == 2
        and lax.axis_size("dp") == 4
        and experts == 16
        and shared_gate.shape[1] == hidden
        and hidden % 256 == 0
        and power_of_two(lax.axis_size("col"))
        and cont_lengths.shape[0] == 1
        and tok_block % 512 == 0
        and tok_block <= 2048
    )
    return (paired_body if paired else body)(*shards)


def solution(mesh):
    in_specs = (
        P(("dp", "col"), "row"),
        P(("dp", "col"), "row"),
        P("dp", None),
        P("dp", None),
        P("row"),
        P("row", "col"),
        P("col", "row"),
        P("row"),
        P("row", None),
        P("row", "col"),
        P("row", "col"),
        P("col", "row"),
        P(None, "row", "col"),
        P(None, "row", "col"),
        P(None, "col", "row"),
    )
    out_specs = (
        P(("dp", "col"), "row"),
        P(("dp", "col"), "row"),
        P("row"),
        P("row", "col"),
        P("col", "row"),
        P("row"),
        P("row", None),
        P("row", "col"),
        P("row", "col"),
        P("col", "row"),
        P(None, "row", "col"),
        P(None, "row", "col"),
        P(None, "col", "row"),
        P(),
    )
    return jax.shard_map(chosen_body, mesh=mesh, in_specs=in_specs, out_specs=out_specs, check_vma=False)
```

```python
import functools

import jax
import jax.numpy as jnp
from jax import lax
from jax.experimental import pallas as pl
from jax.experimental.pallas import tpu as pltpu
from jax.sharding import PartitionSpec as P

HD = 64


EPSILON = 1e-05
HIGHEST = lax.Precision.HIGHEST


def for_sending(value):
    return jax.tree.map(lambda a: a.astype(jnp.bfloat16) if a.dtype == jnp.float32 else a, value)


def feature_sums(values):
    return lax.psum(values, "row")


def token_gather(values):
    return lax.all_gather(values, "col", axis=0, tiled=True)


def slot_gather(values):
    return jax.tree.map(
        lambda part, own: part.astype(own.dtype),
        lax.all_gather(for_sending(values), "row", axis=0, tiled=True),
        values,
    )


def row_partials(term_fn, row_count):
    return lax.psum_scatter(
        term_fn(jnp.int32(0), lax.axis_size("row") * row_count),
        "row",
        scatter_dimension=0,
        tiled=True,
    )


def col_partials(term_fn, row_count):
    return lax.psum_scatter(
        term_fn(jnp.int32(0), lax.axis_size("col") * row_count).astype(jnp.bfloat16),
        "col",
        scatter_dimension=0,
        tiled=True,
    ).astype(jnp.float32)


def token_stats(values):
    return lax.psum(values, ("dp", "col"))


def rows_of(source, row_start, row_count):
    return lax.dynamic_slice_in_dim(source, row_start, row_count, 0)


def angle_table(position):
    half_dim = HD // 2
    frequency = 10000.0 ** (-jnp.arange(half_dim, dtype=jnp.float32) * 2.0 / HD)
    return position.astype(jnp.float32)[:, None] * frequency[None, :]


def rotate(values, angles):
    half_dim = values.shape[-1] // 2
    cosine = jnp.cos(angles)[:, None, :]
    sine_part = jnp.sin(angles)[:, None, :]
    first_half = values[..., :half_dim]
    second_half = values[..., half_dim:]
    return jnp.concatenate(
        [
            first_half * cosine - second_half * sine_part,
            first_half * sine_part + second_half * cosine,
        ],
        -1,
    )


def token_layout(cont_lengths, offsets, group_len):
    prompt_len = group_len // 2
    group_ids = offsets // group_len
    inner_pos = offsets % group_len
    seg_ends = jnp.cumsum(cont_lengths, axis=1)
    seg_starts = seg_ends - cont_lengths
    group_pick = (
        group_ids[:, None] == jnp.arange(cont_lengths.shape[0], dtype=jnp.int32)[None, :]
    ).astype(jnp.int32)
    ends_own = jnp.sum(group_pick[:, :, None] * seg_ends[None, :, :], 1)
    starts_own = jnp.sum(group_pick[:, :, None] * seg_starts[None, :, :], 1)
    after_prompt = inner_pos - prompt_len
    segment = 1 + jnp.sum((after_prompt[:, None] >= ends_own).astype(jnp.int32), 1)
    segment = jnp.where(after_prompt < 0, 0, segment)
    slot_pick = segment[:, None] - 1 == jnp.arange(cont_lengths.shape[1], dtype=jnp.int32)[None, :]
    seg_begin = jnp.sum(jnp.where(slot_pick, starts_own, 0), 1)
    position = jnp.where(segment == 0, inner_pos, prompt_len + after_prompt - seg_begin)
    return (group_ids, segment, position)


def gate_up_grad(pre_gate, pre_up, hidden_grad):
    gate_sig = jax.nn.sigmoid(pre_gate)
    grad_gate = hidden_grad * pre_up * gate_sig * (1.0 + pre_gate * (1.0 - gate_sig))
    grad_up = hidden_grad * pre_gate * gate_sig
    return jnp.concatenate([grad_gate, grad_up], 1).astype(jnp.bfloat16)


def body(
    inputs,
    cotangent,
    routes,
    cont_lengths,
    first_gain,
    attend_in,
    attend_out,
    second_gain,
    router_weight,
    shared_gate,
    shared_up,
    shared_down,
    expert_gate,
    expert_up,
    expert_down,
):
    row_size = lax.axis_size("row")
    col_size = lax.axis_size("col")
    data_size = lax.axis_size("dp")
    row_index = lax.axis_index("row")
    col_index = lax.axis_index("col")
    tok_rest, feat_dev = inputs.shape
    feat_full = feat_dev * row_size
    tok_block = tok_rest * col_size
    tok_query = tok_block // row_size
    experts = expert_gate.shape[0]
    hidden_dev = expert_gate.shape[2]
    shared_dev = shared_gate.shape[1]
    head_cols = attend_in.shape[1]
    heads_dev = head_cols // (3 * HD)
    capacity = tok_block * 3 // experts
    slots_dev = experts * capacity // row_size
    group_len = tok_block // cont_lengths.shape[0]
    key_block = min(1024, tok_query)
    block_count = group_len // key_block
    score_scale = HD ** (-0.5)
    tokens_all = float(data_size * tok_block)
    group_base = row_index * tok_query // group_len * group_len
    inputs_f = inputs.astype(jnp.float32)
    squares_one = feature_sums(jnp.sum(inputs_f * inputs_f, 1))
    scale_one = lax.rsqrt(squares_one / feat_full + EPSILON)[:, None]
    normed_one = (inputs_f * scale_one * first_gain).astype(jnp.bfloat16)
    normed_all = token_gather(normed_one)

    def qkv_term(row_start, row_count):
        return jnp.dot(
            rows_of(normed_all, row_start, row_count), attend_in, preferred_element_type=jnp.float32
        )

    qkv_raw = row_partials(qkv_term, tok_query).reshape(tok_query, heads_dev, 3, HD)
    query_offsets = row_index * tok_query + jnp.arange(tok_query, dtype=jnp.int32)
    query_group, query_segment, query_position = token_layout(
        cont_lengths, query_offsets, group_len
    )
    key_group, key_segment, key_position = token_layout(
        cont_lengths, jnp.arange(tok_block, dtype=jnp.int32), group_len
    )
    query_angles = angle_table(query_position)
    queries = rotate(qkv_raw[:, :, 0], query_angles).astype(jnp.bfloat16)
    keys_own = rotate(qkv_raw[:, :, 1], query_angles).astype(jnp.bfloat16)
    values_own = qkv_raw[:, :, 2].astype(jnp.bfloat16)
    keys_all, values_all = slot_gather(
        (keys_own.reshape(tok_query, heads_dev * HD), values_own.reshape(tok_query, heads_dev * HD))
    )

    def block_scores(block_start):
        key_rows = rows_of(keys_all, block_start, key_block).reshape(key_block, heads_dev, HD)
        block_group = rows_of(key_group, block_start, key_block)
        block_segment = rows_of(key_segment, block_start, key_block)
        block_position = rows_of(key_position, block_start, key_block)
        visible = (
            (query_group[:, None] == block_group[None, :])
            & ((block_segment[None, :] == 0) | (block_segment[None, :] == query_segment[:, None]))
            & (block_position[None, :] <= query_position[:, None])
        )
        scores = (
            jnp.einsum("qhd,khd->hqk", queries, key_rows, preferred_element_type=jnp.float32)
            * score_scale
        )
        return (scores, visible[None], key_rows)

    def forward_step(carry, block_index):
        run_max, run_total, run_accum = carry
        block_start = group_base + block_index * key_block
        scores, mask_now, key_rows = block_scores(block_start)
        value_rows = (
            rows_of(values_all, block_start, key_block)
            .reshape(key_block, heads_dev, HD)
            .astype(jnp.float32)
        )
        new_max = jnp.maximum(run_max, jnp.max(jnp.where(mask_now, scores, -1e30), -1))
        weights = jnp.where(mask_now, jnp.exp(scores - new_max[..., None]), 0.0)
        run_decay = jnp.exp(run_max - new_max)
        run_total = run_total * run_decay + jnp.sum(weights, -1)
        run_accum = run_accum * run_decay[..., None] + jnp.einsum(
            "hqk,khd->hqd", weights, value_rows, precision=HIGHEST
        )
        return ((new_max, run_total, run_accum), None)

    start_carry = (
        jnp.full((heads_dev, tok_query), -1e30, jnp.float32),
        jnp.zeros((heads_dev, tok_query), jnp.float32),
        jnp.zeros((heads_dev, tok_query, HD), jnp.float32),
    )
    (run_max, run_total, run_accum), unused_out = lax.scan(
        forward_step, start_carry, jnp.arange(block_count, dtype=jnp.int32)
    )
    log_total = run_max + jnp.log(run_total)
    attended = run_accum / run_total[..., None]
    attn_rows = attended.transpose(1, 0, 2).reshape(tok_query, heads_dev * HD).astype(jnp.bfloat16)
    outputs_all = slot_gather(attn_rows)

    def attention_term(row_start, row_count):
        return jnp.dot(
            rows_of(outputs_all, row_start, row_count),
            attend_out,
            preferred_element_type=jnp.float32,
        )

    mixed_one = inputs_f + col_partials(attention_term, tok_rest)
    gained = mixed_one * second_gain
    squares_two, logit_part = feature_sums(
        (jnp.sum(mixed_one * mixed_one, 1), jnp.dot(gained, router_weight, precision=HIGHEST))
    )
    scale_two = lax.rsqrt(squares_two / feat_full + EPSILON)[:, None]
    router_probs = jax.nn.softmax(logit_part * scale_two, -1)
    routes_rest = lax.dynamic_slice_in_dim(routes, col_index * tok_rest, tok_rest, 0)
    route_hot = routes_rest[:, :, None] == jnp.arange(experts, dtype=jnp.int32)[None, None, :]
    gate_vals = jnp.sum(jnp.where(route_hot, router_probs[:, None, :], 0.0), -1)
    count_total, prob_total = token_stats(
        (jnp.sum(route_hot.astype(jnp.float32), (0, 1)), jnp.sum(router_probs, 0))
    )
    balance_loss = experts * jnp.sum(count_total / (2.0 * tokens_all) * prob_total / tokens_all)
    unit_two = mixed_one * scale_two
    normed_two = (unit_two * second_gain).astype(jnp.bfloat16)
    normed_two_all = token_gather(normed_two)
    flat_routes = routes.reshape(-1)
    flat_hot = (flat_routes[:, None] == jnp.arange(experts, dtype=jnp.int32)[None, :]).astype(
        jnp.int32
    )
    earlier = jnp.cumsum(flat_hot, 0) - flat_hot
    slot_of = flat_routes * capacity + jnp.sum(earlier * flat_hot, 1)
    slot_pairs = slot_of.reshape(tok_block, 2)
    slot_source = (
        jnp.full((experts * capacity,), 2 * tok_block, jnp.int32)
        .at[slot_of]
        .set(jnp.arange(2 * tok_block, dtype=jnp.int32))
    )
    padded_two = jnp.concatenate([normed_two_all, jnp.zeros((1, feat_dev), jnp.bfloat16)], 0)
    expert_rows = padded_two[slot_source // 2]
    shared_both = jnp.concatenate([shared_gate, shared_up], 1)

    def shared_term(row_start, row_count):
        return jnp.dot(
            rows_of(normed_two_all, row_start, row_count),
            shared_both,
            preferred_element_type=jnp.float32,
        )

    shared_pre = row_partials(shared_term, tok_query)
    shared_g = shared_pre[:, :shared_dev]
    shared_u = shared_pre[:, shared_dev:]
    shared_hidden = (jax.nn.silu(shared_g) * shared_u).astype(jnp.bfloat16)
    expert_both = jnp.concatenate([expert_gate, expert_up], 2)

    def expert_term(row_start, row_count):
        group_count = row_count // capacity
        picked = rows_of(expert_rows, row_start, row_count).reshape(group_count, capacity, feat_dev)
        return jnp.einsum(
            "ecd,edf->ecf", picked, expert_both, preferred_element_type=jnp.float32
        ).reshape(row_count, 2 * hidden_dev)

    expert_pre = row_partials(expert_term, slots_dev)
    expert_g = expert_pre[:, :hidden_dev]
    expert_u = expert_pre[:, hidden_dev:]
    expert_hidden = (jax.nn.silu(expert_g) * expert_u).astype(jnp.bfloat16)
    shared_all, expert_all = slot_gather((shared_hidden, expert_hidden))
    expert_out = jnp.einsum(
        "ecf,efd->ecd",
        expert_all.reshape(experts, capacity, hidden_dev),
        expert_down,
        preferred_element_type=jnp.float32,
    ).reshape(experts * capacity, feat_dev)

    def output_term(row_start, row_count):
        shared_part = jnp.dot(
            rows_of(shared_all, row_start, row_count),
            shared_down,
            preferred_element_type=jnp.float32,
        )
        pair_slots = rows_of(slot_pairs, row_start, row_count)
        return jnp.concatenate(
            [shared_part, expert_out[pair_slots[:, 0]], expert_out[pair_slots[:, 1]]], 1
        )

    branch_sums = col_partials(output_term, tok_rest)
    shared_result = branch_sums[:, :feat_dev]
    expert_pick = branch_sums[:, feat_dev:].reshape(tok_rest, 2, feat_dev)
    expert_result = jnp.sum(gate_vals[:, :, None] * expert_pick, 1)
    layer_out = (mixed_one + shared_result + expert_result).astype(jnp.bfloat16)
    cot_f = cotangent.astype(jnp.float32)
    gate_grad = feature_sums(jnp.sum(expert_pick * cot_f[:, None, :], -1))
    expert_cot = (
        (gate_vals[:, :, None] * cot_f[:, None, :])
        .astype(jnp.bfloat16)
        .reshape(tok_rest, 2 * feat_dev)
    )
    cot_all = token_gather(jnp.concatenate([cotangent, expert_cot], 1))
    shared_cot = cot_all[:, :feat_dev]
    pair_cot = jnp.concatenate(
        [
            cot_all[:, feat_dev:].reshape(2 * tok_block, feat_dev),
            jnp.zeros((1, feat_dev), jnp.bfloat16),
        ],
        0,
    )
    slot_cot = pair_cot[slot_source]
    shared_down_grad = jnp.einsum(
        "tf,td->fd", shared_all, shared_cot, preferred_element_type=jnp.float32
    )

    def shared_back(row_start, row_count):
        return jnp.einsum(
            "td,fd->tf",
            rows_of(shared_cot, row_start, row_count),
            shared_down,
            preferred_element_type=jnp.float32,
        )

    shared_pgrad = gate_up_grad(shared_g, shared_u, row_partials(shared_back, tok_query))
    expert_down_grad = jnp.einsum(
        "ecf,ecd->efd",
        expert_all.reshape(experts, capacity, hidden_dev),
        slot_cot.reshape(experts, capacity, feat_dev),
        preferred_element_type=jnp.float32,
    )

    def expert_back(row_start, row_count):
        group_count = row_count // capacity
        picked = rows_of(slot_cot, row_start, row_count).reshape(group_count, capacity, feat_dev)
        return jnp.einsum(
            "ecd,efd->ecf", picked, expert_down, preferred_element_type=jnp.float32
        ).reshape(row_count, hidden_dev)

    expert_pgrad = gate_up_grad(expert_g, expert_u, row_partials(expert_back, slots_dev))
    shared_pall, expert_pall = slot_gather((shared_pgrad, expert_pgrad))
    expert_pall_view = expert_pall.reshape(experts, capacity, 2 * hidden_dev)
    expert_both_grad = jnp.einsum(
        "ecd,ecf->edf",
        expert_rows.reshape(experts, capacity, feat_dev),
        expert_pall_view,
        preferred_element_type=jnp.float32,
    )
    expert_input_grad = jnp.einsum(
        "ecf,edf->ecd", expert_pall_view, expert_both, preferred_element_type=jnp.float32
    ).reshape(experts * capacity, feat_dev)
    shared_both_grad = jnp.einsum(
        "td,tf->df", normed_two_all, shared_pall, preferred_element_type=jnp.float32
    )

    def normed_back(row_start, row_count):
        pair_slots = rows_of(slot_pairs, row_start, row_count)
        shared_part = jnp.einsum(
            "tf,df->td",
            rows_of(shared_pall, row_start, row_count),
            shared_both,
            preferred_element_type=jnp.float32,
        )
        return (
            shared_part + expert_input_grad[pair_slots[:, 0]] + expert_input_grad[pair_slots[:, 1]]
        )

    normed_grad = col_partials(normed_back, tok_rest)
    prob_grad = jnp.sum(
        jnp.where(route_hot, gate_grad[:, :, None], 0.0), 1
    ) + experts * count_total / (2.0 * tokens_all * tokens_all)
    logit_grad = router_probs * (prob_grad - jnp.sum(router_probs * prob_grad, -1, keepdims=True))
    router_grad = jnp.einsum("td,te->de", unit_two * second_gain, logit_grad, precision=HIGHEST)
    two_grad = normed_grad + jnp.einsum("te,de->td", logit_grad, router_weight, precision=HIGHEST)
    gained_two = two_grad * second_gain
    second_gain_grad = jnp.sum(two_grad * unit_two, 0)
    inner_two = feature_sums(jnp.sum(gained_two * unit_two, 1))[:, None] / feat_full
    mixed_grad = cot_f + scale_two * (gained_two - unit_two * inner_two)
    mix_all = token_gather(mixed_grad.astype(jnp.bfloat16))
    attend_out_grad = jnp.einsum(
        "tc,td->cd", outputs_all, mix_all, preferred_element_type=jnp.float32
    )

    def output_back(row_start, row_count):
        return jnp.einsum(
            "td,cd->tc",
            rows_of(mix_all, row_start, row_count),
            attend_out,
            preferred_element_type=jnp.float32,
        )

    attn_grad = (
        row_partials(output_back, tok_query).astype(jnp.bfloat16).reshape(tok_query, heads_dev, HD)
    )
    attn_grad_f = attn_grad.astype(jnp.float32)
    row_delta = jnp.sum(attn_grad_f.transpose(1, 0, 2) * attended, -1)
    queries_f = queries.astype(jnp.float32)

    def backward_step(query_grad, block_index):
        block_start = group_base + block_index * key_block
        scores, mask_now, key_rows = block_scores(block_start)
        value_rows = rows_of(values_all, block_start, key_block).reshape(key_block, heads_dev, HD)
        weights = jnp.where(mask_now, jnp.exp(scores - log_total[..., None]), 0.0)
        prob_dot = jnp.einsum(
            "qhd,khd->hqk", attn_grad, value_rows, preferred_element_type=jnp.float32
        )
        score_grad = weights * (prob_dot - row_delta[..., None])
        query_grad = (
            query_grad
            + jnp.einsum(
                "hqk,khd->qhd", score_grad, key_rows.astype(jnp.float32), precision=HIGHEST
            )
            * score_scale
        )
        key_grad = (
            jnp.einsum("hqk,qhd->khd", score_grad, queries_f, precision=HIGHEST) * score_scale
        )
        value_grad = jnp.einsum("hqk,qhd->khd", weights, attn_grad_f, precision=HIGHEST)
        return (
            query_grad,
            jnp.concatenate(
                [
                    key_grad.reshape(key_block, heads_dev * HD),
                    value_grad.reshape(key_block, heads_dev * HD),
                ],
                1,
            ),
        )

    query_grad, kv_terms = lax.scan(
        backward_step,
        jnp.zeros((tok_query, heads_dev, HD), jnp.float32),
        jnp.arange(block_count, dtype=jnp.int32),
    )
    kv_group = kv_terms.reshape(group_len, 2 * heads_dev * HD)
    kv_full = lax.dynamic_update_slice_in_dim(
        jnp.zeros((tok_block, 2 * heads_dev * HD), jnp.float32), kv_group, group_base, 0
    )

    def kv_term(row_start, row_count):
        return rows_of(kv_full, row_start, row_count)

    kv_grad = row_partials(kv_term, tok_query)
    key_grad_raw = rotate(
        kv_grad[:, : heads_dev * HD].reshape(tok_query, heads_dev, HD), -query_angles
    )
    value_grad_raw = kv_grad[:, heads_dev * HD :].reshape(tok_query, heads_dev, HD)
    query_grad_raw = rotate(query_grad, -query_angles)
    qkv_grad = (
        jnp.stack([query_grad_raw, key_grad_raw, value_grad_raw], 2)
        .reshape(tok_query, head_cols)
        .astype(jnp.bfloat16)
    )
    qkv_all = slot_gather(qkv_grad)
    attend_in_grad = jnp.einsum(
        "td,tc->dc", normed_all, qkv_all, preferred_element_type=jnp.float32
    )

    def input_back(row_start, row_count):
        return jnp.einsum(
            "tc,dc->td",
            rows_of(qkv_all, row_start, row_count),
            attend_in,
            preferred_element_type=jnp.float32,
        )

    one_grad = col_partials(input_back, tok_rest)
    unit_one = inputs_f * scale_one
    gained_one = one_grad * first_gain
    first_gain_grad = jnp.sum(one_grad * unit_one, 0)
    inner_one = feature_sums(jnp.sum(gained_one * unit_one, 1))[:, None] / feat_full
    input_grad = (mixed_grad + scale_one * (gained_one - unit_one * inner_one)).astype(jnp.bfloat16)
    first_gain_grad, second_gain_grad, router_grad = token_stats(
        (first_gain_grad, second_gain_grad, router_grad)
    )
    summed = (
        lax.psum(attend_in_grad.astype(jnp.bfloat16), "dp").astype(jnp.float32),
        lax.psum(attend_out_grad.astype(jnp.bfloat16), "dp").astype(jnp.float32),
        lax.psum(shared_both_grad.astype(jnp.bfloat16), "dp").astype(jnp.float32),
        lax.psum(shared_down_grad.astype(jnp.bfloat16), "dp").astype(jnp.float32),
        lax.psum(expert_both_grad.astype(jnp.bfloat16), "dp").astype(jnp.float32),
        lax.psum(expert_down_grad.astype(jnp.bfloat16), "dp").astype(jnp.float32),
    )
    shared_both_sum = summed[2]
    expert_both_sum = summed[4]
    return (
        layer_out,
        input_grad,
        first_gain_grad,
        summed[0],
        summed[1],
        second_gain_grad,
        router_grad,
        shared_both_sum[:, :shared_dev],
        shared_both_sum[:, shared_dev:],
        summed[3],
        expert_both_sum[:, :, :hidden_dev],
        expert_both_sum[:, :, hidden_dev:],
        summed[5],
        balance_loss,
    )


F32 = jnp.float32
BF16 = jnp.bfloat16
MASKED = -1e30
LIGHT = pl.CostEstimate(flops=1, transcendentals=0, bytes_accessed=1)


def swap(value, axis, step=1):
    size = lax.axis_size(axis)
    return lax.ppermute(value, axis, [(i, i ^ step) for i in range(size)])


def shifted(value, axis, step):
    size = lax.axis_size(axis)
    return lax.ppermute(value, axis, [(i, (i + step) % size) for i in range(size)])


def in_order(parts, axis):
    size, me = len(parts), lax.axis_index(axis)
    whole = jnp.zeros((size,) + parts[0].shape, parts[0].dtype)
    for step, part in enumerate(parts):
        whole = lax.dynamic_update_index_in_dim(whole, part, (me - step) % size, 0)
    return whole


def col_parts(value):
    return [value] + [shifted(value, "col", s) for s in range(1, lax.axis_size("col"))]


def col_rows(value):
    whole = in_order(col_parts(value), "col")
    return whole.reshape((-1,) + value.shape[1:])


def col_sum_rows(whole):
    size, me = lax.axis_size("col"), lax.axis_index("col")
    blocks = whole.reshape((size, whole.shape[0] // size) + whole.shape[1:])
    total = lax.dynamic_index_in_dim(blocks, me, 0, False).astype(F32)
    for step in range(1, size):
        block = lax.dynamic_index_in_dim(blocks, (me + step) % size, 0, False)
        total = total + shifted(block, "col", step).astype(F32)
    return total


def sum_by_swaps(value, axes):
    for axis in axes:
        step = 1
        while step < lax.axis_size(axis):
            value = value + swap(value, axis, step)
            step *= 2
    return value


def stage(*values):
    return lax.optimization_barrier(values)


def held(value, *others):
    return lax.optimization_barrier((value,) + others)[0]


def high_low(value):
    high = value.astype(BF16)
    return high, (value - high.astype(F32)).astype(BF16)


def with_rows(value, extra):
    high, low = high_low(extra)
    rows = jnp.concatenate([high, low], -2)
    room = [(0, 0)] * (rows.ndim - 1) + [(0, value.shape[-1] - rows.shape[-1])]
    return jnp.concatenate([value, jnp.pad(rows, room)], -2)


def split_rows(value, count, extra, width):
    tail = value[..., count:, :width].astype(F32)
    return value[..., :count, :], tail[..., :extra, :] + tail[..., extra:, :]


def add_kernel(one_ref, two_ref, *sum_refs):
    total = (one_ref[...].astype(F32) + two_ref[...].astype(F32)).astype(BF16)
    for index, sum_ref in enumerate(sum_refs):
        pl.when(pl.program_id(0) == index)(lambda sum_ref=sum_ref: sum_ref.__setitem__(Ellipsis, total))


def added(one, two):
    steps = one.shape[0]
    shape = (1,) + one.shape[1:]
    spec = pl.BlockSpec(shape, lambda i: (i,) + (0,) * (one.ndim - 1))
    return pl.pallas_call(
        add_kernel,
        grid=(steps,),
        in_specs=[spec, spec],
        out_specs=[whole_block(shape)] * steps,
        out_shape=[jax.ShapeDtypeStruct(shape, BF16)] * steps,
        cost_estimate=LIGHT,
        name="added",
    )(one, two)


def pair_half(whole):
    core = lax.axis_index("dp") % 2
    halves = whole.reshape((2, whole.shape[0] // 2) + whole.shape[1:])
    mine = lax.dynamic_index_in_dim(halves, core, 0, False)
    other = lax.dynamic_index_in_dim(halves, 1 - core, 0, False)
    return (mine.astype(F32) + swap(other, "dp", 1).astype(F32)).astype(BF16)


def sent_back(blocks):
    return [blocks[0]] + [shifted(blocks[step], "col", -step) for step in range(1, len(blocks))]


def summed_up(blocks):
    total = blocks[0].astype(F32)
    for block in blocks[1:]:
        total = total + block.astype(F32)
    return total


def cross_sum(half):
    step = 2
    while step < lax.axis_size("dp"):
        half = (half.astype(F32) + swap(half, "dp", step).astype(F32)).astype(BF16)
        step *= 2
    return half


def both_halves(half):
    core = lax.axis_index("dp") % 2
    rest = swap(half, "dp", 1)
    first = jnp.where(core == 0, half, rest)
    second = jnp.where(core == 0, rest, half)
    return jnp.concatenate([first, second], 0).astype(F32)


def matmul(left, right, left_dim, right_dim):
    return lax.dot_general(
        left, right, (((left_dim,), (right_dim,)), ((), ())), preferred_element_type=F32
    )


def whole_block(shape):
    return pl.BlockSpec(shape, lambda *unused: (0,) * len(shape))


def visible_to(start_rows, row_base, row_count, key_count, prompt_len):
    row_ids = row_base + lax.broadcasted_iota(jnp.int32, (row_count, key_count), 0)
    key_ids = lax.broadcasted_iota(jnp.int32, (row_count, key_count), 1)
    own_segment = (key_ids < prompt_len) | (key_ids >= start_rows)
    return (key_ids <= row_ids) & own_segment


def attend_kernel(
    heads, block, prompt_len, scale,
    left_ref, right_ref, weight_left_ref, weight_right_ref, out_weight_ref, cos_ref, sin_ref, start_ref,
    qkv_ref, attended_ref, log_ref, partial_ref,
):
    raw = jnp.dot(left_ref[...], weight_left_ref[...], preferred_element_type=F32)
    raw = raw + jnp.dot(right_ref[...], weight_right_ref[...], preferred_element_type=F32)
    cosine, sine = cos_ref[...], sin_ref[...]
    half = HD // 2
    tokens = raw.shape[0]
    partial = jnp.zeros(partial_ref.shape, F32)
    for head in range(heads):
        base = head * 3 * HD
        for kind in range(3):
            piece = raw[:, base + kind * HD : base + (kind + 1) * HD]
            if kind < 2:
                one, two = piece[:, :half], piece[:, half:]
                piece = jnp.concatenate(
                    [one * cosine - two * sine, one * sine + two * cosine], 1
                )
            qkv_ref[3 * head + kind] = piece.astype(BF16)
        for low in range(0, tokens, block):
            rows = pl.ds(low, block)
            keys = low + block
            scores = matmul(qkv_ref[3 * head, rows], qkv_ref[3 * head + 1, :keys], 1, 1) * scale
            seen = visible_to(start_ref[rows], low, block, keys, prompt_len)
            scores = jnp.where(seen, scores, MASKED)
            top = jnp.max(scores, 1, keepdims=True)
            weights = jnp.exp(scores - top)
            total = jnp.sum(weights, 1, keepdims=True)
            result = matmul(weights.astype(BF16), qkv_ref[3 * head + 2, :keys], 1, 0) / total
            attended_ref[head, rows] = result
            log_ref[head, rows] = top + jnp.log(total)
        partial = partial + jnp.dot(
            attended_ref[head].astype(BF16),
            out_weight_ref[head * HD : (head + 1) * HD],
            preferred_element_type=F32,
        )
    partial_ref[...] = partial.astype(BF16)


def attend(left, right, weight_left, weight_right, out_weight, cosine, sine, start, block):
    tokens, features = left.shape
    heads = weight_left.shape[1] // (3 * HD)
    return pl.pallas_call(
        functools.partial(attend_kernel, heads, block, tokens // 2, HD ** (-0.5)),
        out_shape=(
            jax.ShapeDtypeStruct((3 * heads, tokens, HD), BF16),
            jax.ShapeDtypeStruct((heads, tokens, HD), F32),
            jax.ShapeDtypeStruct((heads, tokens, 1), F32),
            jax.ShapeDtypeStruct((tokens, features), BF16),
        ),
        cost_estimate=LIGHT,
        name="attend",
    )(left, right, weight_left, weight_right, out_weight, cosine, sine, start)


def attend_back_kernel(
    heads, block, prompt_len, scale,
    own_ref, peer_ref, qkv_ref, attended_ref, log_ref, cos_ref, sin_ref, start_ref, normed_ref, weight_ref,
    one_ref, grad_ref, key_acc, value_acc, query_acc,
):
    cosine, sine = cos_ref[...], sin_ref[...]
    half = HD // 2
    tokens = own_ref.shape[0]
    upper = (own_ref[...].astype(F32) + peer_ref[...].astype(F32)).astype(BF16)
    pieces = []
    for head in range(heads):
        head_grad = upper[:, head * HD : (head + 1) * HD]
        delta = jnp.sum(head_grad.astype(F32) * attended_ref[head], 1, keepdims=True)
        key_acc[...] = jnp.zeros_like(key_acc)
        value_acc[...] = jnp.zeros_like(value_acc)
        for low in range(0, tokens, block):
            rows = pl.ds(low, block)
            keys = low + block
            query = qkv_ref[3 * head, rows]
            key = qkv_ref[3 * head + 1, :keys]
            scores = matmul(query, key, 1, 1) * scale
            seen = visible_to(start_ref[rows], low, block, keys, prompt_len)
            weights = jnp.where(seen, jnp.exp(scores - log_ref[head, rows]), 0.0)
            grad_rows = head_grad[low : low + block]
            prob_dot = matmul(grad_rows, qkv_ref[3 * head + 2, :keys], 1, 1)
            score_grad = (weights * (prob_dot - delta[low : low + block]) * scale).astype(BF16)
            query_acc[rows] = matmul(score_grad, key, 1, 0)
            key_acc[:keys] += matmul(score_grad, query, 0, 0)
            value_acc[:keys] += matmul(weights.astype(BF16), grad_rows, 0, 0)
        for piece in (query_acc[...], key_acc[...]):
            one, two = piece[:, :half], piece[:, half:]
            pieces += [one * cosine + two * sine, two * cosine - one * sine]
        pieces.append(value_acc[...])
    qkv_grad = jnp.concatenate(pieces, 1).astype(BF16)
    one_ref[...] = matmul(qkv_grad, weight_ref[...], 1, 1)
    grad_ref[...] = matmul(normed_ref[...], qkv_grad, 0, 0).astype(BF16)


def attend_back(own, peer, qkv, attended, log_total, cosine, sine, start, normed, weight, block):
    heads, tokens, unused = attended.shape
    return pl.pallas_call(
        functools.partial(attend_back_kernel, heads, block, tokens // 2, HD ** (-0.5)),
        out_shape=(
            jax.ShapeDtypeStruct(normed.shape, F32),
            jax.ShapeDtypeStruct(weight.shape, BF16),
        ),
        scratch_shapes=[pltpu.VMEM((tokens, HD), F32)] * 3,
        cost_estimate=LIGHT,
        name="attend_back",
    )(own, peer, qkv, attended, log_total, cosine, sine, start, normed, weight)


def picks(rank_ref, capacity):
    rank = rank_ref[0]
    return lax.broadcasted_iota(jnp.int32, (capacity, rank.shape[1]), 0) == rank


def ones_where(mask):
    return jnp.where(mask, 1.0, 0.0).astype(BF16)


def pack_kernel(place_ref, gate_ref, up_ref, down_ref, out_ref):
    out_ref[0, 0] = gate_ref[0]
    out_ref[0, 1] = up_ref[0]
    out_ref[0, 2] = down_ref[0].astype(F32).T.astype(BF16)


def pack(place, gate, up, down, first, count, parts):
    features, hidden = gate.shape[1], gate.shape[2] // parts

    def row_place(i, place):
        return (0, place[i], 0) if parts > 1 else (first + place[i], 0, 0)

    def lane_place(i, place):
        return (0, 0, place[i]) if parts > 1 else (first + place[i], 0, 0)

    return pl.pallas_call(
        pack_kernel,
        grid_spec=pltpu.PrefetchScalarGridSpec(
            num_scalar_prefetch=1,
            grid=(count,),
            in_specs=[
                pl.BlockSpec((1, features, hidden), lane_place),
                pl.BlockSpec((1, features, hidden), lane_place),
                pl.BlockSpec((1, hidden, features), row_place),
            ],
            out_specs=pl.BlockSpec((1, 3, features, hidden), lambda i, place: (i, 0, 0, 0)),
        ),
        out_shape=jax.ShapeDtypeStruct((count, 3, features, hidden), BF16),
        cost_estimate=LIGHT,
        name="pack",
    )(place, gate, up, down)


def gated(pre_gate, pre_up, hidden_grad):
    sigma = 1.0 / (1.0 + jnp.exp(-pre_gate))
    silu = pre_gate * sigma
    grad_gate = hidden_grad * pre_up * sigma * (1.0 + pre_gate * (1.0 - sigma))
    return silu * pre_up, grad_gate, hidden_grad * silu


def shared_kernel(
    place_ref, token_ref, token_peer_ref, cot_ref, cot_peer_ref, gate_ref, up_ref, down_ref, near_ref, far_ref,
    out_in_ref, dx_in_ref, own_grad_ref, other_grad_ref, out_ref, dx_ref, peer_ref,
):
    step = pl.program_id(0)

    @pl.when(step == 0)
    def start():
        peer_ref[...] = near_ref[0]
        out_ref[...] = out_in_ref[...]
        dx_ref[...] = dx_in_ref[...]

    @pl.when(step > 0)
    def turn():
        peer_ref[...] = far_ref[0]

    rows, rows_peer = token_ref[...], token_peer_ref[...]
    gate, up, down = gate_ref[0], up_ref[0], down_ref[0]
    pre_gate = matmul(rows, gate, 1, 0) + matmul(rows_peer, peer_ref[0], 1, 0)
    pre_up = matmul(rows, up, 1, 0) + matmul(rows_peer, peer_ref[1], 1, 0)
    back = matmul(cot_ref[...], down, 1, 1) + matmul(cot_peer_ref[...], peer_ref[2], 1, 0)
    result, grad_gate, grad_up = gated(pre_gate, pre_up, back)
    result, grad_gate, grad_up = result.astype(BF16), grad_gate.astype(BF16), grad_up.astype(BF16)
    out_ref[...] += matmul(result, down, 1, 0)
    dx_ref[...] += matmul(grad_gate, gate, 1, 1) + matmul(grad_up, up, 1, 1)
    grads = (
        matmul(rows, grad_gate, 0, 0).astype(BF16),
        matmul(rows, grad_up, 0, 0).astype(BF16),
        matmul(cot_ref[...], result, 0, 0).astype(BF16),
    )

    def write(target_ref):
        for kind in range(3):
            target_ref[0, kind] = grads[kind]

    pl.when(step == 0)(lambda: write(own_grad_ref))
    pl.when(step > 0)(lambda: write(other_grad_ref))


def run_shared(place, tokens_own, tokens_peer, cot_own, cot_peer, gate, up, down, near, far, out_sum, dx_sum):
    tokens, features = tokens_own.shape
    hidden = gate.shape[2] // 2
    grads = jax.ShapeDtypeStruct((1, 3, features, hidden), BF16)
    sums = jax.ShapeDtypeStruct((tokens, features), F32)
    return pl.pallas_call(
        shared_kernel,
        grid_spec=pltpu.PrefetchScalarGridSpec(
            num_scalar_prefetch=1,
            grid=(2,),
            in_specs=[whole_block((tokens, features))] * 4
            + [
                pl.BlockSpec((1, features, hidden), lambda i, place: (0, 0, place[i])),
                pl.BlockSpec((1, features, hidden), lambda i, place: (0, 0, place[i])),
                pl.BlockSpec((1, hidden, features), lambda i, place: (0, place[i], 0)),
            ]
            + [whole_block((1, 3, features, hidden))] * 2
            + [whole_block((tokens, features))] * 2,
            out_specs=(whole_block(grads.shape),) * 2 + (whole_block(sums.shape),) * 2,
            scratch_shapes=[pltpu.VMEM((3, features, hidden), BF16)],
        ),
        out_shape=(grads, grads, sums, sums),
        cost_estimate=LIGHT,
        name="run_shared",
    )(place, tokens_own, tokens_peer, cot_own, cot_peer, gate, up, down, near, far, out_sum, dx_sum)


def experts_kernel(
    capacity,
    place_ref, rank_ref, prob_ref, token_ref, token_peer_ref, cot_ref, cot_peer_ref,
    gate_ref, up_ref, down_ref, *refs,
):
    peer_refs, (out_in_ref, dx_in_ref) = refs[:4], refs[4:-6]
    own_grad_ref, other_grad_ref, share_ref, out_ref, dx_ref, peer_ref = refs[-6:]
    step = pl.program_id(0)

    @pl.when(step == 0)
    def start():
        out_ref[...] = out_in_ref[...]
        dx_ref[...] = dx_in_ref[...]

    for index, source_ref in enumerate(peer_refs):
        pl.when(step == index)(lambda source_ref=source_ref: peer_ref.__setitem__(Ellipsis, source_ref[0]))

    mask = picks(rank_ref, capacity)
    chosen = ones_where(mask)
    gate_val = jnp.sum(jnp.where(mask, prob_ref[0], 0.0), 1, keepdims=True)
    rows, rows_peer, cot_rows, cot_rows_peer = (
        jnp.dot(chosen, ref[...], preferred_element_type=F32).astype(BF16)
        for ref in (token_ref, token_peer_ref, cot_ref, cot_peer_ref)
    )
    gate, up, down = gate_ref[0], up_ref[0], down_ref[0]
    pre_gate = matmul(rows, gate, 1, 0) + matmul(rows_peer, peer_ref[0], 1, 0)
    pre_up = matmul(rows, up, 1, 0) + matmul(rows_peer, peer_ref[1], 1, 0)
    raw_back = matmul(cot_rows, down, 1, 1) + matmul(cot_rows_peer, peer_ref[2], 1, 0)
    result, grad_gate, grad_up = gated(pre_gate, pre_up, gate_val * raw_back)
    result = result.astype(BF16).astype(F32)
    share = jnp.sum(result * raw_back, 1, keepdims=True)
    share_ref[0] = jnp.sum(jnp.where(mask, share, 0.0), 0, keepdims=True)
    scaled = (gate_val * result).astype(BF16)
    grad_gate = grad_gate.astype(BF16)
    grad_up = grad_up.astype(BF16)
    out_rows = matmul(scaled, down, 1, 0).astype(BF16)
    out_ref[...] += matmul(chosen, out_rows, 0, 0)
    dx_rows = (matmul(grad_gate, gate, 1, 1) + matmul(grad_up, up, 1, 1)).astype(BF16)
    dx_ref[...] += matmul(chosen, dx_rows, 0, 0)
    grads = (
        matmul(rows, grad_gate, 0, 0).astype(BF16),
        matmul(rows, grad_up, 0, 0).astype(BF16),
        matmul(cot_rows, scaled, 0, 0).astype(BF16),
    )

    def write(target_ref):
        for kind in range(3):
            target_ref[0, kind] = grads[kind]

    pl.when(step < 2)(lambda: write(own_grad_ref))
    pl.when(step >= 2)(lambda: write(other_grad_ref))


def run_experts(
    place, rank, probs, tokens_own, tokens_peer, cot_own, cot_peer, gate, up, down, peers,
    out_sum, dx_sum, first, capacity,
):
    tokens, features = out_sum.shape
    hidden = gate.shape[2]

    def at(shape, base):
        return pl.BlockSpec((1,) + shape, lambda i, place: (base + place[i], 0, 0))

    block = (1, 3, features, hidden)
    grads = jax.ShapeDtypeStruct((2, 3, features, hidden), BF16)
    sums = jax.ShapeDtypeStruct((tokens, features), F32)
    return pl.pallas_call(
        functools.partial(experts_kernel, capacity),
        grid_spec=pltpu.PrefetchScalarGridSpec(
            num_scalar_prefetch=1,
            grid=(4,),
            in_specs=[at((1, tokens), first)] * 2
            + [whole_block((tokens, features))] * 4
            + [
                at((features, hidden), first),
                at((features, hidden), first),
                at((hidden, features), first),
            ]
            + [whole_block(block)] * 4
            + [whole_block((tokens, features))] * 2,
            out_specs=(
                pl.BlockSpec(block, lambda i, place: (place[jnp.minimum(i, 1)] // 2, 0, 0, 0)),
                pl.BlockSpec(block, lambda i, place: (place[jnp.maximum(i, 2)] // 2, 0, 0, 0)),
                at((1, tokens), 0),
                whole_block(sums.shape),
                whole_block(sums.shape),
            ),
            scratch_shapes=[pltpu.VMEM((3, features, hidden), BF16)],
        ),
        out_shape=(grads, grads, jax.ShapeDtypeStruct((4, 1, tokens), F32), sums, sums),
        cost_estimate=LIGHT,
        name="run_experts",
    )(
        place, rank, probs, tokens_own, tokens_peer, cot_own, cot_peer, gate, up, down, *peers,
        out_sum, dx_sum,
    )


def spread_kernel(core_ref, half_ref, rest_ref, *refs):
    gate_ref, up_ref, down_ref, flag_ref = refs[-4:]
    flag_ref[...] = jnp.zeros_like(flag_ref)

    def write(source_ref):
        gate_ref[0] = source_ref[0, 0].astype(F32)
        up_ref[0] = source_ref[0, 1].astype(F32)
        down_ref[0] = source_ref[0, 2].astype(F32).T

    own = pl.program_id(0) < pl.num_programs(0) // 2
    pl.when(own)(lambda: write(half_ref))
    pl.when(jnp.logical_not(own))(lambda: write(rest_ref))


def spread(core, half_grads, rest_grads, earlier, first, experts):
    aliased = min(len(earlier), 3)
    half, unused, features, hidden = half_grads.shape

    def own_index(i, core):
        return (jnp.minimum(i, half - 1), 0, 0, 0)

    def rest_index(i, core):
        return (jnp.maximum(i - half, 0), 0, 0, 0)

    def out_index(i, core):
        place = jnp.where(i < half, 2 * i + core[0], 2 * (i - half) + 1 - core[0])
        return (first + place, 0, 0)

    shapes = ((features, hidden), (features, hidden), (hidden, features))
    return pl.pallas_call(
        spread_kernel,
        grid_spec=pltpu.PrefetchScalarGridSpec(
            num_scalar_prefetch=1,
            grid=(2 * half,),
            in_specs=[
                pl.BlockSpec((1, 3, features, hidden), own_index),
                pl.BlockSpec((1, 3, features, hidden), rest_index),
            ]
            + [pl.BlockSpec(memory_space=pl.ANY)] * len(earlier),
            out_specs=tuple(pl.BlockSpec((1,) + shape, out_index) for shape in shapes)
            + (whole_block((8, 128)),),
        ),
        out_shape=tuple(jax.ShapeDtypeStruct((experts,) + shape, F32) for shape in shapes)
        + (jax.ShapeDtypeStruct((8, 128), F32),),
        input_output_aliases={3 + i: i for i in range(aliased)},
        cost_estimate=LIGHT,
        name="spread",
    )(core, half_grads, rest_grads, *earlier)


def paired_body(
    inputs,
    cotangent,
    routes,
    cont_lengths,
    first_gain,
    attend_in,
    attend_out,
    second_gain,
    router_weight,
    shared_gate,
    shared_up,
    shared_down,
    expert_gate,
    expert_up,
    expert_down,
):
    col_size = lax.axis_size("col")
    data_size = lax.axis_size("dp")
    col_index = lax.axis_index("col")
    tok_rest, feat_dev = inputs.shape
    feat_full = feat_dev * 2
    tok_block = tok_rest * col_size
    experts = expert_gate.shape[0]
    shared_dev = shared_gate.shape[1]
    capacity = tok_block * 3 // experts
    tokens_all = float(data_size * tok_block)
    prompt_len = tok_block // 2
    block = 256
    chunk = 4
    shards = lax.axis_index("dp")
    core = (shards % 2).reshape(1)
    place = jnp.stack([shards, shards ^ 2, shards ^ 1, shards ^ 3])
    sides = jnp.stack([shards % 2, 1 - shards % 2])
    firsts = list(range(0, experts, 4))

    own_parts = col_parts(inputs)
    gain_high, gain_low = high_low(first_gain)
    gain_last = (first_gain - gain_high.astype(F32) - gain_low.astype(F32)).astype(BF16)
    gain_rows = jnp.pad(jnp.stack([gain_high, gain_low, gain_last]), ((0, 5), (0, 0)))
    peer_first = swap(jnp.concatenate([inputs, gain_rows], 0), "row")
    peer_gain = jnp.sum(peer_first[tok_rest : tok_rest + 3].astype(F32)[::-1], 0)
    peer_weight = swap(attend_in, "row")
    peer_parts = [peer_first[:tok_rest]] + [swap(part, "row") for part in own_parts[1:]]
    own_all = in_order(own_parts, "col").reshape(tok_block, feat_dev).astype(F32)

    shared_gate, shared_up, shared_down = shared_gate[None], shared_up[None], shared_down[None]

    def pack_experts(place, index):
        return pack(place, expert_gate, expert_up, expert_down, firsts[index], 1, 1)

    late_place = held(place, own_parts[1:])
    packed = [pack_experts(late_place, 0), pack_experts(late_place, 1)]
    peer_parts[1] = held(peer_parts[1], packed)

    peer_all = in_order(peer_parts, "col").reshape(tok_block, feat_dev).astype(F32)
    squares_one = jnp.sum(own_all * own_all, 1) + jnp.sum(peer_all * peer_all, 1)
    scale_all = lax.rsqrt(squares_one / feat_full + EPSILON)[:, None]
    unit_all = own_all * scale_all
    normed_own = (unit_all * first_gain).astype(BF16)
    normed_peer = (peer_all * scale_all * peer_gain).astype(BF16)

    offsets = jnp.arange(tok_block, dtype=jnp.int32)
    after = offsets - prompt_len
    ends = jnp.cumsum(cont_lengths[0])
    begin = jnp.max(jnp.where(ends[None, :] <= after[:, None], ends[None, :], 0), 1)
    start = jnp.where(after < 0, 0, prompt_len + begin)
    position = jnp.where(after < 0, offsets, prompt_len + after - begin)
    angles = angle_table(position)
    cosine, sine = jnp.cos(angles), jnp.sin(angles)
    start = start[:, None]

    expert_ids = jnp.arange(experts, dtype=jnp.int32)
    named = (routes[:, 0][None, :] == expert_ids[:, None]) | (
        routes[:, 1][None, :] == expert_ids[:, None]
    )
    before = (offsets[:, None] < offsets[None, :]).astype(BF16)
    rank = jnp.dot(named.astype(BF16), before, preferred_element_type=F32).astype(jnp.int32)
    rank = jnp.where(named, rank, -1).reshape(experts, col_size, tok_rest)
    rank = jnp.concatenate(
        [
            lax.dynamic_index_in_dim(rank, (col_index - step) % col_size, 1, False)
            for step in range(col_size)
        ],
        1,
    )[:, None, :]
    count_total = sum_by_swaps(jnp.sum(named.astype(F32), 1), ("dp",))

    packed, place, sides, normed_own, normed_peer, peer_weight, cot_sent, count_total, cosine, sine = stage(
        packed, place, sides, normed_own, normed_peer, peer_weight, cotangent, count_total, cosine, sine
    )
    weights = [swap(packed[0], "row")]
    cot_parts = col_parts(cot_sent)
    qkv, attended, log_total, out_partial = attend(
        normed_own, normed_peer, attend_in, peer_weight, attend_out, cosine, sine, start, block
    )
    late_place = held(place, out_partial)
    packed += [pack_experts(late_place, 2), pack_experts(late_place[1:], 2)]
    weights, cot_parts, out_partial, packed, place = stage(weights, cot_parts, out_partial, packed, place)

    weights.append(swap(packed[1], "row"))
    across = swap(weights[0], "dp", 2)
    cot_own = jnp.concatenate(cot_parts, 0)
    inputs_f = inputs.astype(F32)
    mixed_one = inputs_f + col_sum_rows(out_partial)
    late_place, late_sides = held((place, sides), cot_own)
    packed += [pack_experts(late_place, 3), pack_experts(late_place[1:], 3)]
    shared_packed = pack(late_sides, shared_gate, shared_up, shared_down, 0, 1, 2)
    weights, across, cot_own, mixed_one, shared_packed, packed = stage(
        weights, across, cot_own, mixed_one, shared_packed, packed
    )

    gained = mixed_one * second_gain
    partial_stats = jnp.concatenate(
        [
            jnp.sum(mixed_one * mixed_one, 1, keepdims=True),
            jnp.dot(gained, router_weight, precision=HIGHEST),
        ],
        1,
    )
    peer_stats = swap(partial_stats, "row")
    stats = partial_stats + peer_stats
    scale_two = lax.rsqrt(stats[:, :1] / feat_full + EPSILON)
    router_probs = jax.nn.softmax(stats[:, 1:] * scale_two, -1)
    unit_two = mixed_one * scale_two
    normed_two = (unit_two * second_gain).astype(BF16)
    normed_sent = with_rows(normed_two, router_probs.T)
    normed_sent, cot_own, shared_packed, weights, across = stage(
        normed_sent, cot_own, shared_packed, weights, across
    )

    sent_parts = col_parts(normed_sent)
    cot_peer = swap(cot_own, "row")
    sent_parts, cot_peer, weights, across, packed = stage(sent_parts, cot_peer, weights, across, packed)

    opened = [split_rows(part, tok_rest, experts, tok_rest) for part in sent_parts]
    tokens_own = jnp.concatenate([part[0] for part in opened], 0)
    probs = jnp.concatenate([part[1] for part in opened], 1)[:, None, :]
    tokens_peer = swap(tokens_own, "row")
    far = [swap(weights[0], "dp", 1), swap(across, "dp", 1)]
    peers = [(weights[0], across)]
    across = swap(weights[1], "dp", 2)
    tokens_own, tokens_peer, probs, far, packed, weights = stage(
        tokens_own, tokens_peer, probs, far, packed, weights
    )

    ready, landed, totalled, arrived = [], [], [], []
    expert_grads, finished = [], {}

    def launch(count):
        flights = [(name, half, swap(half, "dp", 2)) for name, half in ready[:count]]
        returns = [(name, total, swap(total, "dp", 1)) for name, total in totalled]
        del ready[:count], totalled[:]
        return flights, returns

    def follow(*values, flying=None, placing=True):
        for name, mine, theirs in landed:
            total = added(held(mine, *values) if values else mine, theirs)[0]
            if flying:
                flying[1].append((name, total, swap(total, "dp", 1)))
            else:
                totalled.append((name, total))
        del landed[:]
        if not placing:
            return
        for name, total, rest in arrived:
            if isinstance(name, int):
                turn = held(core, *values) if values else core
                expert_grads[:] = spread(turn, total, rest, tuple(expert_grads), name, experts)
            else:
                finished[name] = (total, rest)
        del arrived[:]

    def land(launched, *values):
        flights, returns = launched
        got = stage(flights_of(flights), flights_of(returns), flights_of(ready), flights_of(totalled),
                    expert_grads[3:], values)
        landed[:] = [(old[0],) + new for old, new in zip(flights, got[0])]
        arrived[:] = arrived + [(old[0],) + new for old, new in zip(returns, got[1])]
        ready[:] = [(old[0],) + new for old, new in zip(ready, got[2])]
        totalled[:] = [(old[0],) + new for old, new in zip(totalled, got[3])]
        expert_grads[3:] = got[4]
        return got[5]

    def flights_of(items):
        return [item[1:] for item in items]

    def pair_up(name, mine, theirs, *values):
        for index, half in enumerate(added(held(mine, *values) if values else mine, theirs)):
            ready.append((name + 2 * index if isinstance(name, int) else name, half))

    shares = []

    def run(index, near, far, out_sum, dx_sum):
        mine, other, share, out_new, dx_new = run_experts(
            place, rank, probs, tokens_own, tokens_peer, cot_own, cot_peer,
            expert_gate, expert_up, expert_down, tuple(near) + tuple(far), out_sum, dx_sum, firsts[index], capacity,
        )
        shares.append(share[:, 0])
        return mine, other, out_new, dx_new

    zeros = jnp.zeros((tok_block, feat_dev), F32)
    third = swap(packed[2], "row")
    mine, other, out_sum, dx_sum = run(0, peers[0], far, zeros, zeros)
    third, across, weights, mine, other, out_sum, dx_sum, packed, shared_packed = stage(
        third, across, weights, mine, other, out_sum, dx_sum, packed, shared_packed
    )
    near = (weights[1], across)
    far = [swap(part, "dp", 1) for part in near]
    pair_up(firsts[0], mine, swap(other, "dp", 1))
    launched = launch(1)
    third = [third, swap(packed[3], "row")]
    shared_near = swap(shared_packed, "row")
    mine, other, out_sum, dx_sum = run(1, near, far, out_sum, dx_sum)
    third, mine, other, out_sum, dx_sum, packed, shared_near = land(
        launched, third, mine, other, out_sum, dx_sum, packed, shared_near
    )
    launched = launch(1)
    far = [swap(part, "dp", 1) for part in third]
    fourth = swap(packed[4], "row")
    shared_far = swap(shared_near, "dp", 1)
    theirs = swap(other, "dp", 1)
    earlier = mine
    shared_mine, shared_other, out_sum, dx_sum = run_shared(
        sides, tokens_own, tokens_peer, cot_own, cot_peer,
        shared_gate, shared_up, shared_down, shared_near, shared_far, out_sum, dx_sum,
    )
    pair_up(firsts[1], earlier, theirs, out_sum)
    follow(out_sum, flying=launched)
    far, third, fourth, out_sum, dx_sum, packed, shared_mine, shared_other = land(
        launched, far, third, fourth, out_sum, dx_sum, packed, shared_mine, shared_other
    )
    launched = launch(1)
    fourth = [fourth, swap(packed[5], "row")]
    fourth_far = [swap(fourth[0], "dp", 1)]
    mine, other, out_sum, dx_sum = run(2, third, far, out_sum, dx_sum)
    follow(out_sum)
    fourth, fourth_far, mine, other, out_sum, dx_sum = land(
        launched, fourth, fourth_far, mine, other, out_sum, dx_sum
    )
    launched = launch(1)
    fourth_far.append(swap(fourth[1], "dp", 1))
    theirs = swap(other, "dp", 1)
    earlier = mine
    mine, other, out_sum, dx_sum = run(3, fourth, fourth_far, out_sum, dx_sum)
    pair_up(firsts[2], earlier, theirs, out_sum)
    follow(out_sum, placing=False)
    mine, other, out_sum, dx_sum, shares, shared_mine, shared_other = land(
        launched, mine, other, out_sum, dx_sum, shares, shared_mine, shared_other
    )

    launched = launch(1)
    shares = jnp.concatenate(shares, 0)
    dx_blocks = []
    for step in range(col_size):
        rows = slice(step * tok_rest, (step + 1) * tok_rest)
        dx_blocks.append(with_rows(dx_sum[rows].astype(BF16), shares[:, rows]))
    dx_blocks = sent_back(dx_blocks)
    follow(dx_blocks[1:], flying=launched)
    dx_blocks, mine, other, shared_mine, shared_other = land(
        launched, dx_blocks, mine, other, shared_mine, shared_other
    )
    launched = launch(1)
    normed_grad, gate_grad = split_rows(summed_up(dx_blocks), tok_rest, experts, tok_rest)
    prob_grad = gate_grad.T + experts * count_total / (2.0 * tokens_all * tokens_all)
    logit_grad = router_probs * (prob_grad - jnp.sum(router_probs * prob_grad, -1, keepdims=True))
    two_grad = normed_grad + jnp.einsum("te,de->td", logit_grad, router_weight, precision=HIGHEST)
    gained_two = two_grad * second_gain
    inner_two = jnp.sum(gained_two * unit_two, 1, keepdims=True)
    inner_two = (inner_two + swap(inner_two, "row")) / feat_full
    cot_f = cotangent.astype(F32)
    mixed_grad = cot_f + scale_two * (gained_two - unit_two * inner_two)
    mix_parts = col_parts(mixed_grad.astype(BF16))
    theirs = swap(other, "dp", 1)
    pair_up(firsts[3], mine, theirs, mix_parts[1:])
    follow(mix_parts[1:], flying=launched)
    mix_parts, logit_grad, two_grad, out_sum, shared_mine, shared_other = land(
        launched, mix_parts, logit_grad, two_grad, out_sum, shared_mine, shared_other
    )

    launched = launch(1)
    mix_all = in_order(mix_parts, "col").reshape(tok_block, feat_dev)
    attn_own = matmul(mix_all, attend_out, 1, 1).astype(BF16)
    attn_peer = swap(attn_own, "row")
    out_low = out_sum.astype(BF16)
    out_blocks = sent_back([out_low[step * tok_rest : (step + 1) * tok_rest] for step in range(col_size)])
    follow(attn_own, flying=launched)
    attn_peer = held(attn_peer, [item[1] for item in launched[1]], expert_grads[3:])
    heads = attended.shape[0]
    attn_rows = attended.astype(BF16)
    attend_out_grad = jnp.concatenate(
        [matmul(attn_rows[head], mix_all, 0, 0) for head in range(heads)], 0
    ).astype(BF16)
    router_grad = jnp.einsum("td,te->ed", unit_two * second_gain, logit_grad, precision=HIGHEST)
    second_gain_grad = jnp.sum(two_grad * unit_two, 0)
    one_partial, attend_in_grad = attend_back(
        attn_own, attn_peer, qkv, attended, log_total, cosine, sine, start, normed_own, attend_in, block
    )
    shared_half = added(held(shared_mine, one_partial), swap(shared_other, "dp", 1))[0]
    one_partial, attend_in_grad, attend_out_grad, out_blocks, router_grad, second_gain_grad, shared_half = land(
        launched, one_partial, attend_in_grad, attend_out_grad, out_blocks, router_grad, second_gain_grad,
        shared_half,
    )

    launched = launch(1)
    one_low = one_partial.astype(BF16)
    one_blocks = one_low.reshape(col_size, tok_rest, feat_dev)
    one_blocks = sent_back(
        [
            lax.dynamic_index_in_dim(one_blocks, (col_index - step) % col_size, 0, False)
            for step in range(col_size)
        ]
    )
    width = attend_in_grad.shape[1]
    attend_half = pair_half(
        jnp.concatenate([attend_in_grad, attend_out_grad.reshape(-1, width)], 0)
    )
    first_gain_grad = jnp.sum(one_partial * unit_all, 0)
    prob_sums = jnp.pad(jnp.sum(router_probs, 0), (0, feat_dev - experts))
    totals = jnp.concatenate(
        [first_gain_grad[None], second_gain_grad[None], prob_sums[None], router_grad], 0
    )
    totals = totals + swap(totals, "dp", 1)
    layer_out = (mixed_one + summed_up(out_blocks)).astype(BF16)
    follow(one_blocks[1:], flying=launched)
    one_blocks, attend_half, totals = land(launched, one_blocks, attend_half, totals)

    totals = totals + swap(totals, "dp", 2)
    ready += [("attend", attend_half[None]), ("shared", shared_half)]
    launched = launch(9)
    one_grad = summed_up(one_blocks)
    own_rows = col_index * tok_rest
    unit_one = rows_of(unit_all, own_rows, tok_rest)
    scale_one = rows_of(scale_all, own_rows, tok_rest)
    gained_one = one_grad * first_gain
    inner_one = jnp.sum(gained_one * unit_one, 1, keepdims=True)
    inner_one = (inner_one + swap(inner_one, "row")) / feat_full
    input_grad = (mixed_grad + scale_one * (gained_one - unit_one * inner_one)).astype(BF16)
    follow(flying=launched)
    input_grad, totals = land(launched, input_grad, totals)
    totals = sum_by_swaps(totals, ("col",))
    while ready or landed or totalled or arrived:
        follow()
        launched = launch(9)
        landed, arrived = landed + launched[0], arrived + launched[1]

    prob_total = totals[2, :experts]
    balance_loss = experts * jnp.sum(count_total / (2.0 * tokens_all) * prob_total / tokens_all)
    shared_grads = [jnp.concatenate(pair, 3) for pair in (finished["shared"], finished["shared"][::-1])]
    shared_grads = jnp.where(core == 0, *shared_grads)[0].astype(F32)
    attend_grads = [jnp.concatenate(pair, 1) for pair in (finished["attend"], finished["attend"][::-1])]
    attend_grads = jnp.where(core == 0, *attend_grads)[0].astype(F32)
    return (
        layer_out,
        input_grad,
        totals[0],
        attend_grads[:feat_dev],
        attend_grads[feat_dev:].reshape(attend_out_grad.shape),
        totals[1],
        totals[3:].T,
        shared_grads[0],
        shared_grads[1],
        shared_grads[2].T,
        expert_grads[0],
        expert_grads[1],
        expert_grads[2],
        balance_loss,
    )


def power_of_two(number):
    return number & (number - 1) == 0


def chosen_body(*shards):
    inputs, cont_lengths, shared_gate = shards[0], shards[3], shards[9]
    experts, unused, hidden = shards[12].shape
    tok_block = inputs.shape[0] * lax.axis_size("col")
    paired = (
        lax.axis_size("row") == 2
        and lax.axis_size("dp") == 4
        and experts == 16
        and shared_gate.shape[1] == hidden
        and hidden % 256 == 0
        and power_of_two(lax.axis_size("col"))
        and cont_lengths.shape[0] == 1
        and tok_block % 512 == 0
        and tok_block <= 2048
    )
    return (paired_body if paired else body)(*shards)


def solution(mesh):
    in_specs = (
        P(("dp", "col"), "row"),
        P(("dp", "col"), "row"),
        P("dp", None),
        P("dp", None),
        P("row"),
        P("row", "col"),
        P("col", "row"),
        P("row"),
        P("row", None),
        P("row", "col"),
        P("row", "col"),
        P("col", "row"),
        P(None, "row", "col"),
        P(None, "row", "col"),
        P(None, "col", "row"),
    )
    out_specs = (
        P(("dp", "col"), "row"),
        P(("dp", "col"), "row"),
        P("row"),
        P("row", "col"),
        P("col", "row"),
        P("row"),
        P("row", None),
        P("row", "col"),
        P("row", "col"),
        P("col", "row"),
        P(None, "row", "col"),
        P(None, "row", "col"),
        P(None, "col", "row"),
        P(),
    )
    return jax.shard_map(chosen_body, mesh=mesh, in_specs=in_specs, out_specs=out_specs, check_vma=False)
```

```python
import functools

import jax
import jax.numpy as jnp
from jax import lax
from jax.experimental import pallas as pl
from jax.experimental.pallas import tpu as pltpu
from jax.sharding import PartitionSpec as P

HD = 64


EPSILON = 1e-05
HIGHEST = lax.Precision.HIGHEST


def for_sending(value):
    return jax.tree.map(lambda a: a.astype(jnp.bfloat16) if a.dtype == jnp.float32 else a, value)


def feature_sums(values):
    return lax.psum(values, "row")


def token_gather(values):
    return lax.all_gather(values, "col", axis=0, tiled=True)


def slot_gather(values):
    return jax.tree.map(
        lambda part, own: part.astype(own.dtype),
        lax.all_gather(for_sending(values), "row", axis=0, tiled=True),
        values,
    )


def row_partials(term_fn, row_count):
    return lax.psum_scatter(
        term_fn(jnp.int32(0), lax.axis_size("row") * row_count),
        "row",
        scatter_dimension=0,
        tiled=True,
    )


def col_partials(term_fn, row_count):
    return lax.psum_scatter(
        term_fn(jnp.int32(0), lax.axis_size("col") * row_count).astype(jnp.bfloat16),
        "col",
        scatter_dimension=0,
        tiled=True,
    ).astype(jnp.float32)


def token_stats(values):
    return lax.psum(values, ("dp", "col"))


def rows_of(source, row_start, row_count):
    return lax.dynamic_slice_in_dim(source, row_start, row_count, 0)


def angle_table(position):
    half_dim = HD // 2
    frequency = 10000.0 ** (-jnp.arange(half_dim, dtype=jnp.float32) * 2.0 / HD)
    return position.astype(jnp.float32)[:, None] * frequency[None, :]


def rotate(values, angles):
    half_dim = values.shape[-1] // 2
    cosine = jnp.cos(angles)[:, None, :]
    sine_part = jnp.sin(angles)[:, None, :]
    first_half = values[..., :half_dim]
    second_half = values[..., half_dim:]
    return jnp.concatenate(
        [
            first_half * cosine - second_half * sine_part,
            first_half * sine_part + second_half * cosine,
        ],
        -1,
    )


def token_layout(cont_lengths, offsets, group_len):
    prompt_len = group_len // 2
    group_ids = offsets // group_len
    inner_pos = offsets % group_len
    seg_ends = jnp.cumsum(cont_lengths, axis=1)
    seg_starts = seg_ends - cont_lengths
    group_pick = (
        group_ids[:, None] == jnp.arange(cont_lengths.shape[0], dtype=jnp.int32)[None, :]
    ).astype(jnp.int32)
    ends_own = jnp.sum(group_pick[:, :, None] * seg_ends[None, :, :], 1)
    starts_own = jnp.sum(group_pick[:, :, None] * seg_starts[None, :, :], 1)
    after_prompt = inner_pos - prompt_len
    segment = 1 + jnp.sum((after_prompt[:, None] >= ends_own).astype(jnp.int32), 1)
    segment = jnp.where(after_prompt < 0, 0, segment)
    slot_pick = segment[:, None] - 1 == jnp.arange(cont_lengths.shape[1], dtype=jnp.int32)[None, :]
    seg_begin = jnp.sum(jnp.where(slot_pick, starts_own, 0), 1)
    position = jnp.where(segment == 0, inner_pos, prompt_len + after_prompt - seg_begin)
    return (group_ids, segment, position)


def gate_up_grad(pre_gate, pre_up, hidden_grad):
    gate_sig = jax.nn.sigmoid(pre_gate)
    grad_gate = hidden_grad * pre_up * gate_sig * (1.0 + pre_gate * (1.0 - gate_sig))
    grad_up = hidden_grad * pre_gate * gate_sig
    return jnp.concatenate([grad_gate, grad_up], 1).astype(jnp.bfloat16)


def body(
    inputs,
    cotangent,
    routes,
    cont_lengths,
    first_gain,
    attend_in,
    attend_out,
    second_gain,
    router_weight,
    shared_gate,
    shared_up,
    shared_down,
    expert_gate,
    expert_up,
    expert_down,
):
    row_size = lax.axis_size("row")
    col_size = lax.axis_size("col")
    data_size = lax.axis_size("dp")
    row_index = lax.axis_index("row")
    col_index = lax.axis_index("col")
    tok_rest, feat_dev = inputs.shape
    feat_full = feat_dev * row_size
    tok_block = tok_rest * col_size
    tok_query = tok_block // row_size
    experts = expert_gate.shape[0]
    hidden_dev = expert_gate.shape[2]
    shared_dev = shared_gate.shape[1]
    head_cols = attend_in.shape[1]
    heads_dev = head_cols // (3 * HD)
    capacity = tok_block * 3 // experts
    slots_dev = experts * capacity // row_size
    group_len = tok_block // cont_lengths.shape[0]
    key_block = min(1024, tok_query)
    block_count = group_len // key_block
    score_scale = HD ** (-0.5)
    tokens_all = float(data_size * tok_block)
    group_base = row_index * tok_query // group_len * group_len
    inputs_f = inputs.astype(jnp.float32)
    squares_one = feature_sums(jnp.sum(inputs_f * inputs_f, 1))
    scale_one = lax.rsqrt(squares_one / feat_full + EPSILON)[:, None]
    normed_one = (inputs_f * scale_one * first_gain).astype(jnp.bfloat16)
    normed_all = token_gather(normed_one)

    def qkv_term(row_start, row_count):
        return jnp.dot(
            rows_of(normed_all, row_start, row_count), attend_in, preferred_element_type=jnp.float32
        )

    qkv_raw = row_partials(qkv_term, tok_query).reshape(tok_query, heads_dev, 3, HD)
    query_offsets = row_index * tok_query + jnp.arange(tok_query, dtype=jnp.int32)
    query_group, query_segment, query_position = token_layout(
        cont_lengths, query_offsets, group_len
    )
    key_group, key_segment, key_position = token_layout(
        cont_lengths, jnp.arange(tok_block, dtype=jnp.int32), group_len
    )
    query_angles = angle_table(query_position)
    queries = rotate(qkv_raw[:, :, 0], query_angles).astype(jnp.bfloat16)
    keys_own = rotate(qkv_raw[:, :, 1], query_angles).astype(jnp.bfloat16)
    values_own = qkv_raw[:, :, 2].astype(jnp.bfloat16)
    keys_all, values_all = slot_gather(
        (keys_own.reshape(tok_query, heads_dev * HD), values_own.reshape(tok_query, heads_dev * HD))
    )

    def block_scores(block_start):
        key_rows = rows_of(keys_all, block_start, key_block).reshape(key_block, heads_dev, HD)
        block_group = rows_of(key_group, block_start, key_block)
        block_segment = rows_of(key_segment, block_start, key_block)
        block_position = rows_of(key_position, block_start, key_block)
        visible = (
            (query_group[:, None] == block_group[None, :])
            & ((block_segment[None, :] == 0) | (block_segment[None, :] == query_segment[:, None]))
            & (block_position[None, :] <= query_position[:, None])
        )
        scores = (
            jnp.einsum("qhd,khd->hqk", queries, key_rows, preferred_element_type=jnp.float32)
            * score_scale
        )
        return (scores, visible[None], key_rows)

    def forward_step(carry, block_index):
        run_max, run_total, run_accum = carry
        block_start = group_base + block_index * key_block
        scores, mask_now, key_rows = block_scores(block_start)
        value_rows = (
            rows_of(values_all, block_start, key_block)
            .reshape(key_block, heads_dev, HD)
            .astype(jnp.float32)
        )
        new_max = jnp.maximum(run_max, jnp.max(jnp.where(mask_now, scores, -1e30), -1))
        weights = jnp.where(mask_now, jnp.exp(scores - new_max[..., None]), 0.0)
        run_decay = jnp.exp(run_max - new_max)
        run_total = run_total * run_decay + jnp.sum(weights, -1)
        run_accum = run_accum * run_decay[..., None] + jnp.einsum(
            "hqk,khd->hqd", weights, value_rows, precision=HIGHEST
        )
        return ((new_max, run_total, run_accum), None)

    start_carry = (
        jnp.full((heads_dev, tok_query), -1e30, jnp.float32),
        jnp.zeros((heads_dev, tok_query), jnp.float32),
        jnp.zeros((heads_dev, tok_query, HD), jnp.float32),
    )
    (run_max, run_total, run_accum), unused_out = lax.scan(
        forward_step, start_carry, jnp.arange(block_count, dtype=jnp.int32)
    )
    log_total = run_max + jnp.log(run_total)
    attended = run_accum / run_total[..., None]
    attn_rows = attended.transpose(1, 0, 2).reshape(tok_query, heads_dev * HD).astype(jnp.bfloat16)
    outputs_all = slot_gather(attn_rows)

    def attention_term(row_start, row_count):
        return jnp.dot(
            rows_of(outputs_all, row_start, row_count),
            attend_out,
            preferred_element_type=jnp.float32,
        )

    mixed_one = inputs_f + col_partials(attention_term, tok_rest)
    gained = mixed_one * second_gain
    squares_two, logit_part = feature_sums(
        (jnp.sum(mixed_one * mixed_one, 1), jnp.dot(gained, router_weight, precision=HIGHEST))
    )
    scale_two = lax.rsqrt(squares_two / feat_full + EPSILON)[:, None]
    router_probs = jax.nn.softmax(logit_part * scale_two, -1)
    routes_rest = lax.dynamic_slice_in_dim(routes, col_index * tok_rest, tok_rest, 0)
    route_hot = routes_rest[:, :, None] == jnp.arange(experts, dtype=jnp.int32)[None, None, :]
    gate_vals = jnp.sum(jnp.where(route_hot, router_probs[:, None, :], 0.0), -1)
    count_total, prob_total = token_stats(
        (jnp.sum(route_hot.astype(jnp.float32), (0, 1)), jnp.sum(router_probs, 0))
    )
    balance_loss = experts * jnp.sum(count_total / (2.0 * tokens_all) * prob_total / tokens_all)
    unit_two = mixed_one * scale_two
    normed_two = (unit_two * second_gain).astype(jnp.bfloat16)
    normed_two_all = token_gather(normed_two)
    flat_routes = routes.reshape(-1)
    flat_hot = (flat_routes[:, None] == jnp.arange(experts, dtype=jnp.int32)[None, :]).astype(
        jnp.int32
    )
    earlier = jnp.cumsum(flat_hot, 0) - flat_hot
    slot_of = flat_routes * capacity + jnp.sum(earlier * flat_hot, 1)
    slot_pairs = slot_of.reshape(tok_block, 2)
    slot_source = (
        jnp.full((experts * capacity,), 2 * tok_block, jnp.int32)
        .at[slot_of]
        .set(jnp.arange(2 * tok_block, dtype=jnp.int32))
    )
    padded_two = jnp.concatenate([normed_two_all, jnp.zeros((1, feat_dev), jnp.bfloat16)], 0)
    expert_rows = padded_two[slot_source // 2]
    shared_both = jnp.concatenate([shared_gate, shared_up], 1)

    def shared_term(row_start, row_count):
        return jnp.dot(
            rows_of(normed_two_all, row_start, row_count),
            shared_both,
            preferred_element_type=jnp.float32,
        )

    shared_pre = row_partials(shared_term, tok_query)
    shared_g = shared_pre[:, :shared_dev]
    shared_u = shared_pre[:, shared_dev:]
    shared_hidden = (jax.nn.silu(shared_g) * shared_u).astype(jnp.bfloat16)
    expert_both = jnp.concatenate([expert_gate, expert_up], 2)

    def expert_term(row_start, row_count):
        group_count = row_count // capacity
        picked = rows_of(expert_rows, row_start, row_count).reshape(group_count, capacity, feat_dev)
        return jnp.einsum(
            "ecd,edf->ecf", picked, expert_both, preferred_element_type=jnp.float32
        ).reshape(row_count, 2 * hidden_dev)

    expert_pre = row_partials(expert_term, slots_dev)
    expert_g = expert_pre[:, :hidden_dev]
    expert_u = expert_pre[:, hidden_dev:]
    expert_hidden = (jax.nn.silu(expert_g) * expert_u).astype(jnp.bfloat16)
    shared_all, expert_all = slot_gather((shared_hidden, expert_hidden))
    expert_out = jnp.einsum(
        "ecf,efd->ecd",
        expert_all.reshape(experts, capacity, hidden_dev),
        expert_down,
        preferred_element_type=jnp.float32,
    ).reshape(experts * capacity, feat_dev)

    def output_term(row_start, row_count):
        shared_part = jnp.dot(
            rows_of(shared_all, row_start, row_count),
            shared_down,
            preferred_element_type=jnp.float32,
        )
        pair_slots = rows_of(slot_pairs, row_start, row_count)
        return jnp.concatenate(
            [shared_part, expert_out[pair_slots[:, 0]], expert_out[pair_slots[:, 1]]], 1
        )

    branch_sums = col_partials(output_term, tok_rest)
    shared_result = branch_sums[:, :feat_dev]
    expert_pick = branch_sums[:, feat_dev:].reshape(tok_rest, 2, feat_dev)
    expert_result = jnp.sum(gate_vals[:, :, None] * expert_pick, 1)
    layer_out = (mixed_one + shared_result + expert_result).astype(jnp.bfloat16)
    cot_f = cotangent.astype(jnp.float32)
    gate_grad = feature_sums(jnp.sum(expert_pick * cot_f[:, None, :], -1))
    expert_cot = (
        (gate_vals[:, :, None] * cot_f[:, None, :])
        .astype(jnp.bfloat16)
        .reshape(tok_rest, 2 * feat_dev)
    )
    cot_all = token_gather(jnp.concatenate([cotangent, expert_cot], 1))
    shared_cot = cot_all[:, :feat_dev]
    pair_cot = jnp.concatenate(
        [
            cot_all[:, feat_dev:].reshape(2 * tok_block, feat_dev),
            jnp.zeros((1, feat_dev), jnp.bfloat16),
        ],
        0,
    )
    slot_cot = pair_cot[slot_source]
    shared_down_grad = jnp.einsum(
        "tf,td->fd", shared_all, shared_cot, preferred_element_type=jnp.float32
    )

    def shared_back(row_start, row_count):
        return jnp.einsum(
            "td,fd->tf",
            rows_of(shared_cot, row_start, row_count),
            shared_down,
            preferred_element_type=jnp.float32,
        )

    shared_pgrad = gate_up_grad(shared_g, shared_u, row_partials(shared_back, tok_query))
    expert_down_grad = jnp.einsum(
        "ecf,ecd->efd",
        expert_all.reshape(experts, capacity, hidden_dev),
        slot_cot.reshape(experts, capacity, feat_dev),
        preferred_element_type=jnp.float32,
    )

    def expert_back(row_start, row_count):
        group_count = row_count // capacity
        picked = rows_of(slot_cot, row_start, row_count).reshape(group_count, capacity, feat_dev)
        return jnp.einsum(
            "ecd,efd->ecf", picked, expert_down, preferred_element_type=jnp.float32
        ).reshape(row_count, hidden_dev)

    expert_pgrad = gate_up_grad(expert_g, expert_u, row_partials(expert_back, slots_dev))
    shared_pall, expert_pall = slot_gather((shared_pgrad, expert_pgrad))
    expert_pall_view = expert_pall.reshape(experts, capacity, 2 * hidden_dev)
    expert_both_grad = jnp.einsum(
        "ecd,ecf->edf",
        expert_rows.reshape(experts, capacity, feat_dev),
        expert_pall_view,
        preferred_element_type=jnp.float32,
    )
    expert_input_grad = jnp.einsum(
        "ecf,edf->ecd", expert_pall_view, expert_both, preferred_element_type=jnp.float32
    ).reshape(experts * capacity, feat_dev)
    shared_both_grad = jnp.einsum(
        "td,tf->df", normed_two_all, shared_pall, preferred_element_type=jnp.float32
    )

    def normed_back(row_start, row_count):
        pair_slots = rows_of(slot_pairs, row_start, row_count)
        shared_part = jnp.einsum(
            "tf,df->td",
            rows_of(shared_pall, row_start, row_count),
            shared_both,
            preferred_element_type=jnp.float32,
        )
        return (
            shared_part + expert_input_grad[pair_slots[:, 0]] + expert_input_grad[pair_slots[:, 1]]
        )

    normed_grad = col_partials(normed_back, tok_rest)
    prob_grad = jnp.sum(
        jnp.where(route_hot, gate_grad[:, :, None], 0.0), 1
    ) + experts * count_total / (2.0 * tokens_all * tokens_all)
    logit_grad = router_probs * (prob_grad - jnp.sum(router_probs * prob_grad, -1, keepdims=True))
    router_grad = jnp.einsum("td,te->de", unit_two * second_gain, logit_grad, precision=HIGHEST)
    two_grad = normed_grad + jnp.einsum("te,de->td", logit_grad, router_weight, precision=HIGHEST)
    gained_two = two_grad * second_gain
    second_gain_grad = jnp.sum(two_grad * unit_two, 0)
    inner_two = feature_sums(jnp.sum(gained_two * unit_two, 1))[:, None] / feat_full
    mixed_grad = cot_f + scale_two * (gained_two - unit_two * inner_two)
    mix_all = token_gather(mixed_grad.astype(jnp.bfloat16))
    attend_out_grad = jnp.einsum(
        "tc,td->cd", outputs_all, mix_all, preferred_element_type=jnp.float32
    )

    def output_back(row_start, row_count):
        return jnp.einsum(
            "td,cd->tc",
            rows_of(mix_all, row_start, row_count),
            attend_out,
            preferred_element_type=jnp.float32,
        )

    attn_grad = (
        row_partials(output_back, tok_query).astype(jnp.bfloat16).reshape(tok_query, heads_dev, HD)
    )
    attn_grad_f = attn_grad.astype(jnp.float32)
    row_delta = jnp.sum(attn_grad_f.transpose(1, 0, 2) * attended, -1)
    queries_f = queries.astype(jnp.float32)

    def backward_step(query_grad, block_index):
        block_start = group_base + block_index * key_block
        scores, mask_now, key_rows = block_scores(block_start)
        value_rows = rows_of(values_all, block_start, key_block).reshape(key_block, heads_dev, HD)
        weights = jnp.where(mask_now, jnp.exp(scores - log_total[..., None]), 0.0)
        prob_dot = jnp.einsum(
            "qhd,khd->hqk", attn_grad, value_rows, preferred_element_type=jnp.float32
        )
        score_grad = weights * (prob_dot - row_delta[..., None])
        query_grad = (
            query_grad
            + jnp.einsum(
                "hqk,khd->qhd", score_grad, key_rows.astype(jnp.float32), precision=HIGHEST
            )
            * score_scale
        )
        key_grad = (
            jnp.einsum("hqk,qhd->khd", score_grad, queries_f, precision=HIGHEST) * score_scale
        )
        value_grad = jnp.einsum("hqk,qhd->khd", weights, attn_grad_f, precision=HIGHEST)
        return (
            query_grad,
            jnp.concatenate(
                [
                    key_grad.reshape(key_block, heads_dev * HD),
                    value_grad.reshape(key_block, heads_dev * HD),
                ],
                1,
            ),
        )

    query_grad, kv_terms = lax.scan(
        backward_step,
        jnp.zeros((tok_query, heads_dev, HD), jnp.float32),
        jnp.arange(block_count, dtype=jnp.int32),
    )
    kv_group = kv_terms.reshape(group_len, 2 * heads_dev * HD)
    kv_full = lax.dynamic_update_slice_in_dim(
        jnp.zeros((tok_block, 2 * heads_dev * HD), jnp.float32), kv_group, group_base, 0
    )

    def kv_term(row_start, row_count):
        return rows_of(kv_full, row_start, row_count)

    kv_grad = row_partials(kv_term, tok_query)
    key_grad_raw = rotate(
        kv_grad[:, : heads_dev * HD].reshape(tok_query, heads_dev, HD), -query_angles
    )
    value_grad_raw = kv_grad[:, heads_dev * HD :].reshape(tok_query, heads_dev, HD)
    query_grad_raw = rotate(query_grad, -query_angles)
    qkv_grad = (
        jnp.stack([query_grad_raw, key_grad_raw, value_grad_raw], 2)
        .reshape(tok_query, head_cols)
        .astype(jnp.bfloat16)
    )
    qkv_all = slot_gather(qkv_grad)
    attend_in_grad = jnp.einsum(
        "td,tc->dc", normed_all, qkv_all, preferred_element_type=jnp.float32
    )

    def input_back(row_start, row_count):
        return jnp.einsum(
            "tc,dc->td",
            rows_of(qkv_all, row_start, row_count),
            attend_in,
            preferred_element_type=jnp.float32,
        )

    one_grad = col_partials(input_back, tok_rest)
    unit_one = inputs_f * scale_one
    gained_one = one_grad * first_gain
    first_gain_grad = jnp.sum(one_grad * unit_one, 0)
    inner_one = feature_sums(jnp.sum(gained_one * unit_one, 1))[:, None] / feat_full
    input_grad = (mixed_grad + scale_one * (gained_one - unit_one * inner_one)).astype(jnp.bfloat16)
    first_gain_grad, second_gain_grad, router_grad = token_stats(
        (first_gain_grad, second_gain_grad, router_grad)
    )
    summed = (
        lax.psum(attend_in_grad.astype(jnp.bfloat16), "dp").astype(jnp.float32),
        lax.psum(attend_out_grad.astype(jnp.bfloat16), "dp").astype(jnp.float32),
        lax.psum(shared_both_grad.astype(jnp.bfloat16), "dp").astype(jnp.float32),
        lax.psum(shared_down_grad.astype(jnp.bfloat16), "dp").astype(jnp.float32),
        lax.psum(expert_both_grad.astype(jnp.bfloat16), "dp").astype(jnp.float32),
        lax.psum(expert_down_grad.astype(jnp.bfloat16), "dp").astype(jnp.float32),
    )
    shared_both_sum = summed[2]
    expert_both_sum = summed[4]
    return (
        layer_out,
        input_grad,
        first_gain_grad,
        summed[0],
        summed[1],
        second_gain_grad,
        router_grad,
        shared_both_sum[:, :shared_dev],
        shared_both_sum[:, shared_dev:],
        summed[3],
        expert_both_sum[:, :, :hidden_dev],
        expert_both_sum[:, :, hidden_dev:],
        summed[5],
        balance_loss,
    )


F32 = jnp.float32
BF16 = jnp.bfloat16
MASKED = -1e30
LIGHT = pl.CostEstimate(flops=1, transcendentals=0, bytes_accessed=1)


def swap(value, axis, step=1):
    size = lax.axis_size(axis)
    return lax.ppermute(value, axis, [(i, i ^ step) for i in range(size)])


def shifted(value, axis, step):
    size = lax.axis_size(axis)
    return lax.ppermute(value, axis, [(i, (i + step) % size) for i in range(size)])


def in_order(parts, axis):
    size, me = len(parts), lax.axis_index(axis)
    whole = jnp.zeros((size,) + parts[0].shape, parts[0].dtype)
    for step, part in enumerate(parts):
        whole = lax.dynamic_update_index_in_dim(whole, part, (me - step) % size, 0)
    return whole


def col_parts(value):
    return [value] + [shifted(value, "col", s) for s in range(1, lax.axis_size("col"))]


def col_rows(value):
    whole = in_order(col_parts(value), "col")
    return whole.reshape((-1,) + value.shape[1:])


def col_sum_rows(whole):
    size, me = lax.axis_size("col"), lax.axis_index("col")
    blocks = whole.reshape((size, whole.shape[0] // size) + whole.shape[1:])
    total = lax.dynamic_index_in_dim(blocks, me, 0, False).astype(F32)
    for step in range(1, size):
        block = lax.dynamic_index_in_dim(blocks, (me + step) % size, 0, False)
        total = total + shifted(block, "col", step).astype(F32)
    return total


def sum_by_swaps(value, axes):
    for axis in axes:
        step = 1
        while step < lax.axis_size(axis):
            value = value + swap(value, axis, step)
            step *= 2
    return value


def stage(*values):
    return lax.optimization_barrier(values)


def held(value, *others):
    return lax.optimization_barrier((value,) + others)[0]


def high_low(value):
    high = value.astype(BF16)
    return high, (value - high.astype(F32)).astype(BF16)


def with_rows(value, extra):
    high, low = high_low(extra)
    rows = jnp.concatenate([high, low], -2)
    room = [(0, 0)] * (rows.ndim - 1) + [(0, value.shape[-1] - rows.shape[-1])]
    return jnp.concatenate([value, jnp.pad(rows, room)], -2)


def split_rows(value, count, extra, width):
    tail = value[..., count:, :width].astype(F32)
    return value[..., :count, :], tail[..., :extra, :] + tail[..., extra:, :]


def add_kernel(one_ref, two_ref, *sum_refs):
    total = (one_ref[...].astype(F32) + two_ref[...].astype(F32)).astype(BF16)
    for index, sum_ref in enumerate(sum_refs):
        pl.when(pl.program_id(0) == index)(lambda sum_ref=sum_ref: sum_ref.__setitem__(Ellipsis, total))


def added(one, two):
    steps = one.shape[0]
    shape = (1,) + one.shape[1:]
    spec = pl.BlockSpec(shape, lambda i: (i,) + (0,) * (one.ndim - 1))
    return pl.pallas_call(
        add_kernel,
        grid=(steps,),
        in_specs=[spec, spec],
        out_specs=[whole_block(shape)] * steps,
        out_shape=[jax.ShapeDtypeStruct(shape, BF16)] * steps,
        cost_estimate=LIGHT,
        name="added",
    )(one, two)


def pair_half(whole):
    core = lax.axis_index("dp") % 2
    halves = whole.reshape((2, whole.shape[0] // 2) + whole.shape[1:])
    mine = lax.dynamic_index_in_dim(halves, core, 0, False)
    other = lax.dynamic_index_in_dim(halves, 1 - core, 0, False)
    return (mine.astype(F32) + swap(other, "dp", 1).astype(F32)).astype(BF16)


def sent_back(blocks):
    return [blocks[0]] + [shifted(blocks[step], "col", -step) for step in range(1, len(blocks))]


def summed_up(blocks):
    total = blocks[0].astype(F32)
    for block in blocks[1:]:
        total = total + block.astype(F32)
    return total


def cross_sum(half):
    step = 2
    while step < lax.axis_size("dp"):
        half = (half.astype(F32) + swap(half, "dp", step).astype(F32)).astype(BF16)
        step *= 2
    return half


def both_halves(half):
    core = lax.axis_index("dp") % 2
    rest = swap(half, "dp", 1)
    first = jnp.where(core == 0, half, rest)
    second = jnp.where(core == 0, rest, half)
    return jnp.concatenate([first, second], 0).astype(F32)


def matmul(left, right, left_dim, right_dim):
    return lax.dot_general(
        left, right, (((left_dim,), (right_dim,)), ((), ())), preferred_element_type=F32
    )


def whole_block(shape):
    return pl.BlockSpec(shape, lambda *unused: (0,) * len(shape))


def visible_to(start_rows, row_base, row_count, key_count, prompt_len):
    row_ids = row_base + lax.broadcasted_iota(jnp.int32, (row_count, key_count), 0)
    key_ids = lax.broadcasted_iota(jnp.int32, (row_count, key_count), 1)
    own_segment = (key_ids < prompt_len) | (key_ids >= start_rows)
    return (key_ids <= row_ids) & own_segment


def attend_kernel(
    heads, block, prompt_len, scale,
    left_ref, right_ref, weight_left_ref, weight_right_ref, out_weight_ref, cos_ref, sin_ref, start_ref,
    qkv_ref, attended_ref, log_ref, partial_ref,
):
    raw = jnp.dot(left_ref[...], weight_left_ref[...], preferred_element_type=F32)
    raw = raw + jnp.dot(right_ref[...], weight_right_ref[...], preferred_element_type=F32)
    cosine, sine = cos_ref[...], sin_ref[...]
    half = HD // 2
    tokens = raw.shape[0]
    partial = jnp.zeros(partial_ref.shape, F32)
    for head in range(heads):
        base = head * 3 * HD
        for kind in range(3):
            piece = raw[:, base + kind * HD : base + (kind + 1) * HD]
            if kind < 2:
                one, two = piece[:, :half], piece[:, half:]
                piece = jnp.concatenate(
                    [one * cosine - two * sine, one * sine + two * cosine], 1
                )
            qkv_ref[3 * head + kind] = piece.astype(BF16)
        for low in range(0, tokens, block):
            rows = pl.ds(low, block)
            keys = low + block
            scores = matmul(qkv_ref[3 * head, rows], qkv_ref[3 * head + 1, :keys], 1, 1) * scale
            seen = visible_to(start_ref[rows], low, block, keys, prompt_len)
            scores = jnp.where(seen, scores, MASKED)
            top = jnp.max(scores, 1, keepdims=True)
            weights = jnp.exp(scores - top)
            total = jnp.sum(weights, 1, keepdims=True)
            result = matmul(weights.astype(BF16), qkv_ref[3 * head + 2, :keys], 1, 0) / total
            attended_ref[head, rows] = result
            log_ref[head, rows] = top + jnp.log(total)
        partial = partial + jnp.dot(
            attended_ref[head].astype(BF16),
            out_weight_ref[head * HD : (head + 1) * HD],
            preferred_element_type=F32,
        )
    partial_ref[...] = partial.astype(BF16)


def attend(left, right, weight_left, weight_right, out_weight, cosine, sine, start, block):
    tokens, features = left.shape
    heads = weight_left.shape[1] // (3 * HD)
    return pl.pallas_call(
        functools.partial(attend_kernel, heads, block, tokens // 2, HD ** (-0.5)),
        out_shape=(
            jax.ShapeDtypeStruct((3 * heads, tokens, HD), BF16),
            jax.ShapeDtypeStruct((heads, tokens, HD), F32),
            jax.ShapeDtypeStruct((heads, tokens, 1), F32),
            jax.ShapeDtypeStruct((tokens, features), BF16),
        ),
        cost_estimate=LIGHT,
        name="attend",
    )(left, right, weight_left, weight_right, out_weight, cosine, sine, start)


def attend_back_kernel(
    heads, block, prompt_len, scale,
    own_ref, peer_ref, qkv_ref, attended_ref, log_ref, cos_ref, sin_ref, start_ref, normed_ref, weight_ref,
    one_ref, grad_ref, key_acc, value_acc, query_acc,
):
    cosine, sine = cos_ref[...], sin_ref[...]
    half = HD // 2
    tokens = own_ref.shape[0]
    upper = (own_ref[...].astype(F32) + peer_ref[...].astype(F32)).astype(BF16)
    pieces = []
    for head in range(heads):
        head_grad = upper[:, head * HD : (head + 1) * HD]
        delta = jnp.sum(head_grad.astype(F32) * attended_ref[head], 1, keepdims=True)
        key_acc[...] = jnp.zeros_like(key_acc)
        value_acc[...] = jnp.zeros_like(value_acc)
        for low in range(0, tokens, block):
            rows = pl.ds(low, block)
            keys = low + block
            query = qkv_ref[3 * head, rows]
            key = qkv_ref[3 * head + 1, :keys]
            scores = matmul(query, key, 1, 1) * scale
            seen = visible_to(start_ref[rows], low, block, keys, prompt_len)
            weights = jnp.where(seen, jnp.exp(scores - log_ref[head, rows]), 0.0)
            grad_rows = head_grad[low : low + block]
            prob_dot = matmul(grad_rows, qkv_ref[3 * head + 2, :keys], 1, 1)
            score_grad = (weights * (prob_dot - delta[low : low + block]) * scale).astype(BF16)
            query_acc[rows] = matmul(score_grad, key, 1, 0)
            key_acc[:keys] += matmul(score_grad, query, 0, 0)
            value_acc[:keys] += matmul(weights.astype(BF16), grad_rows, 0, 0)
        for piece in (query_acc[...], key_acc[...]):
            one, two = piece[:, :half], piece[:, half:]
            pieces += [one * cosine + two * sine, two * cosine - one * sine]
        pieces.append(value_acc[...])
    qkv_grad = jnp.concatenate(pieces, 1).astype(BF16)
    one_ref[...] = matmul(qkv_grad, weight_ref[...], 1, 1)
    grad_ref[...] = matmul(normed_ref[...], qkv_grad, 0, 0).astype(BF16)


def attend_back(own, peer, qkv, attended, log_total, cosine, sine, start, normed, weight, block):
    heads, tokens, unused = attended.shape
    return pl.pallas_call(
        functools.partial(attend_back_kernel, heads, block, tokens // 2, HD ** (-0.5)),
        out_shape=(
            jax.ShapeDtypeStruct(normed.shape, F32),
            jax.ShapeDtypeStruct(weight.shape, BF16),
        ),
        scratch_shapes=[pltpu.VMEM((tokens, HD), F32)] * 3,
        cost_estimate=LIGHT,
        name="attend_back",
    )(own, peer, qkv, attended, log_total, cosine, sine, start, normed, weight)


def picks(rank_ref, capacity):
    rank = rank_ref[0]
    return lax.broadcasted_iota(jnp.int32, (capacity, rank.shape[1]), 0) == rank


def ones_where(mask):
    return jnp.where(mask, 1.0, 0.0).astype(BF16)


def pack_kernel(place_ref, gate_ref, up_ref, down_ref, out_ref):
    out_ref[0, 0] = gate_ref[0]
    out_ref[0, 1] = up_ref[0]
    out_ref[0, 2] = down_ref[0].astype(F32).T.astype(BF16)


def pack(place, gate, up, down, first, count, parts):
    features, hidden = gate.shape[1], gate.shape[2] // parts

    def row_place(i, place):
        return (0, place[i], 0) if parts > 1 else (first + place[i], 0, 0)

    def lane_place(i, place):
        return (0, 0, place[i]) if parts > 1 else (first + place[i], 0, 0)

    return pl.pallas_call(
        pack_kernel,
        grid_spec=pltpu.PrefetchScalarGridSpec(
            num_scalar_prefetch=1,
            grid=(count,),
            in_specs=[
                pl.BlockSpec((1, features, hidden), lane_place),
                pl.BlockSpec((1, features, hidden), lane_place),
                pl.BlockSpec((1, hidden, features), row_place),
            ],
            out_specs=pl.BlockSpec((1, 3, features, hidden), lambda i, place: (i, 0, 0, 0)),
        ),
        out_shape=jax.ShapeDtypeStruct((count, 3, features, hidden), BF16),
        cost_estimate=LIGHT,
        name="pack",
    )(place, gate, up, down)


def gated(pre_gate, pre_up, hidden_grad):
    sigma = 1.0 / (1.0 + jnp.exp(-pre_gate))
    silu = pre_gate * sigma
    grad_gate = hidden_grad * pre_up * sigma * (1.0 + pre_gate * (1.0 - sigma))
    return silu * pre_up, grad_gate, hidden_grad * silu


def shared_kernel(
    place_ref, token_ref, token_peer_ref, cot_ref, cot_peer_ref, gate_ref, up_ref, down_ref, near_ref, far_ref,
    out_in_ref, dx_in_ref, own_grad_ref, other_grad_ref, out_ref, dx_ref, peer_ref,
):
    step = pl.program_id(0)

    @pl.when(step == 0)
    def start():
        peer_ref[...] = near_ref[0]
        out_ref[...] = out_in_ref[...]
        dx_ref[...] = dx_in_ref[...]

    @pl.when(step > 0)
    def turn():
        peer_ref[...] = far_ref[0]

    rows, rows_peer = token_ref[...], token_peer_ref[...]
    gate, up, down = gate_ref[0], up_ref[0], down_ref[0]
    pre_gate = matmul(rows, gate, 1, 0) + matmul(rows_peer, peer_ref[0], 1, 0)
    pre_up = matmul(rows, up, 1, 0) + matmul(rows_peer, peer_ref[1], 1, 0)
    back = matmul(cot_ref[...], down, 1, 1) + matmul(cot_peer_ref[...], peer_ref[2], 1, 0)
    result, grad_gate, grad_up = gated(pre_gate, pre_up, back)
    result, grad_gate, grad_up = result.astype(BF16), grad_gate.astype(BF16), grad_up.astype(BF16)
    out_ref[...] += matmul(result, down, 1, 0)
    dx_ref[...] += matmul(grad_gate, gate, 1, 1) + matmul(grad_up, up, 1, 1)
    grads = (
        matmul(rows, grad_gate, 0, 0).astype(BF16),
        matmul(rows, grad_up, 0, 0).astype(BF16),
        matmul(cot_ref[...], result, 0, 0).astype(BF16),
    )

    def write(target_ref):
        for kind in range(3):
            target_ref[0, kind] = grads[kind]

    pl.when(step == 0)(lambda: write(own_grad_ref))
    pl.when(step > 0)(lambda: write(other_grad_ref))


def run_shared(place, tokens_own, tokens_peer, cot_own, cot_peer, gate, up, down, near, far, out_sum, dx_sum):
    tokens, features = tokens_own.shape
    hidden = gate.shape[2] // 2
    grads = jax.ShapeDtypeStruct((1, 3, features, hidden), BF16)
    sums = jax.ShapeDtypeStruct((tokens, features), F32)
    return pl.pallas_call(
        shared_kernel,
        grid_spec=pltpu.PrefetchScalarGridSpec(
            num_scalar_prefetch=1,
            grid=(2,),
            in_specs=[whole_block((tokens, features))] * 4
            + [
                pl.BlockSpec((1, features, hidden), lambda i, place: (0, 0, place[i])),
                pl.BlockSpec((1, features, hidden), lambda i, place: (0, 0, place[i])),
                pl.BlockSpec((1, hidden, features), lambda i, place: (0, place[i], 0)),
            ]
            + [whole_block((1, 3, features, hidden))] * 2
            + [whole_block((tokens, features))] * 2,
            out_specs=(whole_block(grads.shape),) * 2 + (whole_block(sums.shape),) * 2,
            scratch_shapes=[pltpu.VMEM((3, features, hidden), BF16)],
        ),
        out_shape=(grads, grads, sums, sums),
        cost_estimate=LIGHT,
        name="run_shared",
    )(place, tokens_own, tokens_peer, cot_own, cot_peer, gate, up, down, near, far, out_sum, dx_sum)


def experts_kernel(
    capacity,
    place_ref, rank_ref, prob_ref, token_ref, token_peer_ref, cot_ref, cot_peer_ref,
    gate_ref, up_ref, down_ref, *refs,
):
    peer_refs, (out_in_ref, dx_in_ref) = refs[:4], refs[4:-6]
    own_grad_ref, other_grad_ref, share_ref, out_ref, dx_ref, peer_ref = refs[-6:]
    step = pl.program_id(0)

    @pl.when(step == 0)
    def start():
        out_ref[...] = out_in_ref[...]
        dx_ref[...] = dx_in_ref[...]

    for index, source_ref in enumerate(peer_refs):
        pl.when(step == index)(lambda source_ref=source_ref: peer_ref.__setitem__(Ellipsis, source_ref[0]))

    mask = picks(rank_ref, capacity)
    chosen = ones_where(mask)
    gate_val = jnp.sum(jnp.where(mask, prob_ref[0], 0.0), 1, keepdims=True)
    rows, rows_peer, cot_rows, cot_rows_peer = (
        jnp.dot(chosen, ref[...], preferred_element_type=F32).astype(BF16)
        for ref in (token_ref, token_peer_ref, cot_ref, cot_peer_ref)
    )
    gate, up, down = gate_ref[0], up_ref[0], down_ref[0]
    pre_gate = matmul(rows, gate, 1, 0) + matmul(rows_peer, peer_ref[0], 1, 0)
    pre_up = matmul(rows, up, 1, 0) + matmul(rows_peer, peer_ref[1], 1, 0)
    raw_back = matmul(cot_rows, down, 1, 1) + matmul(cot_rows_peer, peer_ref[2], 1, 0)
    result, grad_gate, grad_up = gated(pre_gate, pre_up, gate_val * raw_back)
    result = result.astype(BF16).astype(F32)
    share = jnp.sum(result * raw_back, 1, keepdims=True)
    share_ref[0] = jnp.sum(jnp.where(mask, share, 0.0), 0, keepdims=True)
    scaled = (gate_val * result).astype(BF16)
    grad_gate = grad_gate.astype(BF16)
    grad_up = grad_up.astype(BF16)
    out_rows = matmul(scaled, down, 1, 0).astype(BF16)
    out_ref[...] += matmul(chosen, out_rows, 0, 0)
    dx_rows = (matmul(grad_gate, gate, 1, 1) + matmul(grad_up, up, 1, 1)).astype(BF16)
    dx_ref[...] += matmul(chosen, dx_rows, 0, 0)
    grads = (
        matmul(rows, grad_gate, 0, 0).astype(BF16),
        matmul(rows, grad_up, 0, 0).astype(BF16),
        matmul(cot_rows, scaled, 0, 0).astype(BF16),
    )

    def write(target_ref):
        for kind in range(3):
            target_ref[0, kind] = grads[kind]

    pl.when(step < 2)(lambda: write(own_grad_ref))
    pl.when(step >= 2)(lambda: write(other_grad_ref))


def run_experts(
    place, rank, probs, tokens_own, tokens_peer, cot_own, cot_peer, gate, up, down, peers,
    out_sum, dx_sum, first, capacity,
):
    tokens, features = out_sum.shape
    hidden = gate.shape[2]

    def at(shape, base):
        return pl.BlockSpec((1,) + shape, lambda i, place: (base + place[i], 0, 0))

    block = (1, 3, features, hidden)
    grads = jax.ShapeDtypeStruct((2, 3, features, hidden), BF16)
    sums = jax.ShapeDtypeStruct((tokens, features), F32)
    return pl.pallas_call(
        functools.partial(experts_kernel, capacity),
        grid_spec=pltpu.PrefetchScalarGridSpec(
            num_scalar_prefetch=1,
            grid=(4,),
            in_specs=[at((1, tokens), first)] * 2
            + [whole_block((tokens, features))] * 4
            + [
                at((features, hidden), first),
                at((features, hidden), first),
                at((hidden, features), first),
            ]
            + [whole_block(block)] * 4
            + [whole_block((tokens, features))] * 2,
            out_specs=(
                pl.BlockSpec(block, lambda i, place: (place[jnp.minimum(i, 1)] // 2, 0, 0, 0)),
                pl.BlockSpec(block, lambda i, place: (place[jnp.maximum(i, 2)] // 2, 0, 0, 0)),
                at((1, tokens), 0),
                whole_block(sums.shape),
                whole_block(sums.shape),
            ),
            scratch_shapes=[pltpu.VMEM((3, features, hidden), BF16)],
        ),
        out_shape=(grads, grads, jax.ShapeDtypeStruct((4, 1, tokens), F32), sums, sums),
        cost_estimate=LIGHT,
        name="run_experts",
    )(
        place, rank, probs, tokens_own, tokens_peer, cot_own, cot_peer, gate, up, down, *peers,
        out_sum, dx_sum,
    )


def spread_kernel(core_ref, half_ref, rest_ref, *refs):
    gate_ref, up_ref, down_ref, flag_ref = refs[-4:]
    flag_ref[...] = jnp.zeros_like(flag_ref)

    def write(source_ref):
        gate_ref[0] = source_ref[0, 0].astype(F32)
        up_ref[0] = source_ref[0, 1].astype(F32)
        down_ref[0] = source_ref[0, 2].astype(F32).T

    own = pl.program_id(0) < pl.num_programs(0) // 2
    pl.when(own)(lambda: write(half_ref))
    pl.when(jnp.logical_not(own))(lambda: write(rest_ref))


def spread(core, half_grads, rest_grads, earlier, first, experts):
    aliased = min(len(earlier), 3)
    half, unused, features, hidden = half_grads.shape

    def own_index(i, core):
        return (jnp.minimum(i, half - 1), 0, 0, 0)

    def rest_index(i, core):
        return (jnp.maximum(i - half, 0), 0, 0, 0)

    def out_index(i, core):
        place = jnp.where(i < half, 2 * i + core[0], 2 * (i - half) + 1 - core[0])
        return (first + place, 0, 0)

    shapes = ((features, hidden), (features, hidden), (hidden, features))
    return pl.pallas_call(
        spread_kernel,
        grid_spec=pltpu.PrefetchScalarGridSpec(
            num_scalar_prefetch=1,
            grid=(2 * half,),
            in_specs=[
                pl.BlockSpec((1, 3, features, hidden), own_index),
                pl.BlockSpec((1, 3, features, hidden), rest_index),
            ]
            + [pl.BlockSpec(memory_space=pl.ANY)] * len(earlier),
            out_specs=tuple(pl.BlockSpec((1,) + shape, out_index) for shape in shapes)
            + (whole_block((8, 128)),),
        ),
        out_shape=tuple(jax.ShapeDtypeStruct((experts,) + shape, F32) for shape in shapes)
        + (jax.ShapeDtypeStruct((8, 128), F32),),
        input_output_aliases={3 + i: i for i in range(aliased)},
        cost_estimate=LIGHT,
        name="spread",
    )(core, half_grads, rest_grads, *earlier)


def paired_body(
    inputs,
    cotangent,
    routes,
    cont_lengths,
    first_gain,
    attend_in,
    attend_out,
    second_gain,
    router_weight,
    shared_gate,
    shared_up,
    shared_down,
    expert_gate,
    expert_up,
    expert_down,
):
    col_size = lax.axis_size("col")
    data_size = lax.axis_size("dp")
    col_index = lax.axis_index("col")
    tok_rest, feat_dev = inputs.shape
    feat_full = feat_dev * 2
    tok_block = tok_rest * col_size
    experts = expert_gate.shape[0]
    shared_dev = shared_gate.shape[1]
    capacity = tok_block * 3 // experts
    tokens_all = float(data_size * tok_block)
    prompt_len = tok_block // 2
    block = 256
    chunk = 4
    shards = lax.axis_index("dp")
    core = (shards % 2).reshape(1)
    place = jnp.stack([shards, shards ^ 2, shards ^ 1, shards ^ 3])
    sides = jnp.stack([shards % 2, 1 - shards % 2])
    firsts = list(range(0, experts, 4))

    own_parts = col_parts(inputs)
    gain_high, gain_low = high_low(first_gain)
    gain_last = (first_gain - gain_high.astype(F32) - gain_low.astype(F32)).astype(BF16)
    gain_rows = jnp.pad(jnp.stack([gain_high, gain_low, gain_last]), ((0, 5), (0, 0)))
    peer_first = swap(jnp.concatenate([inputs, gain_rows], 0), "row")
    peer_gain = jnp.sum(peer_first[tok_rest : tok_rest + 3].astype(F32)[::-1], 0)
    peer_weight = swap(attend_in, "row")
    peer_parts = [peer_first[:tok_rest]] + [swap(part, "row") for part in own_parts[1:]]
    own_all = in_order(own_parts, "col").reshape(tok_block, feat_dev).astype(F32)

    shared_gate, shared_up, shared_down = shared_gate[None], shared_up[None], shared_down[None]

    def pack_experts(place, index):
        return pack(place, expert_gate, expert_up, expert_down, firsts[index], 1, 1)

    late_place = held(place, own_parts[1:])
    packed = [pack_experts(late_place, 0), pack_experts(late_place, 1)]
    peer_parts[1] = held(peer_parts[1], packed)

    peer_all = in_order(peer_parts, "col").reshape(tok_block, feat_dev).astype(F32)
    squares_one = jnp.sum(own_all * own_all, 1) + jnp.sum(peer_all * peer_all, 1)
    scale_all = lax.rsqrt(squares_one / feat_full + EPSILON)[:, None]
    unit_all = own_all * scale_all
    normed_own = (unit_all * first_gain).astype(BF16)
    normed_peer = (peer_all * scale_all * peer_gain).astype(BF16)

    offsets = jnp.arange(tok_block, dtype=jnp.int32)
    after = offsets - prompt_len
    ends = jnp.cumsum(cont_lengths[0])
    begin = jnp.max(jnp.where(ends[None, :] <= after[:, None], ends[None, :], 0), 1)
    start = jnp.where(after < 0, 0, prompt_len + begin)
    position = jnp.where(after < 0, offsets, prompt_len + after - begin)
    angles = angle_table(position)
    cosine, sine = jnp.cos(angles), jnp.sin(angles)
    start = start[:, None]

    expert_ids = jnp.arange(experts, dtype=jnp.int32)
    named = (routes[:, 0][None, :] == expert_ids[:, None]) | (
        routes[:, 1][None, :] == expert_ids[:, None]
    )
    before = (offsets[:, None] < offsets[None, :]).astype(BF16)
    rank = jnp.dot(named.astype(BF16), before, preferred_element_type=F32).astype(jnp.int32)
    rank = jnp.where(named, rank, -1).reshape(experts, col_size, tok_rest)
    rank = jnp.concatenate(
        [
            lax.dynamic_index_in_dim(rank, (col_index - step) % col_size, 1, False)
            for step in range(col_size)
        ],
        1,
    )[:, None, :]
    count_total = sum_by_swaps(jnp.sum(named.astype(F32), 1), ("dp",))

    packed, place, sides, normed_own, normed_peer, peer_weight, cot_sent, count_total, cosine, sine = stage(
        packed, place, sides, normed_own, normed_peer, peer_weight, cotangent, count_total, cosine, sine
    )
    weights = [swap(packed[0], "row")]
    cot_parts = col_parts(cot_sent)
    qkv, attended, log_total, out_partial = attend(
        normed_own, normed_peer, attend_in, peer_weight, attend_out, cosine, sine, start, block
    )
    late_place = held(place, out_partial)
    packed += [pack_experts(late_place, 2), pack_experts(late_place[1:], 2)]
    weights, cot_parts, out_partial, packed, place = stage(weights, cot_parts, out_partial, packed, place)

    weights.append(swap(packed[1], "row"))
    across = swap(weights[0], "dp", 2)
    cot_own = jnp.concatenate(cot_parts, 0)
    inputs_f = inputs.astype(F32)
    mixed_one = inputs_f + col_sum_rows(out_partial)
    late_place, late_sides = held((place, sides), cot_own)
    packed += [pack_experts(late_place, 3), pack_experts(late_place[1:], 3)]
    shared_packed = pack(late_sides, shared_gate, shared_up, shared_down, 0, 1, 2)
    weights, across, cot_own, mixed_one, shared_packed, packed = stage(
        weights, across, cot_own, mixed_one, shared_packed, packed
    )

    gained = mixed_one * second_gain
    partial_stats = jnp.concatenate(
        [
            jnp.sum(mixed_one * mixed_one, 1, keepdims=True),
            jnp.dot(gained, router_weight, precision=HIGHEST),
        ],
        1,
    )
    peer_stats = swap(partial_stats, "row")
    stats = partial_stats + peer_stats
    scale_two = lax.rsqrt(stats[:, :1] / feat_full + EPSILON)
    router_probs = jax.nn.softmax(stats[:, 1:] * scale_two, -1)
    unit_two = mixed_one * scale_two
    normed_two = (unit_two * second_gain).astype(BF16)
    normed_sent = with_rows(normed_two, router_probs.T)
    normed_sent, cot_own, shared_packed, weights, across = stage(
        normed_sent, cot_own, shared_packed, weights, across
    )

    sent_parts = col_parts(normed_sent)
    cot_peer = swap(cot_own, "row")
    sent_parts, cot_peer, weights, across, packed = stage(sent_parts, cot_peer, weights, across, packed)

    opened = [split_rows(part, tok_rest, experts, tok_rest) for part in sent_parts]
    tokens_own = jnp.concatenate([part[0] for part in opened], 0)
    probs = jnp.concatenate([part[1] for part in opened], 1)[:, None, :]
    tokens_peer = swap(tokens_own, "row")
    far = [swap(weights[0], "dp", 1), swap(across, "dp", 1)]
    peers = [(weights[0], across)]
    across = swap(weights[1], "dp", 2)
    tokens_own, tokens_peer, probs, far, packed, weights = stage(
        tokens_own, tokens_peer, probs, far, packed, weights
    )

    ready, landed, totalled, arrived = [], [], [], []
    expert_grads, finished = [], {}

    def launch(count):
        flights = [(name, half, swap(half, "dp", 2)) for name, half in ready[:count]]
        returns = [(name, total, swap(total, "dp", 1)) for name, total in totalled]
        del ready[:count], totalled[:]
        return flights, returns

    def follow(*values, flying=None, placing=True):
        for name, mine, theirs in landed:
            total = added(held(mine, *values) if values else mine, theirs)[0]
            if flying:
                flying[1].append((name, total, swap(total, "dp", 1)))
            else:
                totalled.append((name, total))
        del landed[:]
        if not placing:
            return
        for name, total, rest in arrived:
            if isinstance(name, int):
                turn = held(core, *values) if values else core
                expert_grads[:] = spread(turn, total, rest, tuple(expert_grads), name, experts)
            else:
                finished[name] = (total, rest)
        del arrived[:]

    def land(launched, *values):
        flights, returns = launched
        got = stage(flights_of(flights), flights_of(returns), flights_of(ready), flights_of(totalled),
                    expert_grads[3:], values)
        landed[:] = [(old[0],) + new for old, new in zip(flights, got[0])]
        arrived[:] = arrived + [(old[0],) + new for old, new in zip(returns, got[1])]
        ready[:] = [(old[0],) + new for old, new in zip(ready, got[2])]
        totalled[:] = [(old[0],) + new for old, new in zip(totalled, got[3])]
        expert_grads[3:] = got[4]
        return got[5]

    def flights_of(items):
        return [item[1:] for item in items]

    def pair_up(name, mine, theirs, *values):
        for index, half in enumerate(added(held(mine, *values) if values else mine, theirs)):
            ready.append((name + 2 * index if isinstance(name, int) else name, half))

    shares = []

    def run(index, near, far, out_sum, dx_sum):
        mine, other, share, out_new, dx_new = run_experts(
            place, rank, probs, tokens_own, tokens_peer, cot_own, cot_peer,
            expert_gate, expert_up, expert_down, tuple(near) + tuple(far), out_sum, dx_sum, firsts[index], capacity,
        )
        shares.append(share[:, 0])
        return mine, other, out_new, dx_new

    zeros = jnp.zeros((tok_block, feat_dev), F32)
    third = swap(packed[2], "row")
    mine, other, out_sum, dx_sum = run(0, peers[0], far, zeros, zeros)
    third, across, weights, mine, other, out_sum, dx_sum, packed, shared_packed = stage(
        third, across, weights, mine, other, out_sum, dx_sum, packed, shared_packed
    )
    near = (weights[1], across)
    far = [swap(part, "dp", 1) for part in near]
    pair_up(firsts[0], mine, swap(other, "dp", 1))
    launched = launch(1)
    third = [third, swap(packed[3], "row")]
    shared_near = swap(shared_packed, "row")
    mine, other, out_sum, dx_sum = run(1, near, far, out_sum, dx_sum)
    third, mine, other, out_sum, dx_sum, packed, shared_near = land(
        launched, third, mine, other, out_sum, dx_sum, packed, shared_near
    )
    launched = launch(1)
    far = [swap(part, "dp", 1) for part in third]
    fourth = swap(packed[4], "row")
    shared_far = swap(shared_near, "dp", 1)
    theirs = swap(other, "dp", 1)
    earlier = mine
    shared_mine, shared_other, out_sum, dx_sum = run_shared(
        sides, tokens_own, tokens_peer, cot_own, cot_peer,
        shared_gate, shared_up, shared_down, shared_near, shared_far, out_sum, dx_sum,
    )
    pair_up(firsts[1], earlier, theirs, out_sum)
    follow(out_sum, flying=launched)
    far, third, fourth, out_sum, dx_sum, packed, shared_mine, shared_other = land(
        launched, far, third, fourth, out_sum, dx_sum, packed, shared_mine, shared_other
    )
    launched = launch(1)
    fourth = [fourth, swap(packed[5], "row")]
    fourth_far = [swap(fourth[0], "dp", 1)]
    mine, other, out_sum, dx_sum = run(2, third, far, out_sum, dx_sum)
    follow(out_sum)
    fourth, fourth_far, mine, other, out_sum, dx_sum = land(
        launched, fourth, fourth_far, mine, other, out_sum, dx_sum
    )
    launched = launch(1)
    fourth_far.append(swap(fourth[1], "dp", 1))
    theirs = swap(other, "dp", 1)
    earlier = mine
    mine, other, out_sum, dx_sum = run(3, fourth, fourth_far, out_sum, dx_sum)
    pair_up(firsts[2], earlier, theirs, out_sum)
    follow(out_sum, placing=False)
    mine, other, out_sum, dx_sum, shares, shared_mine, shared_other = land(
        launched, mine, other, out_sum, dx_sum, shares, shared_mine, shared_other
    )

    launched = launch(1)
    shares = jnp.concatenate(shares, 0)
    dx_blocks = []
    for step in range(col_size):
        rows = slice(step * tok_rest, (step + 1) * tok_rest)
        dx_blocks.append(with_rows(dx_sum[rows].astype(BF16), shares[:, rows]))
    dx_blocks = sent_back(dx_blocks)
    follow(dx_blocks[1:], flying=launched)
    dx_blocks, mine, other, shared_mine, shared_other = land(
        launched, dx_blocks, mine, other, shared_mine, shared_other
    )
    launched = launch(1)
    normed_grad, gate_grad = split_rows(summed_up(dx_blocks), tok_rest, experts, tok_rest)
    prob_grad = gate_grad.T + experts * count_total / (2.0 * tokens_all * tokens_all)
    logit_grad = router_probs * (prob_grad - jnp.sum(router_probs * prob_grad, -1, keepdims=True))
    two_grad = normed_grad + jnp.einsum("te,de->td", logit_grad, router_weight, precision=HIGHEST)
    gained_two = two_grad * second_gain
    inner_two = jnp.sum(gained_two * unit_two, 1, keepdims=True)
    inner_two = (inner_two + swap(inner_two, "row")) / feat_full
    cot_f = cotangent.astype(F32)
    mixed_grad = cot_f + scale_two * (gained_two - unit_two * inner_two)
    mix_parts = col_parts(mixed_grad.astype(BF16))
    theirs = swap(other, "dp", 1)
    pair_up(firsts[3], mine, theirs, mix_parts[1:])
    follow(mix_parts[1:], flying=launched)
    mix_parts, logit_grad, two_grad, out_sum, shared_mine, shared_other = land(
        launched, mix_parts, logit_grad, two_grad, out_sum, shared_mine, shared_other
    )

    launched = launch(1)
    mix_all = in_order(mix_parts, "col").reshape(tok_block, feat_dev)
    attn_own = matmul(mix_all, attend_out, 1, 1).astype(BF16)
    attn_peer = swap(attn_own, "row")
    out_low = out_sum.astype(BF16)
    out_blocks = sent_back([out_low[step * tok_rest : (step + 1) * tok_rest] for step in range(col_size)])
    follow(attn_own, flying=launched)
    attn_peer = held(attn_peer, [item[1] for item in launched[1]], expert_grads[3:])
    heads = attended.shape[0]
    attn_rows = attended.astype(BF16)
    attend_out_grad = jnp.concatenate(
        [matmul(attn_rows[head], mix_all, 0, 0) for head in range(heads)], 0
    ).astype(BF16)
    router_grad = jnp.einsum("td,te->ed", unit_two * second_gain, logit_grad, precision=HIGHEST)
    second_gain_grad = jnp.sum(two_grad * unit_two, 0)
    one_partial, attend_in_grad = attend_back(
        attn_own, attn_peer, qkv, attended, log_total, cosine, sine, start, normed_own, attend_in, block
    )
    shared_half = added(held(shared_mine, one_partial), swap(shared_other, "dp", 1))[0]
    one_partial, attend_in_grad, attend_out_grad, out_blocks, router_grad, second_gain_grad, shared_half = land(
        launched, one_partial, attend_in_grad, attend_out_grad, out_blocks, router_grad, second_gain_grad,
        shared_half,
    )

    launched = launch(1)
    one_low = one_partial.astype(BF16)
    one_blocks = one_low.reshape(col_size, tok_rest, feat_dev)
    one_blocks = sent_back(
        [
            lax.dynamic_index_in_dim(one_blocks, (col_index - step) % col_size, 0, False)
            for step in range(col_size)
        ]
    )
    width = attend_in_grad.shape[1]
    attend_half = pair_half(
        jnp.concatenate([attend_in_grad, attend_out_grad.reshape(-1, width)], 0)
    )
    first_gain_grad = jnp.sum(one_partial * unit_all, 0)
    prob_sums = jnp.pad(jnp.sum(router_probs, 0), (0, feat_dev - experts))
    totals = jnp.concatenate(
        [first_gain_grad[None], second_gain_grad[None], prob_sums[None], router_grad], 0
    )
    totals = totals + swap(totals, "dp", 1)
    layer_out = (mixed_one + summed_up(out_blocks)).astype(BF16)
    follow(one_blocks[1:], flying=launched)
    one_blocks, attend_half, totals = land(launched, one_blocks, attend_half, totals)

    totals = sum_by_swaps(totals, ("col",))
    ready += [("attend", attend_half[None]), ("shared", shared_half)]
    launched = launch(9)
    one_grad = summed_up(one_blocks)
    own_rows = col_index * tok_rest
    unit_one = rows_of(unit_all, own_rows, tok_rest)
    scale_one = rows_of(scale_all, own_rows, tok_rest)
    gained_one = one_grad * first_gain
    inner_one = jnp.sum(gained_one * unit_one, 1, keepdims=True)
    inner_one = (inner_one + swap(inner_one, "row")) / feat_full
    input_grad = (mixed_grad + scale_one * (gained_one - unit_one * inner_one)).astype(BF16)
    follow(flying=launched)
    arrived += launched[1]
    del launched[1][:]
    follow()
    input_grad, totals = land(launched, input_grad, totals)
    totals = totals + swap(totals, "dp", 2)
    while ready or landed or totalled or arrived:
        follow()
        launched = launch(9)
        landed, arrived = landed + launched[0], arrived + launched[1]

    prob_total = totals[2, :experts]
    balance_loss = experts * jnp.sum(count_total / (2.0 * tokens_all) * prob_total / tokens_all)
    shared_grads = [jnp.concatenate(pair, 3) for pair in (finished["shared"], finished["shared"][::-1])]
    shared_grads = jnp.where(core == 0, *shared_grads)[0].astype(F32)
    attend_grads = [jnp.concatenate(pair, 1) for pair in (finished["attend"], finished["attend"][::-1])]
    attend_grads = jnp.where(core == 0, *attend_grads)[0].astype(F32)
    return (
        layer_out,
        input_grad,
        totals[0],
        attend_grads[:feat_dev],
        attend_grads[feat_dev:].reshape(attend_out_grad.shape),
        totals[1],
        totals[3:].T,
        shared_grads[0],
        shared_grads[1],
        shared_grads[2].T,
        expert_grads[0],
        expert_grads[1],
        expert_grads[2],
        balance_loss,
    )


def power_of_two(number):
    return number & (number - 1) == 0


def chosen_body(*shards):
    inputs, cont_lengths, shared_gate = shards[0], shards[3], shards[9]
    experts, unused, hidden = shards[12].shape
    tok_block = inputs.shape[0] * lax.axis_size("col")
    paired = (
        lax.axis_size("row") == 2
        and lax.axis_size("dp") == 4
        and experts == 16
        and shared_gate.shape[1] == hidden
        and hidden % 256 == 0
        and power_of_two(lax.axis_size("col"))
        and cont_lengths.shape[0] == 1
        and tok_block % 512 == 0
        and tok_block <= 2048
    )
    return (paired_body if paired else body)(*shards)


def solution(mesh):
    in_specs = (
        P(("dp", "col"), "row"),
        P(("dp", "col"), "row"),
        P("dp", None),
        P("dp", None),
        P("row"),
        P("row", "col"),
        P("col", "row"),
        P("row"),
        P("row", None),
        P("row", "col"),
        P("row", "col"),
        P("col", "row"),
        P(None, "row", "col"),
        P(None, "row", "col"),
        P(None, "col", "row"),
    )
    out_specs = (
        P(("dp", "col"), "row"),
        P(("dp", "col"), "row"),
        P("row"),
        P("row", "col"),
        P("col", "row"),
        P("row"),
        P("row", None),
        P("row", "col"),
        P("row", "col"),
        P("col", "row"),
        P(None, "row", "col"),
        P(None, "row", "col"),
        P(None, "col", "row"),
        P(),
    )
    return jax.shard_map(chosen_body, mesh=mesh, in_specs=in_specs, out_specs=out_specs, check_vma=False)
```
